512 devices in a mesh: mem: 32 (over x, z), lat: 4 (over y_lo, core), lon: 4 (over y_hi).
Axes of the slice: x: 4, y: 8 (y_hi: 4, y_lo: 2; y = y_hi * 2 + y_lo), z: 8, core: 2. Of those that a mesh axis runs over, the one named last changes fastest.
Arguments:
- perturb: float32 [64, 1536, 2048], P('mem', 'lat', 'lon'), may hold values from -6 to 6
- loc_lat: float32 [384], replicated, may hold values from 1 to 96
- loc_lon: float32 [512], replicated, may hold values from 1 to 128
- obs_cell: int32 [4, 4, 2048], P('lat', 'lon'), may hold values from 0 to 196607
- obs_count: int32 [4, 4], P('lat', 'lon'), may hold values from 512 to 2048, as said below
- obs_innov: float32 [4, 4, 2048], P('lat', 'lon'), may hold values from -8 to 8
- obs_error: float32 [4, 4, 2048], P('lat', 'lon'), may hold values from 0.5 to 4
Outputs:
- analysis: float32 [64, 384, 512], P('mem', 'lat', 'lon')
- increment: float32 [1536, 2048], P('lat', 'lon')
The draws below stay inside these ranges and needn't reach their ends.
Inputs may be any that keep to these rules, and one draw needn't show every extreme that they name: `obs_cell`: cells may repeat within a tile. `obs_count`: in every draw at least one tile uses all 2048 slots.
All inputs are finite; a program needn't handle non-finite values.
Results may differ from the reference program's by a relative error of at most 0.0001.
Values sent between devices are 32-bit elements; how exact they have to be, the bound alone decides.
No kernel may reach another device: no remote copies, remote signals or barrier semaphores. Data moves between devices by JAX's collectives and lax.ppermute only.
A program may use at most 64 MiB of HBM per device.

```python
import math
import jax
import jax.numpy as jnp
from jax import lax

NLAT = 1536
NLON = 2048
ITERS = 2
CLAT = 384
CLON = 512
MEMBERS = 64
NQLAT = 384
NQLON = 512
OBS_TILE = 2048
LAT_TILES = 4
LON_TILES = 4


def draw_obs_count(key, part):
    first_key, second_key = jax.random.split(jax.random.fold_in(key, 17))
    counts = jax.random.randint(first_key, (LAT_TILES, LON_TILES), OBS_TILE // 4, OBS_TILE + 1)
    chosen = jax.random.randint(second_key, (), 0, LAT_TILES * LON_TILES)
    flat_index = jnp.arange(LAT_TILES * LON_TILES, dtype=jnp.int32).reshape(LAT_TILES, LON_TILES)
    return jnp.where(flat_index == chosen, OBS_TILE, counts).astype(jnp.int32)


def touch_ends(values, rng, low, high):
    shape = values.shape
    spot = [jax.random.randint(jax.random.fold_in(rng, axis), (), 0, shape[axis]) for axis in range(len(shape))]
    values = values.at[tuple(spot)].set(low)
    longest = shape.index(max(shape))
    spot[longest] = (spot[longest] + 1) % shape[longest]
    return values.at[tuple(spot)].set(high)


def shard_levels(key, dims, cuts, low, high):
    gain = 1.0
    for axis_at, blocks in cuts:
        heights = jax.random.uniform(jax.random.fold_in(jax.random.fold_in(key, 6), axis_at), (blocks,), jnp.float32, low / len(cuts), high / len(cuts))
        gain = gain * jnp.repeat(jnp.exp(heights), dims[axis_at] // blocks).reshape((-1,) + (1,) * (len(dims) - 1 - axis_at))
    return gain


def scatter_about(rng, dims, width, most, shards=(), held_as=jnp.bfloat16):
    gain = shard_levels(rng, dims, shards, -0.22, 0.18) if shards else 1.0
    values = jax.random.normal(rng, dims, jnp.float32) * width * gain
    return jnp.minimum(jnp.maximum(values, -most), most).astype(held_as)


def setup_inputs(seed: int = 0) -> dict:
    key_of = jax.random.split(jax.random.key(seed), 8)
    perturb = scatter_about(key_of[0], (MEMBERS, NLAT, NLON), 1.0, 6.0, ((0, 32), (1, 4), (2, 4)), jnp.float32)
    loc_lat = jnp.clip(jnp.exp(jax.random.uniform(key_of[1], (NQLAT,), jnp.float32, math.log(1.0), math.log(96.0))), 1.0, 96.0)
    loc_lon = jnp.clip(jnp.exp(jax.random.uniform(key_of[2], (NQLON,), jnp.float32, math.log(1.0), math.log(128.0))), 1.0, 128.0)
    obs_cell = touch_ends(jax.random.randint(key_of[3], (LAT_TILES, LON_TILES, OBS_TILE), 0, CLAT * CLON), jax.random.fold_in(key_of[3], 1), 0, (CLAT * CLON) - 1).astype(jnp.int32)
    obs_count = draw_obs_count(jax.random.fold_in(key_of[7], 71), 0)
    obs_innov = scatter_about(key_of[5], (LAT_TILES, LON_TILES, OBS_TILE), 2.0, 8.0, ((0, 4), (1, 4)), jnp.float32)
    obs_error = jnp.clip(jnp.exp(math.log(4.0) - 2.0794415 * jax.random.uniform(key_of[6], (LAT_TILES, LON_TILES, OBS_TILE), jnp.float32) ** shard_levels(key_of[6], (LAT_TILES, LON_TILES, OBS_TILE), ((0, 4), (1, 4)), -0.2, 0.2)), 0.5, 4.0)
    return dict(perturb=perturb, loc_lat=loc_lat, loc_lon=loc_lon, obs_cell=obs_cell, obs_count=obs_count, obs_innov=obs_innov, obs_error=obs_error)


huber_width = 1.0
tiny_floor = 1e-06
highest = lax.Precision.HIGHEST

def kernel_rows(scales, first_row, row_count):
    total_rows = scales.shape[0]
    row_index = first_row + jnp.arange(row_count, dtype=jnp.int32)
    inside = (row_index >= 0) & (row_index < total_rows)
    row_scale = scales[jnp.clip(row_index, 0, total_rows - 1)]
    col_index = jnp.arange(total_rows, dtype=jnp.int32)
    offset = (row_index[:, None] - col_index[None, :]).astype(jnp.float32)
    spread = row_scale[:, None] ** 2 + scales[None, :] ** 2
    weight = jnp.where(inside, (jnp.sqrt(jnp.pi) * row_scale) ** (-0.5), jnp.zeros_like(row_scale))
    return weight[:, None] * jnp.exp(-offset * offset / spread)

def refine_axis(coarse, along):
    coarse_count = coarse.shape[along] - 2
    lower_cells = lax.slice_in_dim(coarse, 0, coarse_count, axis=along)
    middle = lax.slice_in_dim(coarse, 1, coarse_count + 1, axis=along)
    upper_cells = lax.slice_in_dim(coarse, 2, coarse_count + 2, axis=along)
    pieces = (0.375 * lower_cells + 0.625 * middle, 0.125 * lower_cells + 0.875 * middle, 0.875 * middle + 0.125 * upper_cells, 0.625 * middle + 0.375 * upper_cells)
    stacked = jnp.stack(pieces, axis=along + 1)
    new_shape = list(coarse.shape)
    new_shape[along] = 4 * coarse_count
    return stacked.reshape(new_shape)

def refine_both(coarse):
    return refine_axis(refine_axis(coarse, coarse.ndim - 2), coarse.ndim - 1)

def reference(perturb, loc_lat, loc_lon, obs_cell, obs_count, obs_innov, obs_error):
    members = perturb.shape[0]
    member_scale = 1.0 / math.sqrt(members - 1)
    lat_kernel = kernel_rows(loc_lat, 0, NQLAT)
    lon_kernel = kernel_rows(loc_lon, 0, NQLON)
    tile_lat = jnp.arange(LAT_TILES, dtype=jnp.int32)[:, None, None]
    tile_lon = jnp.arange(LON_TILES, dtype=jnp.int32)[None, :, None]
    obs_rows = (tile_lat * CLAT + obs_cell // CLON).astype(jnp.int32)
    obs_cols = (tile_lon * CLON + obs_cell % CLON).astype(jnp.int32)
    usable = (jnp.arange(OBS_TILE, dtype=jnp.int32)[None, None, :] < obs_count[:, :, None]).astype(jnp.float32)

    def refined(control):
        coarse = jnp.dot(jnp.dot(lat_kernel, control, precision=highest), lon_kernel.T, precision=highest)
        return refine_both(jnp.pad(coarse, 1))

    def field_of(controls):

        def add_member(running, member_items):
            control, member = member_items
            return (running + refined(control) * member, None)
        running, _ = lax.scan(add_member, jnp.zeros((NLAT, NLON), jnp.float32), (controls, perturb))
        return member_scale * running

    def adjoint(weights):
        spread = jnp.zeros((NLAT, NLON), jnp.float32).at[obs_rows, obs_cols].add(weights)
        _, pullback = jax.vjp(refined, jnp.zeros((NQLAT, NQLON), jnp.float32))

        def single(member):
            return pullback(member * (member_scale * spread))[0]
        return lax.map(single, perturb)
    analysis = jnp.zeros((members, NQLAT, NQLON), jnp.float32)
    observed = jnp.zeros_like(obs_innov)
    increment = jnp.zeros((NLAT, NLON), jnp.float32)
    for iteration in range(ITERS):
        residual = (observed - obs_innov) / obs_error
        weights = usable * residual / jnp.sqrt(1.0 + (residual / huber_width) ** 2) / obs_error
        gradient = analysis + adjoint(weights)
        image_field = field_of(gradient)
        image_obs = image_field[obs_rows, obs_cols]
        grad_total = jnp.sum(gradient * gradient)
        curvature = jnp.sum(usable * (image_obs / obs_error) ** 2)
        length = grad_total / (grad_total + curvature + tiny_floor)
        analysis = analysis - length * gradient
        observed = observed - length * image_obs
        increment = increment - length * image_field
    return (analysis, increment)
```

```python
import functools
import math

import jax
import jax.numpy as jnp
from jax import lax
from jax.experimental import pallas as pl
from jax.experimental.pallas import tpu as pltpu
from jax.sharding import Mesh
from jax.sharding import PartitionSpec as P

MEM = ("mem_0", "mem_1")
LAT = ("lat_0", "lat_1")
TILES = ("lat_0", "lat_1", "lon")

tiny_floor = 1e-06
highest = lax.Precision.HIGHEST
f32 = jnp.float32
bf16 = jnp.bfloat16

ROWS = 112
COLS = 144
EDGE = 128


def sent_to_all(x, axis):
    copies = jnp.broadcast_to(x, (lax.axis_size(axis), *x.shape))
    return lax.all_to_all(copies, axis, split_axis=0, concat_axis=0, tiled=True)


def scale_run(scales, first, count):
    padded = jnp.pad(scales, (8, 248), constant_values=1.0)
    return lax.dynamic_slice(padded, (first + 8,), (count,))


def kernel_block(scales, first_row, row_count, first_col, col_count):
    total = scales.shape[0]
    rows = first_row + jnp.arange(row_count, dtype=jnp.int32)
    cols = first_col + jnp.arange(col_count, dtype=jnp.int32)
    row_scale = scale_run(scales, first_row, row_count)
    col_scale = scale_run(scales, first_col, col_count)
    inside = (rows >= 0) & (rows < total)
    weight = jnp.where(inside, (jnp.sqrt(jnp.pi) * row_scale) ** (-0.5), jnp.zeros_like(row_scale))
    offset = (rows[:, None] - cols[None, :]).astype(f32)
    spread = row_scale[:, None] ** 2 + col_scale[None, :] ** 2
    return weight[:, None] * jnp.exp(-offset * offset / spread)


def split_two(x):
    high = x.astype(bf16)
    low = (x - high.astype(f32)).astype(bf16)
    return high, low


def hat(position, count):
    cell = lax.broadcasted_iota(jnp.int32, (count, position.shape[-1]), 0).astype(f32)
    return jnp.maximum(1.0 - jnp.abs(position - cell), 0.0)


def nt_dot(a, b):
    return lax.dot_general(a, b, (((1,), (1,)), ((), ())), preferred_element_type=f32)


def picked_kernel(perturb_ref, cell_ref, out_ref):
    members, fine_lat, fine_lon = perturb_ref.shape
    slots = cell_ref.shape[-1]
    step = 512
    blocks = []
    for k in range(members):
        high, low = split_two(perturb_ref[k])
        blocks.append(jnp.concatenate([high, low], axis=1))
    field = jnp.concatenate(blocks, axis=0)
    for start in range(0, slots, step):
        cell = cell_ref[:, start : start + step]
        row = cell // fine_lon
        col = cell - row * fine_lon
        at_col = lax.broadcasted_iota(jnp.int32, (fine_lon, step), 0) == col
        one = jnp.where(at_col, 1.0, 0.0).astype(bf16)
        values = jnp.dot(field, jnp.concatenate([one, one], axis=0), preferred_element_type=f32)
        at_row = lax.broadcasted_iota(jnp.int32, (fine_lat, step), 0) == row
        for k in range(members):
            mine = values[k * fine_lat : (k + 1) * fine_lat]
            out_ref[k : k + 1, start : start + step] = jnp.sum(
                jnp.where(at_row, mine, 0.0), axis=0, keepdims=True
            )


def picked(perturb, cell):
    return pl.pallas_call(
        picked_kernel,
        out_shape=jax.ShapeDtypeStruct((perturb.shape[0], cell.shape[-1]), f32),
        compiler_params=pltpu.CompilerParams(vmem_limit_bytes=56 * 1024 * 1024),
        name="picked",
    )(perturb, cell)


def weights_of(observed, innovation, inverse):
    residual = (observed - innovation) * inverse
    return residual / jnp.sqrt(1.0 + residual * residual) * inverse


def length_of(grad_total, curvature):
    return grad_total / (grad_total + curvature + tiny_floor)


def sweep_kernel(first, scale, lon_tiles, *refs):
    if first:
        tile_ref, known_ref, left_ref, right_ref, left_own_ref, right_own_ref = refs[:6]
        refs = refs[6:]
    else:
        tile_ref, known_ref, seen_ref, left_ref, right_ref, left_own_ref, right_own_ref = refs[:7]
        refs = refs[7:]
    if first:
        part_ref, coarse_ref, grad_ref, total_ref, q_ref, at_row_ref, at_col_ref = refs
    else:
        part_ref, coarse_ref, grad_ref, length_ref, total_ref, q_ref, at_row_ref, at_col_ref = refs
    tiles = known_ref.shape[0]
    slots = known_ref.shape[2] // 5
    members = grad_ref.shape[0]

    def known(n):
        return known_ref[:, 0, n * slots : (n + 1) * slots]

    cell = known(0)
    innovation = known(1)
    inverse = known(2)
    row = jnp.floor(cell * (1.0 / 512.0))
    at_row_ref[...] = (row + 2.5) * 0.25
    at_col_ref[...] = (cell - row * 512.0 + 2.5) * 0.25
    force = weights_of(0.0, innovation, inverse)
    if not first:
        image = seen_ref[:, 0, :slots]
        grad_total = jnp.sum(seen_ref[:, 0, slots:])
        curvature = jnp.sum((image * inverse) ** 2)
        length = length_of(grad_total, curvature)
        force = weights_of(-length * image, innovation, inverse) - length * force
        length_ref[...] = jnp.broadcast_to(length, length_ref.shape)
    for k in range(members):
        q_ref[k] = known(3 + k) * force * scale
    total_ref[...] = jnp.zeros_like(total_ref)

    def one_tile(t, carry):
        lat = t // lon_tiles
        lon = t - lat * lon_tiles
        rows = hat(at_row_ref[pl.ds(t, 1), :], ROWS)
        cols = hat(at_col_ref[pl.ds(t, 1), :], COLS).astype(bf16)
        blocks = []
        for k in range(members):
            blocks.extend(split_two(rows * q_ref[k, pl.ds(t, 1), :]))
        made = nt_dot(jnp.concatenate(blocks, axis=0), cols)
        at = pl.ds(pl.multiple_of(lat * 96, 8), ROWS)
        for k in range(members):
            both = made[2 * k * ROWS : (2 * k + 1) * ROWS] + made[(2 * k + 1) * ROWS : (2 * k + 2) * ROWS]
            total_ref[k, at, pl.ds(pl.multiple_of(lon * 128, 128), 128)] += both[:, :128]
            total_ref[k, at, pl.ds(pl.multiple_of(lon * 128 + 128, 128), COLS - 128)] += both[:, 128:]
        return carry

    lax.fori_loop(0, tiles, one_tile, 0)

    own = tile_ref[0]
    rows = hat(at_row_ref[pl.ds(own, 1), :], ROWS)
    cols = hat(at_col_ref[pl.ds(own, 1), :], COLS).astype(bf16)
    left = jnp.concatenate([left_ref[...], left_own_ref[...]], axis=0)
    image = jnp.zeros((1, slots), f32)
    squares = jnp.zeros((1, EDGE), f32)
    for k in range(members):
        half = jnp.dot(left, total_ref[k], precision=highest, preferred_element_type=f32)
        coarse = jnp.dot(half[:ROWS], right_ref[...], precision=highest, preferred_element_type=f32)
        grad = jnp.dot(half[ROWS:], right_own_ref[...], precision=highest, preferred_element_type=f32)
        coarse_ref[k] = coarse
        grad_ref[k] = grad
        squares = squares + jnp.sum(grad * grad, axis=0, keepdims=True)
        made = jnp.dot(jnp.concatenate(split_two(coarse), axis=0), cols, preferred_element_type=f32)
        value = jnp.sum((made[:ROWS] + made[ROWS:]) * rows, axis=0, keepdims=True)
        image = image + value * known_ref[own, :, (3 + k) * slots : (4 + k) * slots]
    part_ref[:, :slots] = image * scale
    part_ref[:, slots:] = squares


def sweep(tile, known, seen, kernels, scale, lon_tiles, members):
    left, right, left_own, right_own = kernels
    slots = known.shape[2] // 5
    tiles = known.shape[0]
    first = seen is None
    out_shape = [
        jax.ShapeDtypeStruct((1, slots + EDGE), f32),
        jax.ShapeDtypeStruct((members, ROWS, COLS), f32),
        jax.ShapeDtypeStruct((members, left_own.shape[0], right_own.shape[1]), f32),
    ]
    if not first:
        out_shape.append(jax.ShapeDtypeStruct((1, EDGE), f32))
    arrays = [known] if first else [known, seen]
    arrays += [left, right, left_own, right_own]
    whole = pl.BlockSpec(memory_space=pltpu.VMEM)
    return pl.pallas_call(
        functools.partial(sweep_kernel, first, scale, lon_tiles),
        out_shape=out_shape,
        in_specs=[pl.BlockSpec(memory_space=pltpu.SMEM)] + [whole] * len(arrays),
        out_specs=[whole] * len(out_shape),
        scratch_shapes=[
            pltpu.VMEM((members, left.shape[1], right.shape[0]), f32),
            pltpu.VMEM((members, tiles, slots), f32),
            pltpu.VMEM((tiles, slots), f32),
            pltpu.VMEM((tiles, slots), f32),
        ],
        compiler_params=pltpu.CompilerParams(vmem_limit_bytes=56 * 1024 * 1024),
        name="sweep_first" if first else "sweep_second",
    )(tile, *arrays)


def field_kernel(scale, perturb_ref, length_ref, ends_ref, c1_ref, c2_ref, g1_ref, g2_ref, out_ref, analysis_ref):
    members, fine_lat, fine_lon = perturb_ref.shape
    pieces, piece_rows, piece_cols = out_ref.shape
    across = fine_lon // piece_cols
    one = length_ref[0, 0]
    two = length_of(jnp.sum(ends_ref[:, 0, EDGE:]), jnp.sum(ends_ref[:, 0, :EDGE]))

    def refined(count, cells, axis):
        shape = (count, cells) if axis == 0 else (cells, count)
        fine = lax.broadcasted_iota(jnp.int32, shape, axis).astype(f32)
        cell = lax.broadcasted_iota(jnp.int32, shape, 1 - axis).astype(f32)
        return jnp.maximum(1.0 - jnp.abs((fine + 2.5) * 0.25 - cell), 0.0).astype(bf16)

    to_rows = refined(fine_lat, ROWS, 0)
    to_cols = refined(fine_lon, COLS, 1)
    field = jnp.zeros((fine_lat, fine_lon), f32)
    for k in range(members):
        coarse = one * c1_ref[k] + two * c2_ref[k]
        high, low = split_two(coarse)
        tall = jnp.dot(to_rows, high, preferred_element_type=f32) + jnp.dot(to_rows, low, preferred_element_type=f32)
        high, low = split_two(tall)
        fine = jnp.dot(high, to_cols, preferred_element_type=f32) + jnp.dot(low, to_cols, preferred_element_type=f32)
        field = field + fine * perturb_ref[k]
        analysis_ref[k] = -(one * g1_ref[k] + two * g2_ref[k])
    field = -scale * field
    for n in range(pieces):
        i = n // across * piece_rows
        j = n % across * piece_cols
        out_ref[n] = field[i : i + piece_rows, j : j + piece_cols]


def per_device(perturb, loc_lat, loc_lon, obs_cell, obs_count, obs_innov, obs_error):
    members, fine_lat, fine_lon = perturb.shape
    coarse_lat, coarse_lon = fine_lat // 4, fine_lon // 4
    groups = lax.axis_size(MEM)
    scale = 1.0 / math.sqrt(members * groups - 1)
    lat, lon = lax.axis_index(LAT), lax.axis_index("lon")
    lat_tiles, lon_tiles = lax.axis_size(LAT), lax.axis_size("lon")
    slots = obs_cell.shape[-1]
    total_lat, total_lon = lat_tiles * coarse_lat, lon_tiles * coarse_lon
    padded_lat, padded_lon = total_lat + 16, total_lon + 128
    tile = (lat * lon_tiles + lon).astype(jnp.int32).reshape(1)

    cell = obs_cell.reshape(1, slots)
    innovation = obs_innov.reshape(1, slots)
    usable = jnp.arange(slots, dtype=jnp.int32)[None, :] < obs_count.reshape(1, 1)
    inverse = jnp.where(usable, 1.0 / obs_error.reshape(1, slots), 0.0)
    near = picked(perturb, cell)
    message = jnp.concatenate([cell.astype(f32), innovation, inverse, near[:1], near[1:]], axis=1)
    known = sent_to_all(message, TILES)

    first_lat, first_lon = lat * coarse_lat, lon * coarse_lon
    lat_all = kernel_block(loc_lat, -1, padded_lat, 0, total_lat)
    lon_all = kernel_block(loc_lon, -1, padded_lon, 0, total_lon)
    lat_tile = kernel_block(loc_lat, first_lat - 1, ROWS, 0, total_lat)
    lon_tile = kernel_block(loc_lon, first_lon - 1, COLS, 0, total_lon)
    left = jnp.einsum("ab,cb->ac", lat_tile, lat_all, precision=highest)
    right = jnp.einsum("ab,cb->ac", lon_all, lon_tile, precision=highest)
    left_own = kernel_block(loc_lat, -1, padded_lat, first_lat, coarse_lat).T
    right_own = kernel_block(loc_lon, -1, padded_lon, first_lon, coarse_lon)
    kernels = (left, right, left_own, right_own)

    part, coarse_1, grad_1 = sweep(tile, known, None, kernels, scale, lon_tiles, members)
    mine = jnp.sum(sent_to_all(part, MEM), axis=0)
    seen = sent_to_all(mine, TILES)
    part, coarse_2, grad_2, length_1 = sweep(tile, known, seen, kernels, scale, lon_tiles, members)
    mine = jnp.sum(sent_to_all(part, MEM), axis=0)
    bent = (mine[:, :slots] * inverse) ** 2
    bent = jnp.sum(bent.reshape(slots // EDGE, EDGE), axis=0, keepdims=True)
    ends = sent_to_all(jnp.concatenate([bent, mine[:, slots:]], axis=1), TILES)

    whole = pl.BlockSpec(memory_space=pltpu.VMEM)
    piece_cols = 128
    piece_rows = fine_lat * fine_lon // groups // piece_cols
    pieces, analysis = pl.pallas_call(
        functools.partial(field_kernel, scale),
        out_shape=[
            jax.ShapeDtypeStruct((groups, piece_rows, piece_cols), f32),
            jax.ShapeDtypeStruct((members, coarse_lat, coarse_lon), f32),
        ],
        in_specs=[whole] * 7,
        out_specs=[whole] * 2,
        compiler_params=pltpu.CompilerParams(vmem_limit_bytes=56 * 1024 * 1024),
        name="field",
    )(perturb, length_1, ends, coarse_1, coarse_2, grad_1, grad_2)
    summed = jnp.sum(lax.all_to_all(pieces, MEM, 0, 0, tiled=True), axis=0)
    everything = sent_to_all(summed, MEM)
    across = fine_lon // piece_cols
    increment = jnp.transpose(
        everything.reshape(fine_lat // piece_rows, across, piece_rows, piece_cols), (0, 2, 1, 3)
    ).reshape(fine_lat, fine_lon)
    return analysis, increment


def solution(mesh):
    torus = Mesh(
        mesh.devices.reshape(4, -1, 2, mesh.shape["lat"] // 2, mesh.shape["lon"]),
        ("mem_0", "mem_1", "lat_0", "lat_1", "lon"),
    )
    return jax.shard_map(
        per_device,
        mesh=torus,
        in_specs=(
            P(MEM, LAT, "lon"),
            P(),
            P(),
            P(LAT, "lon", None),
            P(LAT, "lon"),
            P(LAT, "lon", None),
            P(LAT, "lon", None),
        ),
        out_specs=(P(MEM, LAT, "lon"), P(LAT, "lon")),
        check_vma=False,
    )
```

```python
import functools
import math

import jax
import jax.numpy as jnp
from jax import lax
from jax.experimental import pallas as pl
from jax.experimental.pallas import tpu as pltpu
from jax.sharding import Mesh
from jax.sharding import PartitionSpec as P

MEM = ("mem_0", "mem_1")
LAT = ("lat_0", "lat_1")
TILES = ("lat_0", "lat_1", "lon")

tiny_floor = 1e-06
highest = lax.Precision.HIGHEST
f32 = jnp.float32
bf16 = jnp.bfloat16

ROWS = 112
COLS = 144
EDGE = 128


def sent_to_all(x, axis):
    copies = jnp.broadcast_to(x, (lax.axis_size(axis), *x.shape))
    return lax.all_to_all(copies, axis, split_axis=0, concat_axis=0, tiled=True)


def scale_run(scales, first, count):
    padded = jnp.pad(scales, (8, 248), constant_values=1.0)
    return lax.dynamic_slice(padded, (first + 8,), (count,))


def kernel_block(scales, first_row, row_count, first_col, col_count):
    total = scales.shape[0]
    rows = first_row + jnp.arange(row_count, dtype=jnp.int32)
    cols = first_col + jnp.arange(col_count, dtype=jnp.int32)
    row_scale = scale_run(scales, first_row, row_count)
    col_scale = scale_run(scales, first_col, col_count)
    inside = (rows >= 0) & (rows < total)
    weight = jnp.where(inside, (jnp.sqrt(jnp.pi) * row_scale) ** (-0.5), jnp.zeros_like(row_scale))
    offset = (rows[:, None] - cols[None, :]).astype(f32)
    spread = row_scale[:, None] ** 2 + col_scale[None, :] ** 2
    return weight[:, None] * jnp.exp(-offset * offset / spread)


def split_two(x):
    high = x.astype(bf16)
    low = (x - high.astype(f32)).astype(bf16)
    return high, low


def nt_dot(a, b):
    return lax.dot_general(a, b, (((1,), (1,)), ((), ())), preferred_element_type=f32)


def dot(a, b):
    return jnp.dot(a, b, preferred_element_type=f32)


def picked_kernel(count_ref, perturb_ref, cell_ref, innov_ref, error_ref, out_ref):
    members, fine_lat, fine_lon = perturb_ref.shape
    slots = cell_ref.shape[-1]
    step = 512
    slot = lax.broadcasted_iota(jnp.int32, (1, slots), 1)
    out_ref[:, :slots] = cell_ref[...].astype(f32)
    out_ref[:, slots : 2 * slots] = innov_ref[...]
    out_ref[:, 2 * slots : 3 * slots] = jnp.where(slot < count_ref[0], 1.0 / error_ref[...], 0.0)
    blocks = []
    for k in range(members):
        blocks.append(jnp.concatenate(split_two(perturb_ref[k]), axis=1))
    field = jnp.concatenate(blocks, axis=0)
    for start in range(0, slots, step):
        cell = cell_ref[:, start : start + step]
        row = cell // fine_lon
        col = cell - row * fine_lon
        at_col = lax.broadcasted_iota(jnp.int32, (fine_lon, step), 0) == col
        one = jnp.where(at_col, 1.0, 0.0).astype(bf16)
        values = dot(field, jnp.concatenate([one, one], axis=0))
        at_row = lax.broadcasted_iota(jnp.int32, (fine_lat, step), 0) == row
        for k in range(members):
            mine = values[k * fine_lat : (k + 1) * fine_lat]
            at = (3 + k) * slots + start
            out_ref[:, at : at + step] = jnp.sum(jnp.where(at_row, mine, 0.0), axis=0, keepdims=True)


def picked(count, perturb, cell, innovation, error):
    whole = pl.BlockSpec(memory_space=pltpu.VMEM)
    fields = 3 + perturb.shape[0]
    return pl.pallas_call(
        picked_kernel,
        out_shape=jax.ShapeDtypeStruct((1, fields * cell.shape[-1]), f32),
        in_specs=[pl.BlockSpec(memory_space=pltpu.SMEM)] + [whole] * 4,
        out_specs=whole,
        compiler_params=pltpu.CompilerParams(vmem_limit_bytes=24 * 1024 * 1024),
        name="picked",
    )(count, perturb, cell, innovation, error)


def weights_of(observed, innovation, inverse):
    residual = (observed - innovation) * inverse
    return residual / jnp.sqrt(1.0 + residual * residual) * inverse


def length_of(grad_total, curvature):
    return grad_total / (grad_total + curvature + tiny_floor)


def hat(below, lower, upper, count):
    groups = []
    wide = (16, below.shape[-1])
    below, lower, upper = (jnp.broadcast_to(x, wide).astype(bf16) for x in (below, lower, upper))
    zero = jnp.zeros(wide, bf16)
    cell = lax.broadcasted_iota(jnp.int32, wide, 0).astype(f32)
    for start in range(0, count, 16):
        at = (cell + start).astype(bf16)
        before = (cell + (start - 1)).astype(bf16)
        groups.append(jnp.where(below == at, lower, jnp.where(below == before, upper, zero)))
    return jnp.concatenate(groups, axis=0)


def sweep_kernel(first, scale, lon_tiles, members, *refs):
    tile_ref, known_ref = refs[:2]
    refs = refs[2:]
    if not first:
        seen_ref = refs[0]
        refs = refs[1:]
    left_ref, left_low_ref, right_ref, right_low_ref, part_ref, coarse_ref, total_ref = refs[:7]
    refs = refs[7:]
    if not first:
        length_ref, force_ref = refs[:2]
        refs = refs[2:]
    hold = refs[0]
    tiles = known_ref.shape[0]
    slots = known_ref.shape[2] // (3 + members)
    width = total_ref.shape[2]

    def known(n):
        return known_ref[:, 0, n * slots : (n + 1) * slots]

    cell = known(0)
    innovation = known(1)
    inverse = known(2)
    row = jnp.floor(cell * (1.0 / 512.0))
    col = (cell - row * 512.0 + 2.5) * 0.25
    row = (row + 2.5) * 0.25
    row_cell, col_cell = jnp.floor(row), jnp.floor(col)
    row_up, col_up = row - row_cell, col - col_cell
    hold[0], hold[1], hold[2], hold[3] = row_cell, col_cell, 1.0 - col_up, col_up
    hold[4], hold[5] = 1.0 - row_up, row_up
    force = weights_of(0.0, innovation, inverse)
    if not first:
        image = seen_ref[:, 0, :slots]
        length = length_of(jnp.sum(force * image), jnp.sum((image * inverse) ** 2))
        force = weights_of(-length * image, innovation, inverse) - length * force
        length_ref[...] = jnp.broadcast_to(length, length_ref.shape)
    hold[6] = force
    n = 7
    for k in range(members):
        q = known(3 + k) * force * scale
        for share in (1.0 - row_up, row_up):
            whole = share * q
            high = whole.astype(bf16).astype(f32)
            hold[n] = high
            hold[n + 1] = whole - high
            n += 2
    total_ref[...] = jnp.zeros_like(total_ref)

    def one_tile(t, carry):
        lat = t // lon_tiles
        lon = t - lat * lon_tiles

        def line(i):
            return hold[i, pl.ds(t, 1), :]

        cols = hat(line(1), line(2), line(3), COLS)
        blocks = []
        for k in range(members):
            for term in range(2):
                at = 7 + 4 * k + term
                blocks.append(hat(line(0), line(at), line(at + 2), ROWS))
        made = nt_dot(jnp.concatenate(blocks, axis=0), cols)
        at = pl.ds(pl.multiple_of(lat * 96, 8), ROWS)
        for k in range(members):
            both = made[2 * k * ROWS : (2 * k + 1) * ROWS] + made[(2 * k + 1) * ROWS : (2 * k + 2) * ROWS]
            total_ref[k, at, pl.ds(pl.multiple_of(lon * 128, 128), 128)] += both[:, :128]
            total_ref[k, at, pl.ds(pl.multiple_of(lon * 128 + 128, 128), COLS - 128)] += both[:, 128:]
        return carry

    lax.fori_loop(0, tiles, one_tile, 0)

    own = tile_ref[0]

    def own_line(i):
        return hold[i, pl.ds(own, 1), :]

    rows = hat(own_line(0), own_line(4), own_line(5), ROWS).astype(f32)
    cols = hat(own_line(1), own_line(2), own_line(3), COLS)
    high, low = zip(*(split_two(total_ref[k]) for k in range(members)))
    high, low = jnp.concatenate(high, axis=1), jnp.concatenate(low, axis=1)
    half = dot(left_ref[...], high) + (dot(left_ref[...], low) + dot(left_low_ref[...], high))
    half = jnp.concatenate([half[:, k * width : (k + 1) * width] for k in range(members)], axis=0)
    high, low = split_two(half)
    coarse = dot(high, right_ref[...]) + (dot(low, right_ref[...]) + dot(high, right_low_ref[...]))
    image = jnp.zeros((1, slots), f32)
    for k in range(members):
        mine = coarse[k * ROWS : (k + 1) * ROWS]
        coarse_ref[k] = mine
        high, low = split_two(mine)
        made = dot(high, cols) + dot(low, cols)
        value = jnp.sum(made * rows, axis=0, keepdims=True)
        image = image + value * known_ref[own, :, (3 + k) * slots : (4 + k) * slots]
    image = image * scale
    if not first:
        force_ref[...] = own_line(6)
    for n in range(part_ref.shape[0]):
        part_ref[n, :, :slots] = image


def sweep(tile, known, seen, kernels, scale, lon_tiles, members, groups):
    slots = known.shape[2] // (3 + members)
    tiles = known.shape[0]
    first = seen is None
    left, _, right, _ = kernels
    out_shape = [
        jax.ShapeDtypeStruct((groups, 1, slots), f32),
        jax.ShapeDtypeStruct((members, ROWS, COLS), f32),
        jax.ShapeDtypeStruct((members, left.shape[1], right.shape[0]), f32),
    ]
    if not first:
        out_shape.append(jax.ShapeDtypeStruct((1, EDGE), f32))
        out_shape.append(jax.ShapeDtypeStruct((1, slots), f32))
    arrays = [known] if first else [known, seen]
    arrays += kernels
    whole = pl.BlockSpec(memory_space=pltpu.VMEM)
    return pl.pallas_call(
        functools.partial(sweep_kernel, first, scale, lon_tiles, members),
        out_shape=out_shape,
        in_specs=[pl.BlockSpec(memory_space=pltpu.SMEM)] + [whole] * len(arrays),
        out_specs=[whole] * len(out_shape),
        scratch_shapes=[pltpu.VMEM((7 + 4 * members, tiles, slots), f32)],
        compiler_params=pltpu.CompilerParams(vmem_limit_bytes=32 * 1024 * 1024),
        name="sweep_first" if first else "sweep_second",
    )(tile, *arrays)


def ends_length(ends_ref):
    return length_of(jnp.sum(ends_ref[:, 0, EDGE:]), jnp.sum(ends_ref[:, 0, :EDGE]))


def field_kernel(scale, perturb_ref, length_ref, ends_ref, c1_ref, c2_ref, out_ref):
    members, fine_lat, fine_lon = perturb_ref.shape
    pieces, piece_rows, piece_cols = out_ref.shape
    across = fine_lon // piece_cols
    one = length_ref[0, 0]
    two = ends_length(ends_ref)

    def refined(count, cells, axis):
        shape = (count, cells) if axis == 0 else (cells, count)
        fine = lax.broadcasted_iota(jnp.int32, shape, axis).astype(f32)
        cell = lax.broadcasted_iota(jnp.int32, shape, 1 - axis).astype(f32)
        return jnp.maximum(1.0 - jnp.abs((fine + 2.5) * 0.25 - cell), 0.0).astype(bf16)

    to_rows = refined(fine_lat, ROWS, 0)
    to_cols = refined(fine_lon, COLS, 1)
    field = jnp.zeros((fine_lat, fine_lon), f32)
    for k in range(members):
        coarse = one * c1_ref[k] + two * c2_ref[k]
        high, low = split_two(coarse)
        tall = dot(to_rows, high) + dot(to_rows, low)
        high, low = split_two(tall)
        field = field + (dot(high, to_cols) + dot(low, to_cols)) * perturb_ref[k]
    field = -scale * field
    for n in range(pieces):
        i = n // across * piece_rows
        j = n % across * piece_cols
        out_ref[n] = field[i : i + piece_rows, j : j + piece_cols]


def analysis_kernel(length_ref, ends_ref, total_1_ref, total_2_ref, left_ref, right_ref, out_ref):
    one = length_ref[0, 0]
    two = ends_length(ends_ref)
    for k in range(out_ref.shape[0]):
        total = one * total_1_ref[k] + two * total_2_ref[k]
        half = jnp.dot(left_ref[...], total, precision=highest, preferred_element_type=f32)
        out_ref[k] = -jnp.dot(half, right_ref[...], precision=highest, preferred_element_type=f32)


def per_device(perturb, loc_lat, loc_lon, obs_cell, obs_count, obs_innov, obs_error):
    members, fine_lat, fine_lon = perturb.shape
    coarse_lat, coarse_lon = fine_lat // 4, fine_lon // 4
    groups = lax.axis_size(MEM)
    scale = 1.0 / math.sqrt(members * groups - 1)
    lat, lon = lax.axis_index(LAT), lax.axis_index("lon")
    lat_tiles, lon_tiles = lax.axis_size(LAT), lax.axis_size("lon")
    slots = obs_cell.shape[-1]
    total_lat, total_lon = lat_tiles * coarse_lat, lon_tiles * coarse_lon
    padded_lat, padded_lon = total_lat + 16, total_lon + 128
    tile = (lat * lon_tiles + lon).astype(jnp.int32).reshape(1)

    cell = obs_cell.reshape(1, slots)
    innovation = obs_innov.reshape(1, slots)
    error = obs_error.reshape(1, slots)
    message = picked(obs_count.reshape(1), perturb, cell, innovation, error)
    known = sent_to_all(message, TILES)

    first_lat, first_lon = lat * coarse_lat, lon * coarse_lon
    lat_all = kernel_block(loc_lat, -1, padded_lat, 0, total_lat)
    lon_all = kernel_block(loc_lon, -1, padded_lon, 0, total_lon)
    lat_tile = kernel_block(loc_lat, first_lat - 1, ROWS, 0, total_lat)
    lon_tile = kernel_block(loc_lon, first_lon - 1, COLS, 0, total_lon)
    left = jnp.einsum("ab,cb->ac", lat_tile, lat_all, precision=highest)
    right = jnp.einsum("ab,cb->ac", lon_all, lon_tile, precision=highest)
    left_own = kernel_block(loc_lat, -1, padded_lat, first_lat, coarse_lat).T
    right_own = kernel_block(loc_lon, -1, padded_lon, first_lon, coarse_lon)
    kernels = [*split_two(left), *split_two(right)]

    part, coarse_1, total_1 = sweep(tile, known, None, kernels, scale, lon_tiles, members, groups)
    mine = jnp.sum(lax.all_to_all(part, MEM, 0, 0, tiled=True), axis=0)
    seen = sent_to_all(mine, TILES)
    part, coarse_2, total_2, length_1, force = sweep(
        tile, known, seen, kernels, scale, lon_tiles, members, groups
    )
    mine = jnp.sum(lax.all_to_all(part, MEM, 0, 0, tiled=True), axis=0)
    inverse = known[tile[0], :, 2 * slots : 3 * slots]
    bent = jnp.stack([(mine * inverse) ** 2, mine * force])
    bent = jnp.sum(bent.reshape(2, slots // EDGE, EDGE), axis=1).reshape(1, 2 * EDGE)
    ends = sent_to_all(bent, TILES)

    whole = pl.BlockSpec(memory_space=pltpu.VMEM)
    piece_cols = 128
    piece_rows = fine_lat * fine_lon // groups // piece_cols
    pieces = pl.pallas_call(
        functools.partial(field_kernel, scale),
        out_shape=jax.ShapeDtypeStruct((groups, piece_rows, piece_cols), f32),
        in_specs=[whole] * 5,
        out_specs=whole,
        compiler_params=pltpu.CompilerParams(vmem_limit_bytes=24 * 1024 * 1024),
        name="field",
    )(perturb, length_1, ends, coarse_1, coarse_2)
    analysis = pl.pallas_call(
        analysis_kernel,
        out_shape=jax.ShapeDtypeStruct((members, coarse_lat, coarse_lon), f32),
        in_specs=[whole] * 6,
        out_specs=whole,
        compiler_params=pltpu.CompilerParams(vmem_limit_bytes=24 * 1024 * 1024),
        cost_estimate=pl.CostEstimate(flops=2 * 10**9, bytes_accessed=5 * 10**6, transcendentals=0),
        name="analysis",
    )(length_1, ends, total_1, total_2, left_own, right_own)
    summed = jnp.sum(lax.all_to_all(pieces, MEM, 0, 0, tiled=True), axis=0)
    everything = sent_to_all(summed, MEM)
    across = fine_lon // piece_cols
    increment = jnp.transpose(
        everything.reshape(fine_lat // piece_rows, across, piece_rows, piece_cols), (0, 2, 1, 3)
    ).reshape(fine_lat, fine_lon)
    return analysis, increment


def solution(mesh):
    torus = Mesh(
        mesh.devices.reshape(4, -1, 2, mesh.shape["lat"] // 2, mesh.shape["lon"]),
        ("mem_0", "mem_1", "lat_0", "lat_1", "lon"),
    )
    return jax.shard_map(
        per_device,
        mesh=torus,
        in_specs=(
            P(MEM, LAT, "lon"),
            P(),
            P(),
            P(LAT, "lon", None),
            P(LAT, "lon"),
            P(LAT, "lon", None),
            P(LAT, "lon", None),
        ),
        out_specs=(P(MEM, LAT, "lon"), P(LAT, "lon")),
        check_vma=False,
    )
```

```python
import functools
import math

import jax
import jax.numpy as jnp
from jax import lax
from jax.experimental import pallas as pl
from jax.experimental.pallas import tpu as pltpu
from jax.sharding import Mesh
from jax.sharding import PartitionSpec as P

MEM = ("mem_0", "mem_1")
LAT = ("lat_0", "lat_1")
TILES = ("lat_0", "lat_1", "lon")

tiny_floor = 1e-06
highest = lax.Precision.HIGHEST
f32 = jnp.float32
bf16 = jnp.bfloat16

ROWS = 112
COLS = 144
LANES = 128
TOGETHER = 2


def sent_to_all(x, axis):
    copies = jnp.broadcast_to(x, (lax.axis_size(axis), *x.shape))
    return lax.all_to_all(copies, axis, split_axis=0, concat_axis=0, tiled=True)


def scale_run(scales, first, count):
    padded = jnp.pad(scales, (8, 248), constant_values=1.0)
    return lax.dynamic_slice(padded, (first + 8,), (count,))


def kernel_block(scales, first_row, row_count, first_col, col_count):
    total = scales.shape[0]
    rows = first_row + jnp.arange(row_count, dtype=jnp.int32)
    cols = first_col + jnp.arange(col_count, dtype=jnp.int32)
    row_scale = scale_run(scales, first_row, row_count)
    col_scale = scale_run(scales, first_col, col_count)
    inside = (rows >= 0) & (rows < total)
    weight = jnp.where(inside, (jnp.sqrt(jnp.pi) * row_scale) ** (-0.5), jnp.zeros_like(row_scale))
    offset = (rows[:, None] - cols[None, :]).astype(f32)
    spread = row_scale[:, None] ** 2 + col_scale[None, :] ** 2
    return weight[:, None] * jnp.exp(-offset * offset / spread)


def split_two(x):
    high = x.astype(bf16)
    low = (x - high.astype(f32)).astype(bf16)
    return high, low


def nt_dot(a, b):
    return lax.dot_general(a, b, (((1,), (1,)), ((), ())), preferred_element_type=f32)


def dot(a, b):
    return jnp.dot(a, b, preferred_element_type=f32)


def lane_rows(read, count):
    return jnp.concatenate([read(r) for r in range(count)], axis=1)


def picked_kernel(count_ref, perturb_ref, cell_ref, innov_ref, error_ref, out_ref):
    members, fine_lat, fine_lon = perturb_ref.shape
    lines = cell_ref.shape[0]
    step = 512
    per_step = step // LANES
    slot = lax.broadcasted_iota(jnp.int32, cell_ref.shape, 0) * LANES + lax.broadcasted_iota(
        jnp.int32, cell_ref.shape, 1
    )
    out_ref[:lines] = cell_ref[...].astype(f32)
    out_ref[lines : 2 * lines] = innov_ref[...]
    out_ref[2 * lines : 3 * lines] = jnp.where(slot < count_ref[0], 1.0 / error_ref[...], 0.0)
    blocks = []
    for k in range(members):
        blocks.append(jnp.concatenate(split_two(perturb_ref[k]), axis=1))
    field = jnp.concatenate(blocks, axis=0)
    for start in range(0, lines, per_step):
        cell = lane_rows(lambda r: cell_ref[start + r : start + r + 1, :], per_step)
        row = cell // fine_lon
        col = cell - row * fine_lon
        at_col = lax.broadcasted_iota(jnp.int32, (fine_lon, step), 0) == col
        one = jnp.where(at_col, 1.0, 0.0).astype(bf16)
        values = dot(field, jnp.concatenate([one, one], axis=0))
        at_row = lax.broadcasted_iota(jnp.int32, (fine_lat, step), 0) == row
        for k in range(members):
            mine = values[k * fine_lat : (k + 1) * fine_lat]
            found = jnp.sum(jnp.where(at_row, mine, 0.0), axis=0, keepdims=True)
            for r in range(per_step):
                at = (3 + k) * lines + start + r
                out_ref[at : at + 1, :] = found[:, r * LANES : (r + 1) * LANES]


def picked(count, perturb, cell, innovation, error):
    whole = pl.BlockSpec(memory_space=pltpu.VMEM)
    fields = 3 + perturb.shape[0]
    return pl.pallas_call(
        picked_kernel,
        out_shape=jax.ShapeDtypeStruct((fields * cell.shape[0], LANES), f32),
        in_specs=[pl.BlockSpec(memory_space=pltpu.SMEM)] + [whole] * 4,
        out_specs=whole,
        compiler_params=pltpu.CompilerParams(vmem_limit_bytes=60 * 1024 * 1024),
        name="picked",
    )(count, perturb, cell, innovation, error)


def weights_of(observed, innovation, inverse):
    residual = (observed - innovation) * inverse
    return residual / jnp.sqrt(1.0 + residual * residual) * inverse


def length_of(grad_total, curvature):
    return grad_total / (grad_total + curvature + tiny_floor)


def masks(below, count):
    cell = lax.broadcasted_iota(jnp.int32, below.shape, 0).astype(f32)
    found = []
    for start in range(0, count, 16):
        at = (cell + start).astype(bf16)
        before = (cell + (start - 1)).astype(bf16)
        found.append((below == at, below == before))
    return found


def hat(where, lower, upper):
    zero = jnp.zeros_like(lower)
    return jnp.concatenate([jnp.where(at, lower, jnp.where(before, upper, zero)) for at, before in where], axis=0)


def sweep_kernel(first, scale, lon_tiles, members, *refs):
    tile_ref, known_ref = refs[:2]
    refs = refs[2:]
    if not first:
        seen_ref = refs[0]
        refs = refs[1:]
    left_ref, left_low_ref, right_ref, right_low_ref, part_ref, coarse_ref, total_out_ref = refs[:7]
    refs = refs[7:]
    if not first:
        length_ref, own_ref = refs[:2]
        refs = refs[2:]
    hold, total_ref, coarse_own_ref, image_ref, sems = refs
    tiles = known_ref.shape[0]
    lines = known_ref.shape[1] // (3 + members)
    width = total_ref.shape[2]

    def known(n):
        return known_ref[:, n * lines : (n + 1) * lines, :]

    cell = known(0)
    innovation = known(1)
    inverse = known(2)
    row = jnp.floor(cell * (1.0 / 512.0))
    col = (cell - row * 512.0 + 2.5) * 0.25
    row = (row + 2.5) * 0.25
    row_cell, col_cell = jnp.floor(row), jnp.floor(col)
    row_up, col_up = row - row_cell, col - col_cell
    hold[0], hold[1], hold[2], hold[3] = row_cell, col_cell, 1.0 - col_up, col_up
    hold[4], hold[5] = 1.0 - row_up, row_up
    force = weights_of(0.0, innovation, inverse)
    if not first:
        image = seen_ref[...]
        length = length_of(jnp.sum(force * image), jnp.sum((image * inverse) ** 2))
        force = weights_of(-length * image, innovation, inverse) - length * force
        length_ref[...] = jnp.broadcast_to(length, length_ref.shape)
    hold[6] = force
    n = 7
    for k in range(members):
        q = known(3 + k) * force * scale
        for share in (1.0 - row_up, row_up):
            whole = share * q
            high = whole.astype(bf16).astype(f32)
            hold[n] = high
            hold[n + 1] = whole - high
            n += 2
    total_ref[...] = jnp.zeros_like(total_ref)

    def line(i, t):
        return lane_rows(
            lambda r: jnp.broadcast_to(hold[i, t, r : r + 1, :], (16, LANES)).astype(bf16), lines
        )

    def add_tile(t):
        lat = t // lon_tiles
        lon = t - lat * lon_tiles
        cols = hat(masks(line(1, t), COLS), line(2, t), line(3, t))
        where = masks(line(0, t), ROWS)
        blocks = []
        for k in range(members):
            for term in range(2):
                at = 7 + 4 * k + term
                blocks.append(hat(where, line(at, t), line(at + 2, t)))
        made = nt_dot(jnp.concatenate(blocks, axis=0), cols)
        at = pl.ds(pl.multiple_of(lat * 96, 8), ROWS)
        for k in range(members):
            both = made[2 * k * ROWS : (2 * k + 1) * ROWS] + made[(2 * k + 1) * ROWS : (2 * k + 2) * ROWS]
            total_ref[k, at, pl.ds(pl.multiple_of(lon * 128, 128), 128)] += both[:, :128]
            total_ref[k, at, pl.ds(pl.multiple_of(lon * 128 + 128, 128), COLS - 128)] += both[:, 128:]

    def some_tiles(t, carry):
        for n in range(TOGETHER):
            add_tile(t * TOGETHER + n)
        return carry

    lax.fori_loop(0, tiles // TOGETHER, some_tiles, 0)
    total_copy = pltpu.make_async_copy(total_ref, total_out_ref, sems.at[0])
    total_copy.start()

    own = tile_ref[0]
    rows = hat(masks(line(0, own), ROWS), line(4, own), line(5, own)).astype(f32)
    cols = hat(masks(line(1, own), COLS), line(2, own), line(3, own))
    high, low = zip(*(split_two(total_ref[k]) for k in range(members)))
    high, low = jnp.concatenate(high, axis=1), jnp.concatenate(low, axis=1)
    half = dot(jnp.concatenate([left_ref[...], left_low_ref[...]], axis=0), high)
    half = half[:ROWS] + (half[ROWS:] + dot(left_ref[...], low))
    half = jnp.concatenate([half[:, k * width : (k + 1) * width] for k in range(members)], axis=0)
    high, low = split_two(half)
    count = high.shape[0]
    coarse = dot(jnp.concatenate([high, low], axis=0), right_ref[...])
    coarse = coarse[:count] + (coarse[count:] + dot(high, right_low_ref[...]))
    for k in range(members):
        coarse_own_ref[k] = coarse[k * ROWS : (k + 1) * ROWS]
    coarse_copy = pltpu.make_async_copy(coarse_own_ref, coarse_ref, sems.at[1])
    coarse_copy.start()
    made = dot(jnp.concatenate(split_two(coarse), axis=0), cols)
    for k in range(members):
        mine = made[k * ROWS : (k + 1) * ROWS] + made[count + k * ROWS : count + (k + 1) * ROWS]
        value = jnp.sum(mine * rows, axis=0, keepdims=True)
        for r in range(lines):
            image_ref[k, r : r + 1, :] = value[:, r * LANES : (r + 1) * LANES]
    image = jnp.zeros((lines, LANES), f32)
    for k in range(members):
        image = image + image_ref[k] * known_ref[own, (3 + k) * lines : (4 + k) * lines, :]
    image = image * scale
    if not first:
        own_ref[0] = known_ref[own, 2 * lines : 3 * lines, :]
        own_ref[1] = hold[6, own]
    for n in range(part_ref.shape[0]):
        part_ref[n] = image
    coarse_copy.wait()
    total_copy.wait()


def sweep(tile, known, seen, kernels, scale, lon_tiles, members, groups):
    tiles = known.shape[0]
    lines = known.shape[1] // (3 + members)
    first = seen is None
    left, _, right, _ = kernels
    total = (members, left.shape[1], right.shape[0])
    whole = pl.BlockSpec(memory_space=pltpu.VMEM)
    out_shape = [
        jax.ShapeDtypeStruct((groups, lines, LANES), f32),
        pltpu.HBM((members, ROWS, COLS), f32),
        pltpu.HBM(total, f32),
    ]
    far = pl.BlockSpec(memory_space=pltpu.HBM)
    out_specs = [whole, far, far]
    if not first:
        out_shape.append(jax.ShapeDtypeStruct((1, LANES), f32))
        out_shape.append(jax.ShapeDtypeStruct((2, lines, LANES), f32))
        out_specs += [whole, whole]
    arrays = [known] if first else [known, seen]
    arrays += kernels
    return pl.pallas_call(
        functools.partial(sweep_kernel, first, scale, lon_tiles, members),
        out_shape=out_shape,
        in_specs=[pl.BlockSpec(memory_space=pltpu.SMEM)] + [whole] * len(arrays),
        out_specs=out_specs,
        scratch_shapes=[
            pltpu.VMEM((7 + 4 * members, tiles, lines, LANES), f32),
            pltpu.VMEM(total, f32),
            pltpu.VMEM((members, ROWS, COLS), f32),
            pltpu.VMEM((members, lines, LANES), f32),
            pltpu.SemaphoreType.DMA((2,)),
        ],
        compiler_params=pltpu.CompilerParams(vmem_limit_bytes=24 * 1024 * 1024),
        name="sweep_first" if first else "sweep_second",
    )(tile, *arrays)


def ends_length(ends_ref):
    return length_of(jnp.sum(ends_ref[:, 1, :]), jnp.sum(ends_ref[:, 0, :]))


def field_kernel(scale, perturb_ref, length_ref, ends_ref, c1_far, c2_far, out_ref, c1_ref, c2_ref, sems):
    copies = [
        pltpu.make_async_copy(c1_far, c1_ref, sems.at[0]),
        pltpu.make_async_copy(c2_far, c2_ref, sems.at[1]),
    ]
    for copy in copies:
        copy.start()
    members, fine_lat, fine_lon = perturb_ref.shape
    pieces, piece_rows, piece_cols = out_ref.shape
    across = fine_lon // piece_cols
    one = length_ref[0, 0]
    two = ends_length(ends_ref)

    def refined(count, cells, axis):
        shape = (count, cells) if axis == 0 else (cells, count)
        fine = lax.broadcasted_iota(jnp.int32, shape, axis).astype(f32)
        cell = lax.broadcasted_iota(jnp.int32, shape, 1 - axis).astype(f32)
        return jnp.maximum(1.0 - jnp.abs((fine + 2.5) * 0.25 - cell), 0.0).astype(bf16)

    to_rows = refined(fine_lat, ROWS, 0)
    to_cols = refined(fine_lon, COLS, 1)
    field = jnp.zeros((fine_lat, fine_lon), f32)
    for copy in copies:
        copy.wait()
    for k in range(members):
        coarse = one * c1_ref[k] + two * c2_ref[k]
        high, low = split_two(coarse)
        tall = dot(to_rows, high) + dot(to_rows, low)
        high, low = split_two(tall)
        field = field + (dot(high, to_cols) + dot(low, to_cols)) * perturb_ref[k]
    field = -scale * field
    for n in range(pieces * piece_rows // 8):
        i = n // across * 8
        j = n % across * piece_cols
        at = n * 8 % piece_rows
        out_ref[n * 8 // piece_rows, at : at + 8, :] = field[i : i + 8, j : j + piece_cols]


def analysis_kernel(length_ref, ends_ref, total_1_ref, total_2_ref, left_ref, right_ref, out_ref):
    one = length_ref[0, 0]
    two = ends_length(ends_ref)
    for k in range(out_ref.shape[0]):
        total = one * total_1_ref[k] + two * total_2_ref[k]
        half = jnp.dot(left_ref[...], total, precision=highest, preferred_element_type=f32)
        out_ref[k] = -jnp.dot(half, right_ref[...], precision=highest, preferred_element_type=f32)


def per_device(perturb, loc_lat, loc_lon, obs_cell, obs_count, obs_innov, obs_error):
    members, fine_lat, fine_lon = perturb.shape
    coarse_lat, coarse_lon = fine_lat // 4, fine_lon // 4
    groups = lax.axis_size(MEM)
    scale = 1.0 / math.sqrt(members * groups - 1)
    lat, lon = lax.axis_index(LAT), lax.axis_index("lon")
    lat_tiles, lon_tiles = lax.axis_size(LAT), lax.axis_size("lon")
    slots = obs_cell.shape[-1]
    total_lat, total_lon = lat_tiles * coarse_lat, lon_tiles * coarse_lon
    padded_lat, padded_lon = total_lat + 16, total_lon + 128
    tile = (lat * lon_tiles + lon).astype(jnp.int32).reshape(1)

    lines = slots // LANES
    cell = obs_cell.reshape(lines, LANES)
    innovation = obs_innov.reshape(lines, LANES)
    error = obs_error.reshape(lines, LANES)
    message = picked(obs_count.reshape(1), perturb, cell, innovation, error)
    known = sent_to_all(message, TILES)

    first_lat, first_lon = lat * coarse_lat, lon * coarse_lon
    lat_all = kernel_block(loc_lat, -1, padded_lat, 0, total_lat)
    lon_all = kernel_block(loc_lon, -1, padded_lon, 0, total_lon)
    lat_tile = kernel_block(loc_lat, first_lat - 1, ROWS, 0, total_lat)
    lon_tile = kernel_block(loc_lon, first_lon - 1, COLS, 0, total_lon)
    left = jnp.einsum("ab,cb->ac", lat_tile, lat_all, precision=highest)
    right = jnp.einsum("ab,cb->ac", lon_all, lon_tile, precision=highest)
    left_own = kernel_block(loc_lat, -1, padded_lat, first_lat, coarse_lat).T
    right_own = kernel_block(loc_lon, -1, padded_lon, first_lon, coarse_lon)
    kernels = [*split_two(left), *split_two(right)]

    part, coarse_1, total_1 = sweep(tile, known, None, kernels, scale, lon_tiles, members, groups)
    mine = jnp.sum(lax.all_to_all(part, MEM, 0, 0, tiled=True), axis=0)
    seen = sent_to_all(mine, TILES)
    part, coarse_2, total_2, length_1, own = sweep(
        tile, known, seen, kernels, scale, lon_tiles, members, groups
    )
    mine = jnp.sum(lax.all_to_all(part, MEM, 0, 0, tiled=True), axis=0)
    bent = jnp.sum(jnp.stack([(mine * own[0]) ** 2, mine * own[1]]), axis=1)
    ends = sent_to_all(bent, TILES)

    whole = pl.BlockSpec(memory_space=pltpu.VMEM)
    piece_cols = 128
    piece_rows = fine_lat * fine_lon // groups // piece_cols
    pieces = pl.pallas_call(
        functools.partial(field_kernel, scale),
        out_shape=jax.ShapeDtypeStruct((groups, piece_rows, piece_cols), f32),
        in_specs=[whole] * 3 + [pl.BlockSpec(memory_space=pltpu.HBM)] * 2,
        out_specs=whole,
        scratch_shapes=[
            pltpu.VMEM((members, ROWS, COLS), f32),
            pltpu.VMEM((members, ROWS, COLS), f32),
            pltpu.SemaphoreType.DMA((2,)),
        ],
        compiler_params=pltpu.CompilerParams(vmem_limit_bytes=24 * 1024 * 1024),
        name="field",
    )(perturb, length_1, ends, coarse_1, coarse_2)
    analysis = pl.pallas_call(
        analysis_kernel,
        out_shape=jax.ShapeDtypeStruct((members, coarse_lat, coarse_lon), f32),
        in_specs=[whole] * 6,
        out_specs=whole,
        compiler_params=pltpu.CompilerParams(vmem_limit_bytes=24 * 1024 * 1024),
        cost_estimate=pl.CostEstimate(flops=2 * 10**9, bytes_accessed=5 * 10**6, transcendentals=0),
        name="analysis",
    )(length_1, ends, total_1, total_2, left_own, right_own)
    summed = jnp.sum(lax.all_to_all(pieces, MEM, 0, 0, tiled=True), axis=0)
    everything = sent_to_all(summed, MEM)
    across = fine_lon // piece_cols
    increment = jnp.transpose(
        everything.reshape(fine_lat // 8, across, 8, piece_cols), (0, 2, 1, 3)
    ).reshape(fine_lat, fine_lon)
    return analysis, increment


def solution(mesh):
    torus = Mesh(
        mesh.devices.reshape(4, -1, 2, mesh.shape["lat"] // 2, mesh.shape["lon"]),
        ("mem_0", "mem_1", "lat_0", "lat_1", "lon"),
    )
    return jax.shard_map(
        per_device,
        mesh=torus,
        in_specs=(
            P(MEM, LAT, "lon"),
            P(),
            P(),
            P(LAT, "lon", None),
            P(LAT, "lon"),
            P(LAT, "lon", None),
            P(LAT, "lon", None),
        ),
        out_specs=(P(MEM, LAT, "lon"), P(LAT, "lon")),
        check_vma=False,
    )
```

```python
import functools
import math

import jax
import jax.numpy as jnp
from jax import lax
from jax.experimental import pallas as pl
from jax.experimental.pallas import tpu as pltpu
from jax.sharding import Mesh
from jax.sharding import PartitionSpec as P

MEM = ("mem_0", "mem_1")
LAT = ("lat_0", "lat_1")
TILES = ("lat_0", "lat_1", "lon")
X, Z = "mem_0", "mem_1"

tiny_floor = 1e-06
highest = lax.Precision.HIGHEST
f32 = jnp.float32
bf16 = jnp.bfloat16

ROWS = 112
COLS = 144
LANES = 128
TOGETHER = 2


def sent_to_all(x, axis):
    copies = jnp.broadcast_to(x, (lax.axis_size(axis), *x.shape))
    return lax.all_to_all(copies, axis, split_axis=0, concat_axis=0, tiled=True)


def scale_run(scales, first, count):
    padded = jnp.pad(scales, (8, 248), constant_values=1.0)
    return lax.dynamic_slice(padded, (first + 8,), (count,))


def kernel_block(scales, first_row, row_count, first_col, col_count):
    total = scales.shape[0]
    rows = first_row + jnp.arange(row_count, dtype=jnp.int32)
    cols = first_col + jnp.arange(col_count, dtype=jnp.int32)
    row_scale = scale_run(scales, first_row, row_count)
    col_scale = scale_run(scales, first_col, col_count)
    inside = (rows >= 0) & (rows < total)
    weight = jnp.where(inside, (jnp.sqrt(jnp.pi) * row_scale) ** (-0.5), jnp.zeros_like(row_scale))
    offset = (rows[:, None] - cols[None, :]).astype(f32)
    spread = row_scale[:, None] ** 2 + col_scale[None, :] ** 2
    return weight[:, None] * jnp.exp(-offset * offset / spread)


def split_two(x):
    high = x.astype(bf16)
    low = (x - high.astype(f32)).astype(bf16)
    return high, low


def nt_dot(a, b):
    return lax.dot_general(a, b, (((1,), (1,)), ((), ())), preferred_element_type=f32)


def dot(a, b):
    return jnp.dot(a, b, preferred_element_type=f32)


def lane_rows(read, count):
    return jnp.concatenate([read(r) for r in range(count)], axis=1)


def picked_kernel(count_ref, perturb_ref, cell_ref, innov_ref, error_ref, copies_ref, out_ref, sems):
    members, fine_lat, fine_lon = perturb_ref.shape
    lines = cell_ref.shape[0]
    step = 512
    per_step = step // LANES
    slot = lax.broadcasted_iota(jnp.int32, cell_ref.shape, 0) * LANES + lax.broadcasted_iota(
        jnp.int32, cell_ref.shape, 1
    )
    out_ref[:lines] = cell_ref[...].astype(f32)
    out_ref[lines : 2 * lines] = innov_ref[...]
    out_ref[2 * lines : 3 * lines] = jnp.where(slot < count_ref[0], 1.0 / error_ref[...], 0.0)
    blocks = []
    for k in range(members):
        blocks.append(jnp.concatenate(split_two(perturb_ref[k]), axis=1))
    field = jnp.concatenate(blocks, axis=0)
    for start in range(0, lines, per_step):
        cell = lane_rows(lambda r: cell_ref[start + r : start + r + 1, :], per_step)
        row = cell // fine_lon
        col = cell - row * fine_lon
        at_col = lax.broadcasted_iota(jnp.int32, (fine_lon, step), 0) == col
        one = jnp.where(at_col, 1.0, 0.0).astype(bf16)
        values = dot(field, jnp.concatenate([one, one], axis=0))
        at_row = lax.broadcasted_iota(jnp.int32, (fine_lat, step), 0) == row
        for k in range(members):
            mine = values[k * fine_lat : (k + 1) * fine_lat]
            found = jnp.sum(jnp.where(at_row, mine, 0.0), axis=0, keepdims=True)
            for r in range(per_step):
                at = (3 + k) * lines + start + r
                out_ref[at : at + 1, :] = found[:, r * LANES : (r + 1) * LANES]
    sends = [
        pltpu.make_async_copy(out_ref, copies_ref.at[n], sems.at[n]) for n in range(copies_ref.shape[0])
    ]
    for send in sends:
        send.start()
    for send in sends:
        send.wait()


def picked(count, perturb, cell, innovation, error, copies):
    whole = pl.BlockSpec(memory_space=pltpu.VMEM)
    message = ((3 + perturb.shape[0]) * cell.shape[0], LANES)
    return pl.pallas_call(
        picked_kernel,
        out_shape=pltpu.HBM((copies, *message), f32),
        in_specs=[pl.BlockSpec(memory_space=pltpu.SMEM)] + [whole] * 4,
        out_specs=pl.BlockSpec(memory_space=pltpu.HBM),
        scratch_shapes=[pltpu.VMEM(message, f32), pltpu.SemaphoreType.DMA((copies,))],
        compiler_params=pltpu.CompilerParams(vmem_limit_bytes=60 * 1024 * 1024),
        name="picked",
    )(count, perturb, cell, innovation, error)


def weights_of(observed, innovation, inverse):
    residual = (observed - innovation) * inverse
    return residual / jnp.sqrt(1.0 + residual * residual) * inverse


def length_of(grad_total, curvature):
    return grad_total / (grad_total + curvature + tiny_floor)


def masks(below, count):
    cell = lax.broadcasted_iota(jnp.int32, below.shape, 0).astype(f32)
    found = []
    for start in range(0, count, 16):
        at = (cell + start).astype(bf16)
        before = (cell + (start - 1)).astype(bf16)
        found.append((below == at, below == before))
    return found


def hat(where, lower, upper):
    zero = jnp.zeros_like(lower)
    return jnp.concatenate([jnp.where(at, lower, jnp.where(before, upper, zero)) for at, before in where], axis=0)


def sweep_kernel(first, scale, lon_tiles, members, *refs):
    tile_ref, known_ref = refs[:2]
    refs = refs[2:]
    if not first:
        seen_ref, perturb_far = refs[:2]
        refs = refs[2:]
    left_ref, left_low_ref, right_ref, right_low_ref, part_ref, total_out_ref = refs[:6]
    refs = refs[6:]
    if first:
        coarse_ref = refs[0]
        refs = refs[1:]
    else:
        length_ref, own_ref = refs[:2]
        refs = refs[2:]
    hold, total_ref, coarse_own_ref, image_ref, sems = refs[:5]
    if not first:
        perturb_ref = refs[5]
        perturb_copy = pltpu.make_async_copy(perturb_far, perturb_ref, sems.at[1])
        perturb_copy.start()
    tiles = known_ref.shape[0]
    lines = known_ref.shape[1] // (3 + members)
    width = total_ref.shape[2]

    def known(n):
        return known_ref[:, n * lines : (n + 1) * lines, :]

    cell = known(0)
    innovation = known(1)
    inverse = known(2)
    row = jnp.floor(cell * (1.0 / 512.0))
    col = (cell - row * 512.0 + 2.5) * 0.25
    row = (row + 2.5) * 0.25
    row_cell, col_cell = jnp.floor(row), jnp.floor(col)
    row_up, col_up = row - row_cell, col - col_cell
    hold[0], hold[1], hold[2], hold[3] = row_cell, col_cell, 1.0 - col_up, col_up
    hold[4], hold[5] = 1.0 - row_up, row_up
    force = weights_of(0.0, innovation, inverse)
    if not first:
        image = seen_ref[...]
        length = length_of(jnp.sum(force * image), jnp.sum((image * inverse) ** 2))
        force = weights_of(-length * image, innovation, inverse) - length * force
        length_ref[...] = jnp.broadcast_to(length, length_ref.shape)
    hold[6] = force
    n = 7
    for k in range(members):
        q = known(3 + k) * force * scale
        for share in (1.0 - row_up, row_up):
            whole = share * q
            high = whole.astype(bf16).astype(f32)
            hold[n] = high
            hold[n + 1] = whole - high
            n += 2
    total_ref[...] = jnp.zeros_like(total_ref)

    def line(i, t):
        return lane_rows(
            lambda r: jnp.broadcast_to(hold[i, t, r : r + 1, :], (16, LANES)).astype(bf16), lines
        )

    def add_tile(t):
        lat = t // lon_tiles
        lon = t - lat * lon_tiles
        cols = hat(masks(line(1, t), COLS), line(2, t), line(3, t))
        where = masks(line(0, t), ROWS)
        blocks = []
        for k in range(members):
            for term in range(2):
                at = 7 + 4 * k + term
                blocks.append(hat(where, line(at, t), line(at + 2, t)))
        made = nt_dot(jnp.concatenate(blocks, axis=0), cols)
        at = pl.ds(pl.multiple_of(lat * 96, 8), ROWS)
        for k in range(members):
            both = made[2 * k * ROWS : (2 * k + 1) * ROWS] + made[(2 * k + 1) * ROWS : (2 * k + 2) * ROWS]
            total_ref[k, at, pl.ds(pl.multiple_of(lon * 128, 128), 128)] += both[:, :128]
            total_ref[k, at, pl.ds(pl.multiple_of(lon * 128 + 128, 128), COLS - 128)] += both[:, 128:]

    def some_tiles(t, carry):
        for n in range(TOGETHER):
            add_tile(t * TOGETHER + n)
        return carry

    lax.fori_loop(0, tiles // TOGETHER, some_tiles, 0)
    total_copy = pltpu.make_async_copy(total_ref, total_out_ref, sems.at[0])
    total_copy.start()

    own = tile_ref[0]
    rows = hat(masks(line(0, own), ROWS), line(4, own), line(5, own)).astype(f32)
    cols = hat(masks(line(1, own), COLS), line(2, own), line(3, own))
    high, low = zip(*(split_two(total_ref[k]) for k in range(members)))
    high, low = jnp.concatenate(high, axis=1), jnp.concatenate(low, axis=1)
    half = dot(jnp.concatenate([left_ref[...], left_low_ref[...]], axis=0), high)
    half = half[:ROWS] + (half[ROWS:] + dot(left_ref[...], low))
    half = jnp.concatenate([half[:, k * width : (k + 1) * width] for k in range(members)], axis=0)
    high, low = split_two(half)
    count = high.shape[0]
    coarse = dot(jnp.concatenate([high, low], axis=0), right_ref[...])
    coarse = coarse[:count] + (coarse[count:] + dot(high, right_low_ref[...]))
    for k in range(members):
        coarse_own_ref[k] = coarse[k * ROWS : (k + 1) * ROWS]
    if first:
        coarse_copy = pltpu.make_async_copy(coarse_own_ref, coarse_ref, sems.at[1])
        coarse_copy.start()
    made = dot(jnp.concatenate(split_two(coarse), axis=0), cols)
    for k in range(members):
        mine = made[k * ROWS : (k + 1) * ROWS] + made[count + k * ROWS : count + (k + 1) * ROWS]
        value = jnp.sum(mine * rows, axis=0, keepdims=True)
        for r in range(lines):
            image_ref[k, r : r + 1, :] = value[:, r * LANES : (r + 1) * LANES]
    image = jnp.zeros((lines, LANES), f32)
    for k in range(members):
        image = image + image_ref[k] * known_ref[own, (3 + k) * lines : (4 + k) * lines, :]
    image = image * scale
    if not first:
        own_ref[0] = known_ref[own, 2 * lines : 3 * lines, :]
        own_ref[1] = hold[6, own]
    for n in range(part_ref.shape[0]):
        part_ref[n, :lines, :] = image
    if not first:
        perturb_copy.wait()
        put_field(perturb_ref, coarse_own_ref, scale, part_ref, lines)
    else:
        coarse_copy.wait()
    total_copy.wait()


def sweep(tile, known, seen, perturb, kernels, scale, lon_tiles, part):
    members, fine_lat, fine_lon = perturb.shape
    tiles = known.shape[0]
    lines = known.shape[1] // (3 + members)
    first = seen is None
    left, _, right, _ = kernels
    total = (members, left.shape[1], right.shape[0])
    whole = pl.BlockSpec(memory_space=pltpu.VMEM)
    far = pl.BlockSpec(memory_space=pltpu.HBM)
    out_shape = [jax.ShapeDtypeStruct(part, f32), pltpu.HBM(total, f32)]
    out_specs = [whole, far]
    if first:
        out_shape.append(pltpu.HBM((members, ROWS, COLS), f32))
        out_specs.append(far)
    else:
        out_shape.append(jax.ShapeDtypeStruct((1, LANES), f32))
        out_shape.append(jax.ShapeDtypeStruct((2, lines, LANES), f32))
        out_specs += [whole, whole]
    arrays = [known] if first else [known, seen, perturb]
    in_specs = [whole] if first else [whole, whole, far]
    arrays += kernels
    in_specs += [whole] * len(kernels)
    scratch = [
        pltpu.VMEM((7 + 4 * members, tiles, lines, LANES), f32),
        pltpu.VMEM(total, f32),
        pltpu.VMEM((members, ROWS, COLS), f32),
        pltpu.VMEM((members, lines, LANES), f32),
        pltpu.SemaphoreType.DMA((2,)),
    ]
    if not first:
        scratch.append(pltpu.VMEM(perturb.shape, f32))
    return pl.pallas_call(
        functools.partial(sweep_kernel, first, scale, lon_tiles, members),
        out_shape=out_shape,
        in_specs=[pl.BlockSpec(memory_space=pltpu.SMEM)] + in_specs,
        out_specs=out_specs,
        scratch_shapes=scratch,
        compiler_params=pltpu.CompilerParams(vmem_limit_bytes=60 * 1024 * 1024),
        cost_estimate=pl.CostEstimate(flops=8 * 10**9, bytes_accessed=10**7, transcendentals=0),
        name="sweep_first" if first else "sweep_second",
    )(tile, *arrays)


def refined(count, cells, axis):
    shape = (count, cells) if axis == 0 else (cells, count)
    fine = lax.broadcasted_iota(jnp.int32, shape, axis).astype(f32)
    cell = lax.broadcasted_iota(jnp.int32, shape, 1 - axis).astype(f32)
    return jnp.maximum(1.0 - jnp.abs((fine + 2.5) * 0.25 - cell), 0.0).astype(bf16)


def put_field(perturb_ref, coarse, scale, out_ref, skip):
    members, fine_lat, fine_lon = perturb_ref.shape
    to_rows = refined(fine_lat, ROWS, 0)
    to_cols = refined(fine_lon, COLS, 1)
    field = jnp.zeros((fine_lat, fine_lon), f32)
    for k in range(members):
        high, low = split_two(coarse[k])
        tall = dot(to_rows, high) + dot(to_rows, low)
        high, low = split_two(tall)
        field = field + (dot(high, to_cols) + dot(low, to_cols)) * perturb_ref[k]
    field = scale * field
    across = fine_lon // LANES
    per_part = fine_lat // 8 * across // out_ref.shape[0]
    for n in range(per_part * out_ref.shape[0]):
        i = n // across * 8
        j = n % across * LANES
        at = skip + n % per_part * 8
        out_ref[n // per_part, at : at + 8, :] = field[i : i + 8, j : j + LANES]


def field_kernel(scale, perturb_ref, coarse_ref, out_ref):
    put_field(perturb_ref, coarse_ref, scale, out_ref, 0)


def gather_x_kernel(image_and_second_ref, first_ref, out_ref):
    parts = out_ref.shape[0]
    lines = image_and_second_ref.shape[1] - first_ref.shape[1]
    rows = first_ref.shape[1] // parts
    image = jnp.sum(image_and_second_ref[:, :lines, :], axis=0)
    for n in range(parts):
        out_ref[n, :lines, :] = image
        out_ref[n, lines : lines + rows, :] = jnp.sum(first_ref[:, n * rows : (n + 1) * rows, :], axis=0)
        at = lines + n * rows
        out_ref[n, lines + rows :, :] = jnp.sum(image_and_second_ref[:, at : at + rows, :], axis=0)


def gather_z_kernel(arrived_ref, own_ref, bent_ref, fields_ref):
    lines = own_ref.shape[1]
    image = jnp.sum(arrived_ref[:, :lines, :], axis=0)
    fields_ref[...] = jnp.sum(arrived_ref[:, lines:, :], axis=0)
    bent = jnp.sum((image * own_ref[0]) ** 2, axis=0, keepdims=True)
    gain = jnp.sum(image * own_ref[1], axis=0, keepdims=True)
    both = jnp.concatenate([bent, gain], axis=0)
    for n in range(bent_ref.shape[0]):
        bent_ref[n] = both


def ends_length(ends_ref):
    return length_of(jnp.sum(ends_ref[:, 1, :]), jnp.sum(ends_ref[:, 0, :]))


def finish_kernel(length_ref, ends_ref, fields_ref, out_ref):
    rows = fields_ref.shape[0] // 2
    one = length_ref[0, 0]
    two = ends_length(ends_ref)
    done = -(one * fields_ref[:rows] + two * fields_ref[rows:])
    for n in range(out_ref.shape[0]):
        out_ref[n] = done


def analysis_kernel(length_ref, ends_ref, total_1_ref, total_2_ref, left_ref, right_ref, out_ref):
    one = length_ref[0, 0]
    two = ends_length(ends_ref)
    for k in range(out_ref.shape[0]):
        total = one * total_1_ref[k] + two * total_2_ref[k]
        half = jnp.dot(left_ref[...], total, precision=highest, preferred_element_type=f32)
        out_ref[k] = -jnp.dot(half, right_ref[...], precision=highest, preferred_element_type=f32)


def small_call(kernel, shapes, flops, name, *arrays):
    whole = pl.BlockSpec(memory_space=pltpu.VMEM)
    made = pl.pallas_call(
        kernel,
        out_shape=[jax.ShapeDtypeStruct(shape, f32) for shape in shapes],
        in_specs=[whole] * len(arrays),
        out_specs=[whole] * len(shapes),
        compiler_params=pltpu.CompilerParams(vmem_limit_bytes=60 * 1024 * 1024),
        cost_estimate=pl.CostEstimate(flops=flops, bytes_accessed=2 * 10**6, transcendentals=0),
        name=name,
    )(*arrays)
    return made if len(shapes) > 1 else made[0]


def per_device(perturb, loc_lat, loc_lon, obs_cell, obs_count, obs_innov, obs_error):
    members, fine_lat, fine_lon = perturb.shape
    coarse_lat, coarse_lon = fine_lat // 4, fine_lon // 4
    groups = lax.axis_size(MEM)
    scale = 1.0 / math.sqrt(members * groups - 1)
    lat, lon = lax.axis_index(LAT), lax.axis_index("lon")
    lat_tiles, lon_tiles = lax.axis_size(LAT), lax.axis_size("lon")
    slots = obs_cell.shape[-1]
    total_lat, total_lon = lat_tiles * coarse_lat, lon_tiles * coarse_lon
    padded_lat, padded_lon = total_lat + 16, total_lon + 128
    tile = (lat * lon_tiles + lon).astype(jnp.int32).reshape(1)

    lines = slots // LANES
    cell = obs_cell.reshape(lines, LANES)
    innovation = obs_innov.reshape(lines, LANES)
    error = obs_error.reshape(lines, LANES)
    message = picked(obs_count.reshape(1), perturb, cell, innovation, error, lat_tiles * lon_tiles)
    known = lax.all_to_all(message, TILES, 0, 0, tiled=True)

    first_lat, first_lon = lat * coarse_lat, lon * coarse_lon
    lat_all = kernel_block(loc_lat, -1, padded_lat, 0, total_lat)
    lon_all = kernel_block(loc_lon, -1, padded_lon, 0, total_lon)
    lat_tile = kernel_block(loc_lat, first_lat - 1, ROWS, 0, total_lat)
    lon_tile = kernel_block(loc_lon, first_lon - 1, COLS, 0, total_lon)
    left = jnp.einsum("ab,cb->ac", lat_tile, lat_all, precision=highest)
    right = jnp.einsum("ab,cb->ac", lon_all, lon_tile, precision=highest)
    left_own = kernel_block(loc_lat, -1, padded_lat, first_lat, coarse_lat).T
    right_own = kernel_block(loc_lon, -1, padded_lon, first_lon, coarse_lon)
    kernels = [*split_two(left), *split_two(right)]

    field_rows = fine_lat * fine_lon // LANES
    along_x, along_z = lax.axis_size(X), lax.axis_size(Z)
    part_rows, piece_rows = field_rows // along_x, field_rows // groups
    part, total_1, coarse_1 = sweep(
        tile, known, None, perturb, kernels, scale, lon_tiles, (groups, lines, LANES)
    )
    first_field = small_call(
        functools.partial(field_kernel, scale), ((along_x, part_rows, LANES),), 3 * 10**8, "field", perturb, coarse_1
    )
    mine = jnp.sum(lax.all_to_all(part, MEM, 0, 0, tiled=True), axis=0)
    seen = sent_to_all(mine, TILES)
    first_field, seen = lax.optimization_barrier((first_field, seen))
    first_field = lax.all_to_all(first_field, X, 0, 0, tiled=True)
    part, total_2, length_1, own = sweep(
        tile, known, seen, perturb, kernels, scale, lon_tiles, (along_x, lines + part_rows, LANES)
    )
    part = lax.all_to_all(part, X, 0, 0, tiled=True)
    part = small_call(
        gather_x_kernel, ((along_z, lines + 2 * piece_rows, LANES),), 10**6, "gather_x", part, first_field
    )
    part = lax.all_to_all(part, Z, 0, 0, tiled=True)
    bent, fields = small_call(
        gather_z_kernel,
        ((lat_tiles * lon_tiles, 2, LANES), (2 * piece_rows, LANES)),
        10**6,
        "gather_z",
        part,
        own,
    )
    ends = lax.all_to_all(bent, TILES, 0, 0, tiled=True)
    done = small_call(finish_kernel, ((along_z, piece_rows, LANES),), 10**6, "finish", length_1, ends, fields)
    done = lax.all_to_all(done, Z, 0, 0, tiled=True).reshape(part_rows, LANES)
    everything = sent_to_all(done, X)
    whole = pl.BlockSpec(memory_space=pltpu.VMEM)
    analysis = pl.pallas_call(
        analysis_kernel,
        out_shape=jax.ShapeDtypeStruct((members, coarse_lat, coarse_lon), f32),
        in_specs=[whole] * 6,
        out_specs=whole,
        compiler_params=pltpu.CompilerParams(vmem_limit_bytes=60 * 1024 * 1024),
        cost_estimate=pl.CostEstimate(flops=2 * 10**9, bytes_accessed=5 * 10**6, transcendentals=0),
        name="analysis",
    )(length_1, ends, total_1, total_2, left_own, right_own)
    across = fine_lon // LANES
    increment = jnp.transpose(
        everything.reshape(fine_lat // 8, across, 8, LANES), (0, 2, 1, 3)
    ).reshape(fine_lat, fine_lon)
    return analysis, increment


def solution(mesh):
    torus = Mesh(
        mesh.devices.reshape(4, -1, 2, mesh.shape["lat"] // 2, mesh.shape["lon"]),
        ("mem_0", "mem_1", "lat_0", "lat_1", "lon"),
    )
    return jax.shard_map(
        per_device,
        mesh=torus,
        in_specs=(
            P(MEM, LAT, "lon"),
            P(),
            P(),
            P(LAT, "lon", None),
            P(LAT, "lon"),
            P(LAT, "lon", None),
            P(LAT, "lon", None),
        ),
        out_specs=(P(MEM, LAT, "lon"), P(LAT, "lon")),
        check_vma=False,
    )
```

```python
import functools
import math

import jax
import jax.numpy as jnp
from jax import lax
from jax.experimental import pallas as pl
from jax.experimental.pallas import tpu as pltpu
from jax.sharding import Mesh
from jax.sharding import PartitionSpec as P

MEM = ("mem_0", "mem_1")
LAT = ("lat_0", "lat_1")
TILES = ("lat_0", "lat_1", "lon")
X, Z = "mem_0", "mem_1"

tiny_floor = 1e-06
highest = lax.Precision.HIGHEST
f32 = jnp.float32
bf16 = jnp.bfloat16

ROWS = 112
COLS = 144
LANES = 128


def sent_to_all(x, axis):
    copies = jnp.broadcast_to(x, (lax.axis_size(axis), *x.shape))
    return lax.all_to_all(copies, axis, split_axis=0, concat_axis=0, tiled=True)


def scale_run(scales, first, count):
    padded = jnp.pad(scales, (8, 248), constant_values=1.0)
    return lax.dynamic_slice(padded, (first + 8,), (count,))


def kernel_block(scales, first_row, row_count, first_col, col_count):
    total = scales.shape[0]
    rows = first_row + jnp.arange(row_count, dtype=jnp.int32)
    cols = first_col + jnp.arange(col_count, dtype=jnp.int32)
    row_scale = scale_run(scales, first_row, row_count)
    col_scale = scale_run(scales, first_col, col_count)
    inside = (rows >= 0) & (rows < total)
    weight = jnp.where(inside, (jnp.sqrt(jnp.pi) * row_scale) ** (-0.5), jnp.zeros_like(row_scale))
    offset = (rows[:, None] - cols[None, :]).astype(f32)
    spread = row_scale[:, None] ** 2 + col_scale[None, :] ** 2
    return weight[:, None] * jnp.exp(-offset * offset / spread)


def split_two(x):
    high = x.astype(bf16)
    low = (x - high.astype(f32)).astype(bf16)
    return high, low


def nt_dot(a, b):
    return lax.dot_general(a, b, (((1,), (1,)), ((), ())), preferred_element_type=f32)


def dot(a, b):
    return jnp.dot(a, b, preferred_element_type=f32)


def lane_rows(read, count):
    return jnp.concatenate([read(r) for r in range(count)], axis=1)


def picked_kernel(count_ref, perturb_ref, cell_ref, innov_ref, error_ref, copies_ref, out_ref, sems):
    members, fine_lat, fine_lon = perturb_ref.shape
    lines = cell_ref.shape[0]
    step = 512
    per_step = step // LANES
    slot = lax.broadcasted_iota(jnp.int32, cell_ref.shape, 0) * LANES + lax.broadcasted_iota(
        jnp.int32, cell_ref.shape, 1
    )
    out_ref[:lines] = cell_ref[...].astype(f32)
    out_ref[lines : 2 * lines] = innov_ref[...]
    out_ref[2 * lines : 3 * lines] = jnp.where(slot < count_ref[0], 1.0 / error_ref[...], 0.0)
    blocks = []
    for k in range(members):
        blocks.append(jnp.concatenate(split_two(perturb_ref[k]), axis=1))
    field = jnp.concatenate(blocks, axis=0)
    for start in range(0, lines, per_step):
        cell = lane_rows(lambda r: cell_ref[start + r : start + r + 1, :], per_step)
        row = cell // fine_lon
        col = cell - row * fine_lon
        at_col = lax.broadcasted_iota(jnp.int32, (fine_lon, step), 0) == col
        one = jnp.where(at_col, 1.0, 0.0).astype(bf16)
        values = dot(field, jnp.concatenate([one, one], axis=0))
        at_row = lax.broadcasted_iota(jnp.int32, (fine_lat, step), 0) == row
        for k in range(members):
            mine = values[k * fine_lat : (k + 1) * fine_lat]
            found = jnp.sum(jnp.where(at_row, mine, 0.0), axis=0, keepdims=True)
            for r in range(per_step):
                at = (3 + k) * lines + start + r
                out_ref[at : at + 1, :] = found[:, r * LANES : (r + 1) * LANES]
    sends = [
        pltpu.make_async_copy(out_ref, copies_ref.at[n], sems.at[n]) for n in range(copies_ref.shape[0])
    ]
    for send in sends:
        send.start()
    for send in sends:
        send.wait()


def picked(count, perturb, cell, innovation, error, copies):
    whole = pl.BlockSpec(memory_space=pltpu.VMEM)
    message = ((3 + perturb.shape[0]) * cell.shape[0], LANES)
    return pl.pallas_call(
        picked_kernel,
        out_shape=pltpu.HBM((copies, *message), f32),
        in_specs=[pl.BlockSpec(memory_space=pltpu.SMEM)] + [whole] * 4,
        out_specs=pl.BlockSpec(memory_space=pltpu.HBM),
        scratch_shapes=[pltpu.VMEM(message, f32), pltpu.SemaphoreType.DMA((copies,))],
        compiler_params=pltpu.CompilerParams(vmem_limit_bytes=60 * 1024 * 1024),
        name="picked",
    )(count, perturb, cell, innovation, error)


def weights_of(observed, innovation, inverse):
    residual = (observed - innovation) * inverse
    return residual / jnp.sqrt(1.0 + residual * residual) * inverse


def length_of(grad_total, curvature):
    return grad_total / (grad_total + curvature + tiny_floor)


def masks(below, count):
    cell = lax.broadcasted_iota(jnp.int32, below.shape, 0).astype(f32)
    found = []
    for start in range(0, count, 16):
        at = (cell + start).astype(bf16)
        before = (cell + (start - 1)).astype(bf16)
        found.append((below == at, below == before))
    return found


def hat(where, lower, upper):
    zero = jnp.zeros_like(lower)
    return jnp.concatenate([jnp.where(at, lower, jnp.where(before, upper, zero)) for at, before in where], axis=0)


def sweep_kernel(first, scale, lon_tiles, members, *refs):
    tile_ref, known_ref = refs[:2]
    refs = refs[2:]
    if not first:
        seen_ref = refs[0]
        refs = refs[1:]
    left_ref, left_low_ref, right_ref, right_low_ref, part_ref, coarse_ref, total_out_ref = refs[:7]
    refs = refs[7:]
    if not first:
        length_ref, own_ref = refs[:2]
        refs = refs[2:]
    hold, total_ref, coarse_own_ref, image_ref, quarters_ref, sems = refs
    tiles = known_ref.shape[0]
    lines = known_ref.shape[1] // (3 + members)
    width = total_ref.shape[2]

    def known(n):
        return known_ref[:, n * lines : (n + 1) * lines, :]

    cell = known(0)
    innovation = known(1)
    inverse = known(2)
    row = jnp.floor(cell * (1.0 / 512.0))
    col = (cell - row * 512.0 + 2.5) * 0.25
    row = (row + 2.5) * 0.25
    row_cell, col_cell = jnp.floor(row), jnp.floor(col)
    row_up, col_up = row - row_cell, col - col_cell
    hold[0], hold[1], hold[2], hold[3] = row_cell, col_cell, 1.0 - col_up, col_up
    hold[4], hold[5] = 1.0 - row_up, row_up
    force = weights_of(0.0, innovation, inverse)
    if not first:
        image = seen_ref[...]
        length = length_of(jnp.sum(force * image), jnp.sum((image * inverse) ** 2))
        force = weights_of(-length * image, innovation, inverse) - length * force
        length_ref[...] = jnp.broadcast_to(length, length_ref.shape)
    hold[6] = force
    n = 7
    for k in range(members):
        q = known(3 + k) * force * scale
        for share in (1.0 - row_up, row_up):
            whole = share * q
            high = whole.astype(bf16).astype(f32)
            hold[n] = high
            hold[n + 1] = whole - high
            n += 2
    total_ref[...] = jnp.zeros_like(total_ref)

    quarter = lines // 4
    for t in range(tiles):
        used = jnp.sum(jnp.where(inverse[t] > 0.0, 1.0, 0.0)).astype(jnp.int32)
        quarters_ref[t] = jnp.maximum((used + (quarter * LANES - 1)) // (quarter * LANES), 1)

    def line(i, t, count):
        return lane_rows(
            lambda r: jnp.broadcast_to(hold[i, t, r : r + 1, :], (16, LANES)).astype(bf16), count
        )

    def add_tile(t, count):
        lat = t // lon_tiles
        lon = t - lat * lon_tiles
        cols = hat(masks(line(1, t, count), COLS), line(2, t, count), line(3, t, count))
        where = masks(line(0, t, count), ROWS)
        blocks = []
        for k in range(members):
            for term in range(2):
                at = 7 + 4 * k + term
                blocks.append(hat(where, line(at, t, count), line(at + 2, t, count)))
        made = nt_dot(jnp.concatenate(blocks, axis=0), cols)
        at = pl.ds(pl.multiple_of(lat * 96, 8), ROWS)
        for k in range(members):
            both = made[2 * k * ROWS : (2 * k + 1) * ROWS] + made[(2 * k + 1) * ROWS : (2 * k + 2) * ROWS]
            total_ref[k, at, pl.ds(pl.multiple_of(lon * 128, 128), 128)] += both[:, :128]
            total_ref[k, at, pl.ds(pl.multiple_of(lon * 128 + 128, 128), COLS - 128)] += both[:, 128:]

    def one_tile(t, carry):
        for n in range(1, 5):
            pl.when(quarters_ref[t] == n)(functools.partial(add_tile, t, n * quarter))
        return carry

    lax.fori_loop(0, tiles, one_tile, 0)
    total_copy = pltpu.make_async_copy(total_ref, total_out_ref, sems.at[0])
    total_copy.start()

    own = tile_ref[0]
    rows = hat(masks(line(0, own, lines), ROWS), line(4, own, lines), line(5, own, lines)).astype(f32)
    cols = hat(masks(line(1, own, lines), COLS), line(2, own, lines), line(3, own, lines))
    high, low = zip(*(split_two(total_ref[k]) for k in range(members)))
    high, low = jnp.concatenate(high, axis=1), jnp.concatenate(low, axis=1)
    half = dot(jnp.concatenate([left_ref[...], left_low_ref[...]], axis=0), high)
    half = half[:ROWS] + (half[ROWS:] + dot(left_ref[...], low))
    half = jnp.concatenate([half[:, k * width : (k + 1) * width] for k in range(members)], axis=0)
    high, low = split_two(half)
    count = high.shape[0]
    coarse = dot(jnp.concatenate([high, low], axis=0), right_ref[...])
    coarse = coarse[:count] + (coarse[count:] + dot(high, right_low_ref[...]))
    for k in range(members):
        coarse_own_ref[k] = coarse[k * ROWS : (k + 1) * ROWS]
    coarse_copy = pltpu.make_async_copy(coarse_own_ref, coarse_ref, sems.at[1])
    coarse_copy.start()
    made = dot(jnp.concatenate(split_two(coarse), axis=0), cols)
    for k in range(members):
        mine = made[k * ROWS : (k + 1) * ROWS] + made[count + k * ROWS : count + (k + 1) * ROWS]
        value = jnp.sum(mine * rows, axis=0, keepdims=True)
        for r in range(lines):
            image_ref[k, r : r + 1, :] = value[:, r * LANES : (r + 1) * LANES]
    image = jnp.zeros((lines, LANES), f32)
    for k in range(members):
        image = image + image_ref[k] * known_ref[own, (3 + k) * lines : (4 + k) * lines, :]
    image = image * scale
    if not first:
        own_ref[0] = known_ref[own, 2 * lines : 3 * lines, :]
        own_ref[1] = hold[6, own]
    for n in range(part_ref.shape[0]):
        part_ref[n] = image
    coarse_copy.wait()
    total_copy.wait()


def sweep(tile, known, seen, kernels, scale, lon_tiles, members, groups):
    tiles = known.shape[0]
    lines = known.shape[1] // (3 + members)
    first = seen is None
    left, _, right, _ = kernels
    total = (members, left.shape[1], right.shape[0])
    whole = pl.BlockSpec(memory_space=pltpu.VMEM)
    out_shape = [
        jax.ShapeDtypeStruct((groups, lines, LANES), f32),
        pltpu.HBM((members, ROWS, COLS), f32),
        pltpu.HBM(total, f32),
    ]
    far = pl.BlockSpec(memory_space=pltpu.HBM)
    out_specs = [whole, far, far]
    if not first:
        out_shape.append(jax.ShapeDtypeStruct((1, LANES), f32))
        out_shape.append(jax.ShapeDtypeStruct((2, lines, LANES), f32))
        out_specs += [whole, whole]
    arrays = [known] if first else [known, seen]
    arrays += kernels
    return pl.pallas_call(
        functools.partial(sweep_kernel, first, scale, lon_tiles, members),
        out_shape=out_shape,
        in_specs=[pl.BlockSpec(memory_space=pltpu.SMEM)] + [whole] * len(arrays),
        out_specs=out_specs,
        scratch_shapes=[
            pltpu.VMEM((7 + 4 * members, tiles, lines, LANES), f32),
            pltpu.VMEM(total, f32),
            pltpu.VMEM((members, ROWS, COLS), f32),
            pltpu.VMEM((members, lines, LANES), f32),
            pltpu.SMEM((tiles,), jnp.int32),
            pltpu.SemaphoreType.DMA((2,)),
        ],
        compiler_params=pltpu.CompilerParams(vmem_limit_bytes=24 * 1024 * 1024),
        name="sweep_first" if first else "sweep_second",
    )(tile, *arrays)


def refined(count, cells, axis):
    shape = (count, cells) if axis == 0 else (cells, count)
    fine = lax.broadcasted_iota(jnp.int32, shape, axis).astype(f32)
    cell = lax.broadcasted_iota(jnp.int32, shape, 1 - axis).astype(f32)
    return jnp.maximum(1.0 - jnp.abs((fine + 2.5) * 0.25 - cell), 0.0).astype(bf16)


def put_field(perturb_ref, coarse, scale, out_ref, skip):
    members, fine_lat, fine_lon = perturb_ref.shape
    to_rows = refined(fine_lat, ROWS, 0)
    to_cols = refined(fine_lon, COLS, 1)
    field = jnp.zeros((fine_lat, fine_lon), f32)
    for k in range(members):
        high, low = split_two(coarse[k])
        tall = dot(to_rows, high) + dot(to_rows, low)
        high, low = split_two(tall)
        field = field + (dot(high, to_cols) + dot(low, to_cols)) * perturb_ref[k]
    field = scale * field
    across = fine_lon // LANES
    per_part = fine_lat // 8 * across // out_ref.shape[0]
    for n in range(per_part * out_ref.shape[0]):
        i = n // across * 8
        j = n % across * LANES
        at = skip + n % per_part * 8
        out_ref[n // per_part, at : at + 8, :] = field[i : i + 8, j : j + LANES]


def fields_kernel(scale, perturb_ref, length_ref, coarse_1_ref, coarse_2_ref, out_ref):
    put_field(perturb_ref, coarse_1_ref, -scale * length_ref[0, 0], out_ref.at[0], 0)
    put_field(perturb_ref, coarse_2_ref, -scale, out_ref.at[1], 0)


def ends_length(ends_ref):
    return length_of(jnp.sum(ends_ref[:, 1, :]), jnp.sum(ends_ref[:, 0, :]))


def join_kernel(ends_ref, fields_ref, out_ref):
    out_ref[...] = fields_ref[0] + ends_length(ends_ref) * fields_ref[1]


def analysis_kernel(length_ref, ends_ref, total_1_ref, total_2_ref, left_ref, right_ref, out_ref):
    one = length_ref[0, 0]
    two = ends_length(ends_ref)
    for k in range(out_ref.shape[0]):
        total = one * total_1_ref[k] + two * total_2_ref[k]
        half = jnp.dot(left_ref[...], total, precision=highest, preferred_element_type=f32)
        out_ref[k] = -jnp.dot(half, right_ref[...], precision=highest, preferred_element_type=f32)


def small_call(kernel, shapes, flops, name, *arrays):
    whole = pl.BlockSpec(memory_space=pltpu.VMEM)
    made = pl.pallas_call(
        kernel,
        out_shape=[jax.ShapeDtypeStruct(shape, f32) for shape in shapes],
        in_specs=[whole] * len(arrays),
        out_specs=[whole] * len(shapes),
        compiler_params=pltpu.CompilerParams(vmem_limit_bytes=20 * 1024 * 1024),
        cost_estimate=pl.CostEstimate(flops=flops, bytes_accessed=2 * 10**6, transcendentals=0),
        name=name,
    )(*arrays)
    return made if len(shapes) > 1 else made[0]


def per_device(perturb, loc_lat, loc_lon, obs_cell, obs_count, obs_innov, obs_error):
    members, fine_lat, fine_lon = perturb.shape
    coarse_lat, coarse_lon = fine_lat // 4, fine_lon // 4
    groups = lax.axis_size(MEM)
    scale = 1.0 / math.sqrt(members * groups - 1)
    lat, lon = lax.axis_index(LAT), lax.axis_index("lon")
    lat_tiles, lon_tiles = lax.axis_size(LAT), lax.axis_size("lon")
    slots = obs_cell.shape[-1]
    total_lat, total_lon = lat_tiles * coarse_lat, lon_tiles * coarse_lon
    padded_lat, padded_lon = total_lat + 16, total_lon + 128
    tile = (lat * lon_tiles + lon).astype(jnp.int32).reshape(1)

    lines = slots // LANES
    cell = obs_cell.reshape(lines, LANES)
    innovation = obs_innov.reshape(lines, LANES)
    error = obs_error.reshape(lines, LANES)
    message = picked(obs_count.reshape(1), perturb, cell, innovation, error, lat_tiles * lon_tiles)
    known = lax.all_to_all(message, TILES, 0, 0, tiled=True)

    first_lat, first_lon = lat * coarse_lat, lon * coarse_lon
    lat_all = kernel_block(loc_lat, -1, padded_lat, 0, total_lat)
    lon_all = kernel_block(loc_lon, -1, padded_lon, 0, total_lon)
    lat_tile = kernel_block(loc_lat, first_lat - 1, ROWS, 0, total_lat)
    lon_tile = kernel_block(loc_lon, first_lon - 1, COLS, 0, total_lon)
    left = jnp.einsum("ab,cb->ac", lat_tile, lat_all, precision=highest)
    right = jnp.einsum("ab,cb->ac", lon_all, lon_tile, precision=highest)
    left_own = kernel_block(loc_lat, -1, padded_lat, first_lat, coarse_lat).T
    right_own = kernel_block(loc_lon, -1, padded_lon, first_lon, coarse_lon)
    kernels = [*split_two(left), *split_two(right)]

    part, coarse_1, total_1 = sweep(tile, known, None, kernels, scale, lon_tiles, members, groups)
    mine = jnp.sum(lax.all_to_all(part, MEM, 0, 0, tiled=True), axis=0)
    seen = sent_to_all(mine, TILES)
    part, coarse_2, total_2, length_1, own = sweep(
        tile, known, seen, kernels, scale, lon_tiles, members, groups
    )
    mine = jnp.sum(lax.all_to_all(part, MEM, 0, 0, tiled=True), axis=0)
    bent = jnp.sum(jnp.stack([(mine * own[0]) ** 2, mine * own[1]]), axis=1)
    ends = sent_to_all(bent, TILES)

    field_rows = fine_lat * fine_lon // LANES
    along_x, along_z = lax.axis_size(X), lax.axis_size(Z)
    part_rows, piece_rows = field_rows // along_x, field_rows // groups
    part = (along_x, part_rows, LANES)
    fields = small_call(
        functools.partial(fields_kernel, scale),
        ((2, *part),),
        10**9,
        "fields",
        perturb,
        length_1,
        coarse_1,
        coarse_2,
    )
    field = small_call(join_kernel, (part,), 10**6, "join", ends, fields)
    field = jnp.sum(lax.all_to_all(field, X, 0, 0, tiled=True), axis=0).reshape(along_z, piece_rows, LANES)
    field = jnp.sum(lax.all_to_all(field, Z, 0, 0, tiled=True), axis=0)
    everything = sent_to_all(sent_to_all(field, Z).reshape(part_rows, LANES), X)
    whole = pl.BlockSpec(memory_space=pltpu.VMEM)
    analysis = pl.pallas_call(
        analysis_kernel,
        out_shape=jax.ShapeDtypeStruct((members, coarse_lat, coarse_lon), f32),
        in_specs=[whole] * 6,
        out_specs=whole,
        compiler_params=pltpu.CompilerParams(vmem_limit_bytes=24 * 1024 * 1024),
        cost_estimate=pl.CostEstimate(flops=2 * 10**9, bytes_accessed=5 * 10**6, transcendentals=0),
        name="analysis",
    )(length_1, ends, total_1, total_2, left_own, right_own)
    across = fine_lon // LANES
    increment = jnp.transpose(
        everything.reshape(fine_lat // 8, across, 8, LANES), (0, 2, 1, 3)
    ).reshape(fine_lat, fine_lon)
    return analysis, increment


def solution(mesh):
    torus = Mesh(
        mesh.devices.reshape(4, -1, 2, mesh.shape["lat"] // 2, mesh.shape["lon"]),
        ("mem_0", "mem_1", "lat_0", "lat_1", "lon"),
    )
    return jax.shard_map(
        per_device,
        mesh=torus,
        in_specs=(
            P(MEM, LAT, "lon"),
            P(),
            P(),
            P(LAT, "lon", None),
            P(LAT, "lon"),
            P(LAT, "lon", None),
            P(LAT, "lon", None),
        ),
        out_specs=(P(MEM, LAT, "lon"), P(LAT, "lon")),
        check_vma=False,
    )
```

```python
import functools
import math

import jax
import jax.numpy as jnp
from jax import lax
from jax.experimental import pallas as pl
from jax.experimental.pallas import tpu as pltpu
from jax.sharding import Mesh
from jax.sharding import PartitionSpec as P

MEM = ("mem_0", "mem_1")
LAT = ("lat_0", "lat_1")
TILES = ("lat_0", "lat_1", "lon")
X, Z = "mem_0", "mem_1"

tiny_floor = 1e-06
highest = lax.Precision.HIGHEST
f32 = jnp.float32
bf16 = jnp.bfloat16

ROWS = 112
COLS = 144
LANES = 128
TOGETHER = 2


def sent_to_all(x, axis):
    copies = jnp.broadcast_to(x, (lax.axis_size(axis), *x.shape))
    return lax.all_to_all(copies, axis, split_axis=0, concat_axis=0, tiled=True)


def scale_run(scales, first, count):
    padded = jnp.pad(scales, (8, 248), constant_values=1.0)
    return lax.dynamic_slice(padded, (first + 8,), (count,))


def kernel_block(scales, first_row, row_count, first_col, col_count):
    total = scales.shape[0]
    rows = first_row + jnp.arange(row_count, dtype=jnp.int32)
    cols = first_col + jnp.arange(col_count, dtype=jnp.int32)
    row_scale = scale_run(scales, first_row, row_count)
    col_scale = scale_run(scales, first_col, col_count)
    inside = (rows >= 0) & (rows < total)
    weight = jnp.where(inside, (jnp.sqrt(jnp.pi) * row_scale) ** (-0.5), jnp.zeros_like(row_scale))
    offset = (rows[:, None] - cols[None, :]).astype(f32)
    spread = row_scale[:, None] ** 2 + col_scale[None, :] ** 2
    return weight[:, None] * jnp.exp(-offset * offset / spread)


def split_two(x):
    high = x.astype(bf16)
    low = (x - high.astype(f32)).astype(bf16)
    return high, low


def nt_dot(a, b):
    return lax.dot_general(a, b, (((1,), (1,)), ((), ())), preferred_element_type=f32)


def dot(a, b):
    return jnp.dot(a, b, preferred_element_type=f32)


def lane_rows(read, count):
    return jnp.concatenate([read(r) for r in range(count)], axis=1)


def picked_kernel(count_ref, perturb_ref, cell_ref, innov_ref, error_ref, copies_ref, out_ref, sems):
    members, fine_lat, fine_lon = perturb_ref.shape
    lines = cell_ref.shape[0]
    step = 512
    per_step = step // LANES
    slot = lax.broadcasted_iota(jnp.int32, cell_ref.shape, 0) * LANES + lax.broadcasted_iota(
        jnp.int32, cell_ref.shape, 1
    )
    out_ref[:lines] = cell_ref[...].astype(f32)
    out_ref[lines : 2 * lines] = innov_ref[...]
    out_ref[2 * lines : 3 * lines] = jnp.where(slot < count_ref[0], 1.0 / error_ref[...], 0.0)
    blocks = []
    for k in range(members):
        blocks.append(jnp.concatenate(split_two(perturb_ref[k]), axis=1))
    field = jnp.concatenate(blocks, axis=0)
    for start in range(0, lines, per_step):
        cell = lane_rows(lambda r: cell_ref[start + r : start + r + 1, :], per_step)
        row = cell // fine_lon
        col = cell - row * fine_lon
        at_col = lax.broadcasted_iota(jnp.int32, (fine_lon, step), 0) == col
        one = jnp.where(at_col, 1.0, 0.0).astype(bf16)
        values = dot(field, jnp.concatenate([one, one], axis=0))
        at_row = lax.broadcasted_iota(jnp.int32, (fine_lat, step), 0) == row
        for k in range(members):
            mine = values[k * fine_lat : (k + 1) * fine_lat]
            found = jnp.sum(jnp.where(at_row, mine, 0.0), axis=0, keepdims=True)
            for r in range(per_step):
                at = (3 + k) * lines + start + r
                out_ref[at : at + 1, :] = found[:, r * LANES : (r + 1) * LANES]
    sends = [
        pltpu.make_async_copy(out_ref, copies_ref.at[n], sems.at[n]) for n in range(copies_ref.shape[0])
    ]
    for send in sends:
        send.start()
    for send in sends:
        send.wait()


def picked(count, perturb, cell, innovation, error, copies):
    whole = pl.BlockSpec(memory_space=pltpu.VMEM)
    message = ((3 + perturb.shape[0]) * cell.shape[0], LANES)
    return pl.pallas_call(
        picked_kernel,
        out_shape=pltpu.HBM((copies, *message), f32),
        in_specs=[pl.BlockSpec(memory_space=pltpu.SMEM)] + [whole] * 4,
        out_specs=pl.BlockSpec(memory_space=pltpu.HBM),
        scratch_shapes=[pltpu.VMEM(message, f32), pltpu.SemaphoreType.DMA((copies,))],
        compiler_params=pltpu.CompilerParams(vmem_limit_bytes=60 * 1024 * 1024),
        name="picked",
    )(count, perturb, cell, innovation, error)


def weights_of(observed, innovation, inverse):
    residual = (observed - innovation) * inverse
    return residual / jnp.sqrt(1.0 + residual * residual) * inverse


def length_of(grad_total, curvature):
    return grad_total / (grad_total + curvature + tiny_floor)


def masks(below, count):
    cell = lax.broadcasted_iota(jnp.int32, below.shape, 0).astype(f32)
    found = []
    for start in range(0, count, 16):
        at = (cell + start).astype(bf16)
        before = (cell + (start - 1)).astype(bf16)
        found.append((below == at, below == before))
    return found


def hat(where, lower, upper):
    zero = jnp.zeros_like(lower)
    return jnp.concatenate([jnp.where(at, lower, jnp.where(before, upper, zero)) for at, before in where], axis=0)


def sweep_kernel(first, scale, lon_tiles, members, *refs):
    tile_ref, known_ref = refs[:2]
    refs = refs[2:]
    if not first:
        seen_ref, perturb_ref, coarse_1_ref = refs[:3]
        refs = refs[3:]
    left_ref, left_low_ref, right_ref, right_low_ref, part_ref, total_out_ref = refs[:6]
    refs = refs[6:]
    if first:
        coarse_ref = refs[0]
        refs = refs[1:]
    else:
        length_ref, own_ref = refs[:2]
        refs = refs[2:]
    hold, total_ref, coarse_own_ref, image_ref, sems = refs
    tiles = known_ref.shape[0]
    lines = known_ref.shape[1] // (3 + members)
    width = total_ref.shape[2]

    def known(n):
        return known_ref[:, n * lines : (n + 1) * lines, :]

    cell = known(0)
    innovation = known(1)
    inverse = known(2)
    row = jnp.floor(cell * (1.0 / 512.0))
    col = (cell - row * 512.0 + 2.5) * 0.25
    row = (row + 2.5) * 0.25
    row_cell, col_cell = jnp.floor(row), jnp.floor(col)
    row_up, col_up = row - row_cell, col - col_cell
    hold[0], hold[1], hold[2], hold[3] = row_cell, col_cell, 1.0 - col_up, col_up
    hold[4], hold[5] = 1.0 - row_up, row_up
    force = weights_of(0.0, innovation, inverse)
    if not first:
        image = seen_ref[...]
        length = length_of(jnp.sum(force * image), jnp.sum((image * inverse) ** 2))
        force = weights_of(-length * image, innovation, inverse) - length * force
        length_ref[...] = jnp.broadcast_to(length, length_ref.shape)
    hold[6] = force
    n = 7
    for k in range(members):
        q = known(3 + k) * force * scale
        for share in (1.0 - row_up, row_up):
            whole = share * q
            high = whole.astype(bf16).astype(f32)
            hold[n] = high
            hold[n + 1] = whole - high
            n += 2
    total_ref[...] = jnp.zeros_like(total_ref)

    def line(i, t):
        return lane_rows(
            lambda r: jnp.broadcast_to(hold[i, t, r : r + 1, :], (16, LANES)).astype(bf16), lines
        )

    def add_tile(t):
        lat = t // lon_tiles
        lon = t - lat * lon_tiles
        cols = hat(masks(line(1, t), COLS), line(2, t), line(3, t))
        where = masks(line(0, t), ROWS)
        blocks = []
        for k in range(members):
            for term in range(2):
                at = 7 + 4 * k + term
                blocks.append(hat(where, line(at, t), line(at + 2, t)))
        made = nt_dot(jnp.concatenate(blocks, axis=0), cols)
        at = pl.ds(pl.multiple_of(lat * 96, 8), ROWS)
        for k in range(members):
            both = made[2 * k * ROWS : (2 * k + 1) * ROWS] + made[(2 * k + 1) * ROWS : (2 * k + 2) * ROWS]
            total_ref[k, at, pl.ds(pl.multiple_of(lon * 128, 128), 128)] += both[:, :128]
            total_ref[k, at, pl.ds(pl.multiple_of(lon * 128 + 128, 128), COLS - 128)] += both[:, 128:]

    def some_tiles(t, carry):
        for n in range(TOGETHER):
            add_tile(t * TOGETHER + n)
        return carry

    lax.fori_loop(0, tiles // TOGETHER, some_tiles, 0)
    total_copy = pltpu.make_async_copy(total_ref, total_out_ref, sems.at[0])
    total_copy.start()

    own = tile_ref[0]
    rows = hat(masks(line(0, own), ROWS), line(4, own), line(5, own)).astype(f32)
    cols = hat(masks(line(1, own), COLS), line(2, own), line(3, own))
    high, low = zip(*(split_two(total_ref[k]) for k in range(members)))
    high, low = jnp.concatenate(high, axis=1), jnp.concatenate(low, axis=1)
    half = dot(jnp.concatenate([left_ref[...], left_low_ref[...]], axis=0), high)
    half = half[:ROWS] + (half[ROWS:] + dot(left_ref[...], low))
    half = jnp.concatenate([half[:, k * width : (k + 1) * width] for k in range(members)], axis=0)
    high, low = split_two(half)
    count = high.shape[0]
    coarse = dot(jnp.concatenate([high, low], axis=0), right_ref[...])
    coarse = coarse[:count] + (coarse[count:] + dot(high, right_low_ref[...]))
    for k in range(members):
        coarse_own_ref[k] = coarse[k * ROWS : (k + 1) * ROWS]
    if first:
        coarse_copy = pltpu.make_async_copy(coarse_own_ref, coarse_ref, sems.at[1])
        coarse_copy.start()
    made = dot(jnp.concatenate(split_two(coarse), axis=0), cols)
    for k in range(members):
        mine = made[k * ROWS : (k + 1) * ROWS] + made[count + k * ROWS : count + (k + 1) * ROWS]
        value = jnp.sum(mine * rows, axis=0, keepdims=True)
        for r in range(lines):
            image_ref[k, r : r + 1, :] = value[:, r * LANES : (r + 1) * LANES]
    image = jnp.zeros((lines, LANES), f32)
    for k in range(members):
        image = image + image_ref[k] * known_ref[own, (3 + k) * lines : (4 + k) * lines, :]
    image = image * scale
    if not first:
        own_ref[0] = known_ref[own, 2 * lines : 3 * lines, :]
        own_ref[1] = hold[6, own]
    for n in range(part_ref.shape[0]):
        part_ref[n, :lines, :] = image
    if first:
        coarse_copy.wait()
    else:
        put_field(perturb_ref, coarse_1_ref, -scale * length, part_ref, lines)
        put_field(perturb_ref, coarse_own_ref, -scale, part_ref, (part_ref.shape[1] + lines) // 2)
    total_copy.wait()


def sweep(tile, known, later, kernels, scale, lon_tiles, members, part):
    tiles = known.shape[0]
    lines = known.shape[1] // (3 + members)
    first = not later
    left, _, right, _ = kernels
    total = (members, left.shape[1], right.shape[0])
    whole = pl.BlockSpec(memory_space=pltpu.VMEM)
    far = pl.BlockSpec(memory_space=pltpu.HBM)
    out_shape = [jax.ShapeDtypeStruct(part, f32), pltpu.HBM(total, f32)]
    out_specs = [whole, far]
    if first:
        out_shape.append(pltpu.HBM((members, ROWS, COLS), f32))
        out_specs.append(far)
    else:
        out_shape.append(jax.ShapeDtypeStruct((1, LANES), f32))
        out_shape.append(jax.ShapeDtypeStruct((2, lines, LANES), f32))
        out_specs += [whole, whole]
    arrays = [known, *later, *kernels]
    return pl.pallas_call(
        functools.partial(sweep_kernel, first, scale, lon_tiles, members),
        out_shape=out_shape,
        in_specs=[pl.BlockSpec(memory_space=pltpu.SMEM)] + [whole] * len(arrays),
        out_specs=out_specs,
        scratch_shapes=[
            pltpu.VMEM((7 + 4 * members, tiles, lines, LANES), f32),
            pltpu.VMEM(total, f32),
            pltpu.VMEM((members, ROWS, COLS), f32),
            pltpu.VMEM((members, lines, LANES), f32),
            pltpu.SemaphoreType.DMA((2,)),
        ],
        compiler_params=pltpu.CompilerParams(vmem_limit_bytes=28 * 1024 * 1024),
        name="sweep_first" if first else "sweep_second",
    )(tile, *arrays)


def refined(count, cells, axis):
    shape = (count, cells) if axis == 0 else (cells, count)
    fine = lax.broadcasted_iota(jnp.int32, shape, axis).astype(f32)
    cell = lax.broadcasted_iota(jnp.int32, shape, 1 - axis).astype(f32)
    return jnp.maximum(1.0 - jnp.abs((fine + 2.5) * 0.25 - cell), 0.0).astype(bf16)


def put_field(perturb_ref, coarse, scale, out_ref, skip):
    members, fine_lat, fine_lon = perturb_ref.shape
    to_rows = refined(fine_lat, ROWS, 0)
    to_cols = refined(fine_lon, COLS, 1)
    field = jnp.zeros((fine_lat, fine_lon), f32)
    for k in range(members):
        high, low = split_two(coarse[k])
        tall = dot(to_rows, high) + dot(to_rows, low)
        high, low = split_two(tall)
        field = field + (dot(high, to_cols) + dot(low, to_cols)) * perturb_ref[k]
    field = scale * field
    across = fine_lon // LANES
    per_part = fine_lat // 8 * across // out_ref.shape[0]
    for n in range(per_part * out_ref.shape[0]):
        i = n // across * 8
        j = n % across * LANES
        at = skip + n % per_part * 8
        out_ref[n // per_part, at : at + 8, :] = field[i : i + 8, j : j + LANES]


def gather_x_kernel(arrived_ref, out_ref):
    parts, rows, _ = out_ref.shape
    lines = rows - (arrived_ref.shape[1] - rows) // (parts - 1)
    fields = (arrived_ref.shape[1] - lines) // 2
    piece = fields // parts
    image = jnp.sum(arrived_ref[:, :lines, :], axis=0)
    for n in range(parts):
        out_ref[n, :lines, :] = image
        for k in range(2):
            at = lines + k * fields + n * piece
            to = lines + k * piece
            out_ref[n, to : to + piece, :] = jnp.sum(arrived_ref[:, at : at + piece, :], axis=0)


def gather_z_kernel(arrived_ref, own_ref, bent_ref, fields_ref):
    lines = own_ref.shape[1]
    image = jnp.sum(arrived_ref[:, :lines, :], axis=0)
    fields_ref[...] = jnp.sum(arrived_ref[:, lines:, :], axis=0)
    bent = jnp.sum((image * own_ref[0]) ** 2, axis=0, keepdims=True)
    gain = jnp.sum(image * own_ref[1], axis=0, keepdims=True)
    both = jnp.concatenate([bent, gain], axis=0)
    for n in range(bent_ref.shape[0]):
        bent_ref[n] = both


def ends_length(ends_ref):
    return length_of(jnp.sum(ends_ref[:, 1, :]), jnp.sum(ends_ref[:, 0, :]))


def finish_kernel(ends_ref, fields_ref, out_ref):
    rows = fields_ref.shape[0] // 2
    done = fields_ref[:rows] + ends_length(ends_ref) * fields_ref[rows:]
    for n in range(out_ref.shape[0]):
        out_ref[n] = done


def analysis_kernel(length_ref, ends_ref, total_1_ref, total_2_ref, left_ref, right_ref, out_ref):
    one = length_ref[0, 0]
    two = ends_length(ends_ref)
    for k in range(out_ref.shape[0]):
        total = one * total_1_ref[k] + two * total_2_ref[k]
        half = jnp.dot(left_ref[...], total, precision=highest, preferred_element_type=f32)
        out_ref[k] = -jnp.dot(half, right_ref[...], precision=highest, preferred_element_type=f32)


def small_call(kernel, shapes, flops, name, *arrays):
    whole = pl.BlockSpec(memory_space=pltpu.VMEM)
    made = pl.pallas_call(
        kernel,
        out_shape=[jax.ShapeDtypeStruct(shape, f32) for shape in shapes],
        in_specs=[whole] * len(arrays),
        out_specs=[whole] * len(shapes),
        compiler_params=pltpu.CompilerParams(vmem_limit_bytes=20 * 1024 * 1024),
        cost_estimate=pl.CostEstimate(flops=flops, bytes_accessed=2 * 10**6, transcendentals=0),
        name=name,
    )(*arrays)
    return made if len(shapes) > 1 else made[0]


def per_device(perturb, loc_lat, loc_lon, obs_cell, obs_count, obs_innov, obs_error):
    members, fine_lat, fine_lon = perturb.shape
    coarse_lat, coarse_lon = fine_lat // 4, fine_lon // 4
    groups = lax.axis_size(MEM)
    scale = 1.0 / math.sqrt(members * groups - 1)
    lat, lon = lax.axis_index(LAT), lax.axis_index("lon")
    lat_tiles, lon_tiles = lax.axis_size(LAT), lax.axis_size("lon")
    slots = obs_cell.shape[-1]
    total_lat, total_lon = lat_tiles * coarse_lat, lon_tiles * coarse_lon
    padded_lat, padded_lon = total_lat + 16, total_lon + 128
    tile = (lat * lon_tiles + lon).astype(jnp.int32).reshape(1)

    lines = slots // LANES
    cell = obs_cell.reshape(lines, LANES)
    innovation = obs_innov.reshape(lines, LANES)
    error = obs_error.reshape(lines, LANES)
    message = picked(obs_count.reshape(1), perturb, cell, innovation, error, lat_tiles * lon_tiles)
    known = lax.all_to_all(message, TILES, 0, 0, tiled=True)

    first_lat, first_lon = lat * coarse_lat, lon * coarse_lon
    lat_all = kernel_block(loc_lat, -1, padded_lat, 0, total_lat)
    lon_all = kernel_block(loc_lon, -1, padded_lon, 0, total_lon)
    lat_tile = kernel_block(loc_lat, first_lat - 1, ROWS, 0, total_lat)
    lon_tile = kernel_block(loc_lon, first_lon - 1, COLS, 0, total_lon)
    left = jnp.einsum("ab,cb->ac", lat_tile, lat_all, precision=highest)
    right = jnp.einsum("ab,cb->ac", lon_all, lon_tile, precision=highest)
    left_own = kernel_block(loc_lat, -1, padded_lat, first_lat, coarse_lat).T
    right_own = kernel_block(loc_lon, -1, padded_lon, first_lon, coarse_lon)
    kernels = [*split_two(left), *split_two(right)]

    field_rows = fine_lat * fine_lon // LANES
    along_x, along_z = lax.axis_size(X), lax.axis_size(Z)
    part_rows, piece_rows = field_rows // along_x, field_rows // groups
    part, total_1, coarse_1 = sweep(tile, known, (), kernels, scale, lon_tiles, members, (groups, lines, LANES))
    mine = jnp.sum(lax.all_to_all(part, MEM, 0, 0, tiled=True), axis=0)
    seen = sent_to_all(mine, TILES)
    shape = (along_x, lines + 2 * part_rows, LANES)
    part, total_2, length_1, own = sweep(
        tile, known, (seen, perturb, coarse_1), kernels, scale, lon_tiles, members, shape
    )
    part = lax.all_to_all(part, X, 0, 0, tiled=True)
    part = small_call(gather_x_kernel, ((along_z, lines + 2 * piece_rows, LANES),), 10**6, "gather_x", part)
    part = lax.all_to_all(part, Z, 0, 0, tiled=True)
    shapes = ((lat_tiles * lon_tiles, 2, LANES), (2 * piece_rows, LANES))
    bent, fields = small_call(gather_z_kernel, shapes, 10**6, "gather_z", part, own)
    ends = lax.all_to_all(bent, TILES, 0, 0, tiled=True)
    done = small_call(finish_kernel, ((along_z, piece_rows, LANES),), 10**6, "finish", ends, fields)
    done = lax.all_to_all(done, Z, 0, 0, tiled=True).reshape(part_rows, LANES)
    everything = sent_to_all(done, X)
    whole = pl.BlockSpec(memory_space=pltpu.VMEM)
    analysis = pl.pallas_call(
        analysis_kernel,
        out_shape=jax.ShapeDtypeStruct((members, coarse_lat, coarse_lon), f32),
        in_specs=[whole] * 6,
        out_specs=whole,
        compiler_params=pltpu.CompilerParams(vmem_limit_bytes=24 * 1024 * 1024),
        cost_estimate=pl.CostEstimate(flops=2 * 10**9, bytes_accessed=5 * 10**6, transcendentals=0),
        name="analysis",
    )(length_1, ends, total_1, total_2, left_own, right_own)
    across = fine_lon // LANES
    increment = jnp.transpose(
        everything.reshape(fine_lat // 8, across, 8, LANES), (0, 2, 1, 3)
    ).reshape(fine_lat, fine_lon)
    return analysis, increment


def solution(mesh):
    torus = Mesh(
        mesh.devices.reshape(4, -1, 2, mesh.shape["lat"] // 2, mesh.shape["lon"]),
        ("mem_0", "mem_1", "lat_0", "lat_1", "lon"),
    )
    return jax.shard_map(
        per_device,
        mesh=torus,
        in_specs=(
            P(MEM, LAT, "lon"),
            P(),
            P(),
            P(LAT, "lon", None),
            P(LAT, "lon"),
            P(LAT, "lon", None),
            P(LAT, "lon", None),
        ),
        out_specs=(P(MEM, LAT, "lon"), P(LAT, "lon")),
        check_vma=False,
    )
```

```python
import functools
import math

import jax
import jax.numpy as jnp
from jax import lax
from jax.experimental import pallas as pl
from jax.experimental.pallas import tpu as pltpu
from jax.sharding import Mesh
from jax.sharding import PartitionSpec as P

MEM = ("mem_0", "mem_1")
LAT = ("lat_0", "lat_1")
TILES = ("lat_0", "lat_1", "lon")
X, Z = "mem_0", "mem_1"

tiny_floor = 1e-06
highest = lax.Precision.HIGHEST
f32 = jnp.float32
bf16 = jnp.bfloat16

ROWS = 112
COLS = 144
LANES = 128
TOGETHER = 2


def sent_to_all(x, axis):
    copies = jnp.broadcast_to(x, (lax.axis_size(axis), *x.shape))
    return lax.all_to_all(copies, axis, split_axis=0, concat_axis=0, tiled=True)


def scale_run(scales, first, count):
    padded = jnp.pad(scales, (8, 248), constant_values=1.0)
    return lax.dynamic_slice(padded, (first + 8,), (count,))


def kernel_block(scales, first_row, row_count, first_col, col_count):
    total = scales.shape[0]
    rows = first_row + jnp.arange(row_count, dtype=jnp.int32)
    cols = first_col + jnp.arange(col_count, dtype=jnp.int32)
    row_scale = scale_run(scales, first_row, row_count)
    col_scale = scale_run(scales, first_col, col_count)
    inside = (rows >= 0) & (rows < total)
    weight = jnp.where(inside, (jnp.sqrt(jnp.pi) * row_scale) ** (-0.5), jnp.zeros_like(row_scale))
    offset = (rows[:, None] - cols[None, :]).astype(f32)
    spread = row_scale[:, None] ** 2 + col_scale[None, :] ** 2
    return weight[:, None] * jnp.exp(-offset * offset / spread)


def split_two(x):
    high = x.astype(bf16)
    low = (x - high.astype(f32)).astype(bf16)
    return high, low


def nt_dot(a, b):
    return lax.dot_general(a, b, (((1,), (1,)), ((), ())), preferred_element_type=f32)


def dot(a, b):
    return jnp.dot(a, b, preferred_element_type=f32)


def lane_rows(read, count):
    return jnp.concatenate([read(r) for r in range(count)], axis=1)


def picked_kernel(count_ref, perturb_ref, cell_ref, innov_ref, error_ref, copies_ref, out_ref, sems):
    members, fine_lat, fine_lon = perturb_ref.shape
    lines = cell_ref.shape[0]
    step = 512
    per_step = step // LANES
    slot = lax.broadcasted_iota(jnp.int32, cell_ref.shape, 0) * LANES + lax.broadcasted_iota(
        jnp.int32, cell_ref.shape, 1
    )
    out_ref[:lines] = cell_ref[...].astype(f32)
    out_ref[lines : 2 * lines] = innov_ref[...]
    out_ref[2 * lines : 3 * lines] = jnp.where(slot < count_ref[0], 1.0 / error_ref[...], 0.0)
    blocks = []
    for k in range(members):
        blocks.append(jnp.concatenate(split_two(perturb_ref[k]), axis=1))
    field = jnp.concatenate(blocks, axis=0)
    for start in range(0, lines, per_step):
        cell = lane_rows(lambda r: cell_ref[start + r : start + r + 1, :], per_step)
        row = cell // fine_lon
        col = cell - row * fine_lon
        at_col = lax.broadcasted_iota(jnp.int32, (fine_lon, step), 0) == col
        one = jnp.where(at_col, 1.0, 0.0).astype(bf16)
        values = dot(field, jnp.concatenate([one, one], axis=0))
        at_row = lax.broadcasted_iota(jnp.int32, (fine_lat, step), 0) == row
        for k in range(members):
            mine = values[k * fine_lat : (k + 1) * fine_lat]
            found = jnp.sum(jnp.where(at_row, mine, 0.0), axis=0, keepdims=True)
            for r in range(per_step):
                at = (3 + k) * lines + start + r
                out_ref[at : at + 1, :] = found[:, r * LANES : (r + 1) * LANES]
    sends = [
        pltpu.make_async_copy(out_ref, copies_ref.at[n], sems.at[n]) for n in range(copies_ref.shape[0])
    ]
    for send in sends:
        send.start()
    for send in sends:
        send.wait()


def picked(count, perturb, cell, innovation, error, copies):
    whole = pl.BlockSpec(memory_space=pltpu.VMEM)
    message = ((3 + perturb.shape[0]) * cell.shape[0], LANES)
    return pl.pallas_call(
        picked_kernel,
        out_shape=pltpu.HBM((copies, *message), f32),
        in_specs=[pl.BlockSpec(memory_space=pltpu.SMEM)] + [whole] * 4,
        out_specs=pl.BlockSpec(memory_space=pltpu.HBM),
        scratch_shapes=[pltpu.VMEM(message, f32), pltpu.SemaphoreType.DMA((copies,))],
        compiler_params=pltpu.CompilerParams(vmem_limit_bytes=60 * 1024 * 1024),
        name="picked",
    )(count, perturb, cell, innovation, error)


def weights_of(observed, innovation, inverse):
    residual = (observed - innovation) * inverse
    return residual / jnp.sqrt(1.0 + residual * residual) * inverse


def length_of(grad_total, curvature):
    return grad_total / (grad_total + curvature + tiny_floor)


def masks(below, count):
    cell = lax.broadcasted_iota(jnp.int32, below.shape, 0).astype(f32)
    found = []
    for start in range(0, count, 16):
        at = (cell + start).astype(bf16)
        before = (cell + (start - 1)).astype(bf16)
        found.append((below == at, below == before))
    return found


def hat(where, lower, upper):
    zero = jnp.zeros_like(lower)
    return jnp.concatenate([jnp.where(at, lower, jnp.where(before, upper, zero)) for at, before in where], axis=0)


def sweep_kernel(first, scale, lon_tiles, members, *refs):
    tile_ref, known_ref = refs[:2]
    refs = refs[2:]
    if not first:
        seen_ref, perturb_ref, coarse_1_ref = refs[:3]
        refs = refs[3:]
    left_ref, left_low_ref, right_ref, right_low_ref, part_ref, total_out_ref = refs[:6]
    refs = refs[6:]
    if first:
        coarse_ref = refs[0]
        refs = refs[1:]
    else:
        length_ref, own_ref = refs[:2]
        refs = refs[2:]
    hold, total_ref, coarse_own_ref, image_ref, sems = refs
    tiles = known_ref.shape[0]
    lines = known_ref.shape[1] // (3 + members)
    width = total_ref.shape[2]

    def known(n):
        return known_ref[:, n * lines : (n + 1) * lines, :]

    cell = known(0)
    innovation = known(1)
    inverse = known(2)
    row = jnp.floor(cell * (1.0 / 512.0))
    col = (cell - row * 512.0 + 2.5) * 0.25
    row = (row + 2.5) * 0.25
    row_cell, col_cell = jnp.floor(row), jnp.floor(col)
    row_up, col_up = row - row_cell, col - col_cell
    hold[0], hold[1], hold[2], hold[3] = row_cell, col_cell, 1.0 - col_up, col_up
    hold[4], hold[5] = 1.0 - row_up, row_up
    force = weights_of(0.0, innovation, inverse)
    if not first:
        image = seen_ref[...]
        length = length_of(jnp.sum(force * image), jnp.sum((image * inverse) ** 2))
        force = weights_of(-length * image, innovation, inverse) - length * force
        length_ref[...] = jnp.broadcast_to(length, length_ref.shape)
    hold[6] = force
    n = 7
    for k in range(members):
        q = known(3 + k) * force * scale
        for share in (1.0 - row_up, row_up):
            whole = share * q
            high = whole.astype(bf16).astype(f32)
            hold[n] = high
            hold[n + 1] = whole - high
            n += 2
    total_ref[...] = jnp.zeros_like(total_ref)

    def line(i, t):
        return lane_rows(
            lambda r: jnp.broadcast_to(hold[i, t, r : r + 1, :], (16, LANES)).astype(bf16), lines
        )

    def add_tile(t):
        lat = t // lon_tiles
        lon = t - lat * lon_tiles
        cols = hat(masks(line(1, t), COLS), line(2, t), line(3, t))
        where = masks(line(0, t), ROWS)
        blocks = []
        for k in range(members):
            for term in range(2):
                at = 7 + 4 * k + term
                blocks.append(hat(where, line(at, t), line(at + 2, t)))
        made = nt_dot(jnp.concatenate(blocks, axis=0), cols)
        at = pl.ds(pl.multiple_of(lat * 96, 8), ROWS)
        for k in range(members):
            both = made[2 * k * ROWS : (2 * k + 1) * ROWS] + made[(2 * k + 1) * ROWS : (2 * k + 2) * ROWS]
            total_ref[k, at, pl.ds(pl.multiple_of(lon * 128, 128), 128)] += both[:, :128]
            total_ref[k, at, pl.ds(pl.multiple_of(lon * 128 + 128, 128), COLS - 128)] += both[:, 128:]

    def some_tiles(t, carry):
        for n in range(TOGETHER):
            add_tile(t * TOGETHER + n)
        return carry

    lax.fori_loop(0, tiles // TOGETHER, some_tiles, 0)
    total_copy = pltpu.make_async_copy(total_ref, total_out_ref, sems.at[0])
    total_copy.start()

    own = tile_ref[0]
    rows = hat(masks(line(0, own), ROWS), line(4, own), line(5, own)).astype(f32)
    cols = hat(masks(line(1, own), COLS), line(2, own), line(3, own))
    high, low = zip(*(split_two(total_ref[k]) for k in range(members)))
    high, low = jnp.concatenate(high, axis=1), jnp.concatenate(low, axis=1)
    half = dot(jnp.concatenate([left_ref[...], left_low_ref[...]], axis=0), high)
    half = half[:ROWS] + (half[ROWS:] + dot(left_ref[...], low))
    half = jnp.concatenate([half[:, k * width : (k + 1) * width] for k in range(members)], axis=0)
    high, low = split_two(half)
    count = high.shape[0]
    coarse = dot(jnp.concatenate([high, low], axis=0), right_ref[...])
    coarse = coarse[:count] + (coarse[count:] + dot(high, right_low_ref[...]))
    for k in range(members):
        coarse_own_ref[k] = coarse[k * ROWS : (k + 1) * ROWS]
    if first:
        coarse_copy = pltpu.make_async_copy(coarse_own_ref, coarse_ref, sems.at[1])
        coarse_copy.start()
    made = dot(jnp.concatenate(split_two(coarse), axis=0), cols)
    for k in range(members):
        mine = made[k * ROWS : (k + 1) * ROWS] + made[count + k * ROWS : count + (k + 1) * ROWS]
        value = jnp.sum(mine * rows, axis=0, keepdims=True)
        for r in range(lines):
            image_ref[k, r : r + 1, :] = value[:, r * LANES : (r + 1) * LANES]
    image = jnp.zeros((lines, LANES), f32)
    for k in range(members):
        image = image + image_ref[k] * known_ref[own, (3 + k) * lines : (4 + k) * lines, :]
    image = image * scale
    if not first:
        own_ref[0] = known_ref[own, 2 * lines : 3 * lines, :]
        own_ref[1] = hold[6, own]
    for n in range(part_ref.shape[0]):
        part_ref[n, :lines, :] = image
    if first:
        coarse_copy.wait()
    else:
        put_field(perturb_ref, coarse_1_ref, -scale * length, part_ref, lines)
        put_field(perturb_ref, coarse_own_ref, -scale, part_ref, (part_ref.shape[1] + lines) // 2)
    total_copy.wait()


def sweep(tile, known, later, kernels, scale, lon_tiles, members, part):
    tiles = known.shape[0]
    lines = known.shape[1] // (3 + members)
    first = not later
    left, _, right, _ = kernels
    total = (members, left.shape[1], right.shape[0])
    whole = pl.BlockSpec(memory_space=pltpu.VMEM)
    far = pl.BlockSpec(memory_space=pltpu.HBM)
    out_shape = [jax.ShapeDtypeStruct(part, f32), pltpu.HBM(total, f32)]
    out_specs = [whole, far]
    if first:
        out_shape.append(pltpu.HBM((members, ROWS, COLS), f32))
        out_specs.append(far)
    else:
        out_shape.append(jax.ShapeDtypeStruct((1, LANES), f32))
        out_shape.append(jax.ShapeDtypeStruct((2, lines, LANES), f32))
        out_specs += [whole, whole]
    arrays = [known, *later, *kernels]
    return pl.pallas_call(
        functools.partial(sweep_kernel, first, scale, lon_tiles, members),
        out_shape=out_shape,
        in_specs=[pl.BlockSpec(memory_space=pltpu.SMEM)] + [whole] * len(arrays),
        out_specs=out_specs,
        scratch_shapes=[
            pltpu.VMEM((7 + 4 * members, tiles, lines, LANES), f32),
            pltpu.VMEM(total, f32),
            pltpu.VMEM((members, ROWS, COLS), f32),
            pltpu.VMEM((members, lines, LANES), f32),
            pltpu.SemaphoreType.DMA((2,)),
        ],
        compiler_params=pltpu.CompilerParams(vmem_limit_bytes=28 * 1024 * 1024),
        name="sweep_first" if first else "sweep_second",
    )(tile, *arrays)


def refined(count, cells, axis):
    shape = (count, cells) if axis == 0 else (cells, count)
    fine = lax.broadcasted_iota(jnp.int32, shape, axis).astype(f32)
    cell = lax.broadcasted_iota(jnp.int32, shape, 1 - axis).astype(f32)
    return jnp.maximum(1.0 - jnp.abs((fine + 2.5) * 0.25 - cell), 0.0).astype(bf16)


def put_field(perturb_ref, coarse, scale, out_ref, skip):
    members, fine_lat, fine_lon = perturb_ref.shape
    to_rows = refined(fine_lat, ROWS, 0)
    to_cols = refined(fine_lon, COLS, 1)
    field = jnp.zeros((fine_lat, fine_lon), f32)
    for k in range(members):
        high, low = split_two(coarse[k])
        tall = dot(to_rows, high) + dot(to_rows, low)
        high, low = split_two(tall)
        field = field + (dot(high, to_cols) + dot(low, to_cols)) * perturb_ref[k]
    field = scale * field
    across = fine_lon // LANES
    per_part = fine_lat // 8 * across // out_ref.shape[0]
    for n in range(per_part * out_ref.shape[0]):
        i = n // across * 8
        j = n % across * LANES
        at = skip + n % per_part * 8
        out_ref[n // per_part, at : at + 8, :] = field[i : i + 8, j : j + LANES]


def gather_x_kernel(arrived_ref, out_ref):
    parts, rows, _ = out_ref.shape
    lines = rows - (arrived_ref.shape[1] - rows) // (parts - 1)
    fields = (arrived_ref.shape[1] - lines) // 2
    piece = fields // parts
    image = jnp.sum(arrived_ref[:, :lines, :], axis=0)
    for n in range(parts):
        out_ref[n, :lines, :] = image
        for k in range(2):
            at = lines + k * fields + n * piece
            to = lines + k * piece
            out_ref[n, to : to + piece, :] = jnp.sum(arrived_ref[:, at : at + piece, :], axis=0)


def gather_z_kernel(arrived_ref, own_ref, bent_ref, fields_ref):
    lines = own_ref.shape[1]
    image = jnp.sum(arrived_ref[:, :lines, :], axis=0)
    fields_ref[...] = jnp.sum(arrived_ref[:, lines:, :], axis=0)
    bent = jnp.sum((image * own_ref[0]) ** 2, axis=0, keepdims=True)
    gain = jnp.sum(image * own_ref[1], axis=0, keepdims=True)
    both = jnp.concatenate([bent, gain], axis=0)
    for n in range(bent_ref.shape[0]):
        bent_ref[n] = both


def ends_length(ends_ref):
    return length_of(jnp.sum(ends_ref[:, 1, :]), jnp.sum(ends_ref[:, 0, :]))


def finish_kernel(ends_ref, fields_ref, out_ref):
    rows = fields_ref.shape[0] // 2
    done = fields_ref[:rows] + ends_length(ends_ref) * fields_ref[rows:]
    for n in range(out_ref.shape[0]):
        out_ref[n] = done


def analysis_kernel(length_ref, ends_ref, total_1_ref, total_2_ref, left_ref, right_ref, out_ref):
    one = length_ref[0, 0]
    two = ends_length(ends_ref)
    for k in range(out_ref.shape[0]):
        total = one * total_1_ref[k] + two * total_2_ref[k]
        half = jnp.dot(left_ref[...], total, precision=highest, preferred_element_type=f32)
        out_ref[k] = -jnp.dot(half, right_ref[...], precision=highest, preferred_element_type=f32)


def small_call(kernel, shapes, flops, name, *arrays):
    whole = pl.BlockSpec(memory_space=pltpu.VMEM)
    made = pl.pallas_call(
        kernel,
        out_shape=[jax.ShapeDtypeStruct(shape, f32) for shape in shapes],
        in_specs=[whole] * len(arrays),
        out_specs=[whole] * len(shapes),
        compiler_params=pltpu.CompilerParams(vmem_limit_bytes=20 * 1024 * 1024),
        cost_estimate=pl.CostEstimate(flops=flops, bytes_accessed=2 * 10**6, transcendentals=0),
        name=name,
    )(*arrays)
    return made if len(shapes) > 1 else made[0]


def per_device(perturb, loc_lat, loc_lon, obs_cell, obs_count, obs_innov, obs_error):
    members, fine_lat, fine_lon = perturb.shape
    coarse_lat, coarse_lon = fine_lat // 4, fine_lon // 4
    groups = lax.axis_size(MEM)
    scale = 1.0 / math.sqrt(members * groups - 1)
    lat, lon = lax.axis_index(LAT), lax.axis_index("lon")
    lat_tiles, lon_tiles = lax.axis_size(LAT), lax.axis_size("lon")
    slots = obs_cell.shape[-1]
    total_lat, total_lon = lat_tiles * coarse_lat, lon_tiles * coarse_lon
    padded_lat, padded_lon = total_lat + 16, total_lon + 128
    tile = (lat * lon_tiles + lon).astype(jnp.int32).reshape(1)

    lines = slots // LANES
    cell = obs_cell.reshape(lines, LANES)
    innovation = obs_innov.reshape(lines, LANES)
    error = obs_error.reshape(lines, LANES)
    message = picked(obs_count.reshape(1), perturb, cell, innovation, error, lat_tiles * lon_tiles)
    known = lax.all_to_all(message, TILES, 0, 0, tiled=True)

    first_lat, first_lon = lat * coarse_lat, lon * coarse_lon
    lat_all = kernel_block(loc_lat, -1, padded_lat, 0, total_lat)
    lon_all = kernel_block(loc_lon, -1, padded_lon, 0, total_lon)
    lat_tile = kernel_block(loc_lat, first_lat - 1, ROWS, 0, total_lat)
    lon_tile = kernel_block(loc_lon, first_lon - 1, COLS, 0, total_lon)
    left = jnp.einsum("ab,cb->ac", lat_tile, lat_all, precision=highest)
    right = jnp.einsum("ab,cb->ac", lon_all, lon_tile, precision=highest)
    left_own = kernel_block(loc_lat, -1, padded_lat, first_lat, coarse_lat).T
    right_own = kernel_block(loc_lon, -1, padded_lon, first_lon, coarse_lon)
    kernels = [*split_two(left), *split_two(right)]

    field_rows = fine_lat * fine_lon // LANES
    along_x, along_z = lax.axis_size(X), lax.axis_size(Z)
    part_rows, piece_rows = field_rows // along_x, field_rows // groups
    part, total_1, coarse_1 = sweep(tile, known, (), kernels, scale, lon_tiles, members, (groups, lines, LANES))
    mine = jnp.sum(lax.all_to_all(part, MEM, 0, 0, tiled=True), axis=0)
    seen = sent_to_all(mine, TILES)
    shape = (along_x, lines + 2 * part_rows, LANES)
    part, total_2, length_1, own = sweep(
        tile, known, (seen, perturb, coarse_1), kernels, scale, lon_tiles, members, shape
    )
    part = lax.all_to_all(part, X, 0, 0, tiled=True)
    part = small_call(gather_x_kernel, ((along_z, lines + 2 * piece_rows, LANES),), 10**6, "gather_x", part)
    part = lax.all_to_all(part, Z, 0, 0, tiled=True)
    shapes = ((lat_tiles * lon_tiles, 2, LANES), (2 * piece_rows, LANES))
    bent, fields = small_call(gather_z_kernel, shapes, 10**6, "gather_z", part, own)
    ends = lax.all_to_all(bent, TILES, 0, 0, tiled=True)
    done = small_call(finish_kernel, ((along_z, piece_rows, LANES),), 10**6, "finish", ends, fields)
    done = lax.all_to_all(done, Z, 0, 0, tiled=True).reshape(part_rows, LANES)
    whole = pl.BlockSpec(memory_space=pltpu.VMEM)
    analysis = pl.pallas_call(
        analysis_kernel,
        out_shape=jax.ShapeDtypeStruct((members, coarse_lat, coarse_lon), f32),
        in_specs=[whole] * 6,
        out_specs=whole,
        compiler_params=pltpu.CompilerParams(vmem_limit_bytes=24 * 1024 * 1024),
        cost_estimate=pl.CostEstimate(flops=2 * 10**9, bytes_accessed=5 * 10**6, transcendentals=0),
        name="analysis",
    )(length_1, ends, total_1, total_2, left_own, right_own)
    done, analysis = lax.optimization_barrier((done, analysis))
    everything = sent_to_all(done, X)
    across = fine_lon // LANES
    increment = jnp.transpose(
        everything.reshape(fine_lat // 8, across, 8, LANES), (0, 2, 1, 3)
    ).reshape(fine_lat, fine_lon)
    return analysis, increment


def solution(mesh):
    torus = Mesh(
        mesh.devices.reshape(4, -1, 2, mesh.shape["lat"] // 2, mesh.shape["lon"]),
        ("mem_0", "mem_1", "lat_0", "lat_1", "lon"),
    )
    return jax.shard_map(
        per_device,
        mesh=torus,
        in_specs=(
            P(MEM, LAT, "lon"),
            P(),
            P(),
            P(LAT, "lon", None),
            P(LAT, "lon"),
            P(LAT, "lon", None),
            P(LAT, "lon", None),
        ),
        out_specs=(P(MEM, LAT, "lon"), P(LAT, "lon")),
        check_vma=False,
    )
```

```python
import functools
import math

import jax
import jax.numpy as jnp
from jax import lax
from jax.experimental import pallas as pl
from jax.experimental.pallas import tpu as pltpu
from jax.sharding import Mesh
from jax.sharding import PartitionSpec as P

MEM = ("mem_0", "mem_1")
LAT = ("lat_0", "lat_1")
TILES = ("lat_0", "lat_1", "lon")
X, Z = "mem_0", "mem_1"

tiny_floor = 1e-06
highest = lax.Precision.HIGHEST
f32 = jnp.float32
bf16 = jnp.bfloat16

ROWS = 112
COLS = 144
LANES = 128
TOGETHER = 2


def sent_to_all(x, axis):
    copies = jnp.broadcast_to(x, (lax.axis_size(axis), *x.shape))
    return lax.all_to_all(copies, axis, split_axis=0, concat_axis=0, tiled=True)


def scale_run(scales, first, count):
    padded = jnp.pad(scales, (8, 248), constant_values=1.0)
    return lax.dynamic_slice(padded, (first + 8,), (count,))


def kernel_block(scales, first_row, row_count, first_col, col_count):
    total = scales.shape[0]
    rows = first_row + jnp.arange(row_count, dtype=jnp.int32)
    cols = first_col + jnp.arange(col_count, dtype=jnp.int32)
    row_scale = scale_run(scales, first_row, row_count)
    col_scale = scale_run(scales, first_col, col_count)
    inside = (rows >= 0) & (rows < total)
    weight = jnp.where(inside, (jnp.sqrt(jnp.pi) * row_scale) ** (-0.5), jnp.zeros_like(row_scale))
    offset = (rows[:, None] - cols[None, :]).astype(f32)
    spread = row_scale[:, None] ** 2 + col_scale[None, :] ** 2
    return weight[:, None] * jnp.exp(-offset * offset / spread)


def split_two(x):
    high = x.astype(bf16)
    low = (x - high.astype(f32)).astype(bf16)
    return high, low


def nt_dot(a, b):
    return lax.dot_general(a, b, (((1,), (1,)), ((), ())), preferred_element_type=f32)


def dot(a, b):
    return jnp.dot(a, b, preferred_element_type=f32)


def lane_rows(read, count):
    return jnp.concatenate([read(r) for r in range(count)], axis=1)


def picked_kernel(count_ref, perturb_ref, cell_ref, innov_ref, error_ref, copies_ref, out_ref, sems):
    members, fine_lat, fine_lon = perturb_ref.shape
    lines = cell_ref.shape[0]
    step = 512
    per_step = step // LANES
    slot = lax.broadcasted_iota(jnp.int32, cell_ref.shape, 0) * LANES + lax.broadcasted_iota(
        jnp.int32, cell_ref.shape, 1
    )
    out_ref[:lines] = cell_ref[...].astype(f32)
    out_ref[lines : 2 * lines] = innov_ref[...]
    out_ref[2 * lines : 3 * lines] = jnp.where(slot < count_ref[0], 1.0 / error_ref[...], 0.0)
    blocks = []
    for k in range(members):
        blocks.extend(split_two(perturb_ref[k]))
    field = jnp.concatenate(blocks, axis=0)
    for start in range(0, lines, per_step):
        cell = lane_rows(lambda r: cell_ref[start + r : start + r + 1, :], per_step)
        row = cell // fine_lon
        col = cell - row * fine_lon
        at_col = lax.broadcasted_iota(jnp.int32, (fine_lon, step), 0) == col
        one = jnp.where(at_col, 1.0, 0.0).astype(bf16)
        values = dot(field, one)
        at_row = lax.broadcasted_iota(jnp.int32, (fine_lat, step), 0) == row
        for k in range(members):
            at = 2 * k * fine_lat
            mine = values[at : at + fine_lat] + values[at + fine_lat : at + 2 * fine_lat]
            found = jnp.sum(jnp.where(at_row, mine, 0.0), axis=0, keepdims=True)
            for r in range(per_step):
                at = (3 + k) * lines + start + r
                out_ref[at : at + 1, :] = found[:, r * LANES : (r + 1) * LANES]
    sends = [
        pltpu.make_async_copy(out_ref, copies_ref.at[n], sems.at[n]) for n in range(copies_ref.shape[0])
    ]
    for send in sends:
        send.start()
    for send in sends:
        send.wait()


def picked(count, perturb, cell, innovation, error, copies):
    whole = pl.BlockSpec(memory_space=pltpu.VMEM)
    message = ((3 + perturb.shape[0]) * cell.shape[0], LANES)
    return pl.pallas_call(
        picked_kernel,
        out_shape=pltpu.HBM((copies, *message), f32),
        in_specs=[pl.BlockSpec(memory_space=pltpu.SMEM)] + [whole] * 4,
        out_specs=pl.BlockSpec(memory_space=pltpu.HBM),
        scratch_shapes=[pltpu.VMEM(message, f32), pltpu.SemaphoreType.DMA((copies,))],
        compiler_params=pltpu.CompilerParams(vmem_limit_bytes=60 * 1024 * 1024),
        name="picked",
    )(count, perturb, cell, innovation, error)


def weights_of(observed, innovation, inverse):
    residual = (observed - innovation) * inverse
    return residual / jnp.sqrt(1.0 + residual * residual) * inverse


def length_of(grad_total, curvature):
    return grad_total / (grad_total + curvature + tiny_floor)


def masks(below, count):
    cell = lax.broadcasted_iota(jnp.int32, below.shape, 0).astype(f32)
    found = []
    for start in range(0, count, 16):
        at = (cell + start).astype(bf16)
        before = (cell + (start - 1)).astype(bf16)
        found.append((below == at, below == before))
    return found


def hat(where, lower, upper):
    zero = jnp.zeros_like(lower)
    return jnp.concatenate([jnp.where(at, lower, jnp.where(before, upper, zero)) for at, before in where], axis=0)


def sweep_kernel(first, scale, lon_tiles, members, *refs):
    tile_ref, known_ref = refs[:2]
    refs = refs[2:]
    if not first:
        seen_ref = refs[0]
        refs = refs[1:]
    left_ref, left_low_ref, right_ref, right_low_ref, part_ref, coarse_ref, total_out_ref = refs[:7]
    refs = refs[7:]
    if not first:
        length_ref, own_ref = refs[:2]
        refs = refs[2:]
    hold, total_ref, coarse_own_ref, image_ref, sems = refs
    tiles = known_ref.shape[0]
    lines = known_ref.shape[1] // (3 + members)
    width = total_ref.shape[2]

    def known(n):
        return known_ref[:, n * lines : (n + 1) * lines, :]

    cell = known(0)
    innovation = known(1)
    inverse = known(2)
    row = jnp.floor(cell * (1.0 / 512.0))
    col = (cell - row * 512.0 + 2.5) * 0.25
    row = (row + 2.5) * 0.25
    row_cell, col_cell = jnp.floor(row), jnp.floor(col)
    row_up, col_up = row - row_cell, col - col_cell
    hold[0], hold[1], hold[2], hold[3] = row_cell, col_cell, 1.0 - col_up, col_up
    hold[4], hold[5] = 1.0 - row_up, row_up
    force = weights_of(0.0, innovation, inverse)
    if not first:
        image = seen_ref[...]
        length = length_of(jnp.sum(force * image), jnp.sum((image * inverse) ** 2))
        force = weights_of(-length * image, innovation, inverse) - length * force
        length_ref[...] = jnp.broadcast_to(length, length_ref.shape)
    hold[6] = force
    n = 7
    for k in range(members):
        q = known(3 + k) * force * scale
        for share in (1.0 - row_up, row_up):
            whole = share * q
            high = whole.astype(bf16).astype(f32)
            hold[n] = high
            hold[n + 1] = whole - high
            n += 2
    total_ref[...] = jnp.zeros_like(total_ref)

    def line(i, t):
        return lane_rows(
            lambda r: jnp.broadcast_to(hold[i, t, r : r + 1, :], (16, LANES)).astype(bf16), lines
        )

    def add_tile(t):
        lat = t // lon_tiles
        lon = t - lat * lon_tiles
        cols = hat(masks(line(1, t), COLS), line(2, t), line(3, t))
        where = masks(line(0, t), ROWS)
        blocks = []
        for k in range(members):
            for term in range(2):
                at = 7 + 4 * k + term
                blocks.append(hat(where, line(at, t), line(at + 2, t)))
        made = nt_dot(jnp.concatenate(blocks, axis=0), cols)
        at = pl.ds(pl.multiple_of(lat * 96, 8), ROWS)
        for k in range(members):
            both = made[2 * k * ROWS : (2 * k + 1) * ROWS] + made[(2 * k + 1) * ROWS : (2 * k + 2) * ROWS]
            total_ref[k, at, pl.ds(pl.multiple_of(lon * 128, 128), 128)] += both[:, :128]
            total_ref[k, at, pl.ds(pl.multiple_of(lon * 128 + 128, 128), COLS - 128)] += both[:, 128:]

    def some_tiles(t, carry):
        for n in range(TOGETHER):
            add_tile(t * TOGETHER + n)
        return carry

    lax.fori_loop(0, tiles // TOGETHER, some_tiles, 0)
    total_copy = pltpu.make_async_copy(total_ref, total_out_ref, sems.at[0])
    total_copy.start()

    own = tile_ref[0]
    rows = hat(masks(line(0, own), ROWS), line(4, own), line(5, own)).astype(f32)
    cols = hat(masks(line(1, own), COLS), line(2, own), line(3, own))
    high, low = zip(*(split_two(total_ref[k]) for k in range(members)))
    high, low = jnp.concatenate(high, axis=1), jnp.concatenate(low, axis=1)
    half = dot(jnp.concatenate([left_ref[...], left_low_ref[...]], axis=0), high)
    half = half[:ROWS] + (half[ROWS:] + dot(left_ref[...], low))
    half = jnp.concatenate([half[:, k * width : (k + 1) * width] for k in range(members)], axis=0)
    high, low = split_two(half)
    count = high.shape[0]
    coarse = dot(jnp.concatenate([high, low], axis=0), right_ref[...])
    coarse = coarse[:count] + (coarse[count:] + dot(high, right_low_ref[...]))
    for k in range(members):
        coarse_own_ref[k] = coarse[k * ROWS : (k + 1) * ROWS]
    coarse_copy = pltpu.make_async_copy(coarse_own_ref, coarse_ref, sems.at[1])
    coarse_copy.start()
    made = dot(jnp.concatenate(split_two(coarse), axis=0), cols)
    for k in range(members):
        mine = made[k * ROWS : (k + 1) * ROWS] + made[count + k * ROWS : count + (k + 1) * ROWS]
        value = jnp.sum(mine * rows, axis=0, keepdims=True)
        for r in range(lines):
            image_ref[k, r : r + 1, :] = value[:, r * LANES : (r + 1) * LANES]
    image = jnp.zeros((lines, LANES), f32)
    for k in range(members):
        image = image + image_ref[k] * known_ref[own, (3 + k) * lines : (4 + k) * lines, :]
    image = image * scale
    if not first:
        own_ref[0] = known_ref[own, 2 * lines : 3 * lines, :]
        own_ref[1] = hold[6, own]
    for n in range(part_ref.shape[0]):
        part_ref[n] = image
    coarse_copy.wait()
    total_copy.wait()


def sweep(tile, known, seen, kernels, scale, lon_tiles, members, groups):
    tiles = known.shape[0]
    lines = known.shape[1] // (3 + members)
    first = seen is None
    left, _, right, _ = kernels
    total = (members, left.shape[1], right.shape[0])
    whole = pl.BlockSpec(memory_space=pltpu.VMEM)
    out_shape = [
        jax.ShapeDtypeStruct((groups, lines, LANES), f32),
        pltpu.HBM((members, ROWS, COLS), f32),
        pltpu.HBM(total, f32),
    ]
    far = pl.BlockSpec(memory_space=pltpu.HBM)
    out_specs = [whole, far, far]
    if not first:
        out_shape.append(jax.ShapeDtypeStruct((1, LANES), f32))
        out_shape.append(jax.ShapeDtypeStruct((2, lines, LANES), f32))
        out_specs += [whole, whole]
    arrays = [known] if first else [known, seen]
    arrays += kernels
    return pl.pallas_call(
        functools.partial(sweep_kernel, first, scale, lon_tiles, members),
        out_shape=out_shape,
        in_specs=[pl.BlockSpec(memory_space=pltpu.SMEM)] + [whole] * len(arrays),
        out_specs=out_specs,
        scratch_shapes=[
            pltpu.VMEM((7 + 4 * members, tiles, lines, LANES), f32),
            pltpu.VMEM(total, f32),
            pltpu.VMEM((members, ROWS, COLS), f32),
            pltpu.VMEM((members, lines, LANES), f32),
            pltpu.SemaphoreType.DMA((2,)),
        ],
        compiler_params=pltpu.CompilerParams(vmem_limit_bytes=24 * 1024 * 1024),
        name="sweep_first" if first else "sweep_second",
    )(tile, *arrays)


def refined(count, cells, axis):
    shape = (count, cells) if axis == 0 else (cells, count)
    fine = lax.broadcasted_iota(jnp.int32, shape, axis).astype(f32)
    cell = lax.broadcasted_iota(jnp.int32, shape, 1 - axis).astype(f32)
    return jnp.maximum(1.0 - jnp.abs((fine + 2.5) * 0.25 - cell), 0.0).astype(bf16)


def put_field(perturb_ref, coarse, scale, out_ref, skip):
    members, fine_lat, fine_lon = perturb_ref.shape
    to_rows = refined(fine_lat, ROWS, 0)
    to_cols = refined(fine_lon, COLS, 1)
    field = jnp.zeros((fine_lat, fine_lon), f32)
    for k in range(members):
        high, low = split_two(coarse[k])
        tall = dot(to_rows, high) + dot(to_rows, low)
        high, low = split_two(tall)
        field = field + (dot(high, to_cols) + dot(low, to_cols)) * perturb_ref[k]
    field = scale * field
    across = fine_lon // LANES
    per_part = fine_lat // 8 * across // out_ref.shape[0]
    for n in range(per_part * out_ref.shape[0]):
        i = n // across * 8
        j = n % across * LANES
        at = skip + n % per_part * 8
        out_ref[n // per_part, at : at + 8, :] = field[i : i + 8, j : j + LANES]


def fields_kernel(scale, perturb_ref, length_ref, coarse_1_ref, coarse_2_ref, out_ref):
    put_field(perturb_ref, coarse_1_ref, -scale * length_ref[0, 0], out_ref.at[0], 0)
    put_field(perturb_ref, coarse_2_ref, -scale, out_ref.at[1], 0)


def ends_length(ends_ref):
    return length_of(jnp.sum(ends_ref[:, 1, :]), jnp.sum(ends_ref[:, 0, :]))


def join_kernel(ends_ref, fields_ref, out_ref):
    out_ref[...] = fields_ref[0] + ends_length(ends_ref) * fields_ref[1]


def analysis_kernel(length_ref, ends_ref, total_1_ref, total_2_ref, left_ref, right_ref, out_ref):
    one = length_ref[0, 0]
    two = ends_length(ends_ref)
    for k in range(out_ref.shape[0]):
        total = one * total_1_ref[k] + two * total_2_ref[k]
        half = jnp.dot(left_ref[...], total, precision=highest, preferred_element_type=f32)
        out_ref[k] = -jnp.dot(half, right_ref[...], precision=highest, preferred_element_type=f32)


def small_call(kernel, shapes, flops, name, *arrays):
    whole = pl.BlockSpec(memory_space=pltpu.VMEM)
    made = pl.pallas_call(
        kernel,
        out_shape=[jax.ShapeDtypeStruct(shape, f32) for shape in shapes],
        in_specs=[whole] * len(arrays),
        out_specs=[whole] * len(shapes),
        compiler_params=pltpu.CompilerParams(vmem_limit_bytes=20 * 1024 * 1024),
        cost_estimate=pl.CostEstimate(flops=flops, bytes_accessed=2 * 10**6, transcendentals=0),
        name=name,
    )(*arrays)
    return made if len(shapes) > 1 else made[0]


def per_device(perturb, loc_lat, loc_lon, obs_cell, obs_count, obs_innov, obs_error):
    members, fine_lat, fine_lon = perturb.shape
    coarse_lat, coarse_lon = fine_lat // 4, fine_lon // 4
    groups = lax.axis_size(MEM)
    scale = 1.0 / math.sqrt(members * groups - 1)
    lat, lon = lax.axis_index(LAT), lax.axis_index("lon")
    lat_tiles, lon_tiles = lax.axis_size(LAT), lax.axis_size("lon")
    slots = obs_cell.shape[-1]
    total_lat, total_lon = lat_tiles * coarse_lat, lon_tiles * coarse_lon
    padded_lat, padded_lon = total_lat + 16, total_lon + 128
    tile = (lat * lon_tiles + lon).astype(jnp.int32).reshape(1)

    lines = slots // LANES
    cell = obs_cell.reshape(lines, LANES)
    innovation = obs_innov.reshape(lines, LANES)
    error = obs_error.reshape(lines, LANES)
    message = picked(obs_count.reshape(1), perturb, cell, innovation, error, lat_tiles * lon_tiles)
    known = lax.all_to_all(message, TILES, 0, 0, tiled=True)

    first_lat, first_lon = lat * coarse_lat, lon * coarse_lon
    lat_all = kernel_block(loc_lat, -1, padded_lat, 0, total_lat)
    lon_all = kernel_block(loc_lon, -1, padded_lon, 0, total_lon)
    lat_tile = kernel_block(loc_lat, first_lat - 1, ROWS, 0, total_lat)
    lon_tile = kernel_block(loc_lon, first_lon - 1, COLS, 0, total_lon)
    left = jnp.einsum("ab,cb->ac", lat_tile, lat_all, precision=highest)
    right = jnp.einsum("ab,cb->ac", lon_all, lon_tile, precision=highest)
    left_own = kernel_block(loc_lat, -1, padded_lat, first_lat, coarse_lat).T
    right_own = kernel_block(loc_lon, -1, padded_lon, first_lon, coarse_lon)
    kernels = [*split_two(left), *split_two(right)]

    part, coarse_1, total_1 = sweep(tile, known, None, kernels, scale, lon_tiles, members, groups)
    mine = jnp.sum(lax.all_to_all(part, MEM, 0, 0, tiled=True), axis=0)
    seen = sent_to_all(mine, TILES)
    part, coarse_2, total_2, length_1, own = sweep(
        tile, known, seen, kernels, scale, lon_tiles, members, groups
    )
    mine = jnp.sum(lax.all_to_all(part, MEM, 0, 0, tiled=True), axis=0)
    bent = jnp.sum(jnp.stack([(mine * own[0]) ** 2, mine * own[1]]), axis=1)
    ends = sent_to_all(bent, TILES)

    field_rows = fine_lat * fine_lon // LANES
    along_x = lax.axis_size(X)
    part_rows, piece_rows = field_rows // along_x, field_rows // groups
    part = (along_x, part_rows, LANES)
    fields = small_call(
        functools.partial(fields_kernel, scale),
        ((2, *part),),
        10**9,
        "fields",
        perturb,
        length_1,
        coarse_1,
        coarse_2,
    )
    field = small_call(join_kernel, (part,), 10**6, "join", ends, fields)
    field = lax.all_to_all(field.reshape(groups, piece_rows, LANES), MEM, 0, 0, tiled=True)
    field = jnp.sum(field, axis=0)
    everything = sent_to_all(sent_to_all(field, Z).reshape(part_rows, LANES), X)
    whole = pl.BlockSpec(memory_space=pltpu.VMEM)
    analysis = pl.pallas_call(
        analysis_kernel,
        out_shape=jax.ShapeDtypeStruct((members, coarse_lat, coarse_lon), f32),
        in_specs=[whole] * 6,
        out_specs=whole,
        compiler_params=pltpu.CompilerParams(vmem_limit_bytes=66584576),
        cost_estimate=pl.CostEstimate(flops=2 * 10**9, bytes_accessed=5 * 10**6, transcendentals=0),
        name="analysis",
    )(length_1, ends, total_1, total_2, left_own, right_own)
    across = fine_lon // LANES
    increment = jnp.transpose(
        everything.reshape(fine_lat // 8, across, 8, LANES), (0, 2, 1, 3)
    ).reshape(fine_lat, fine_lon)
    return analysis, increment


def solution(mesh):
    torus = Mesh(
        mesh.devices.reshape(4, -1, 2, mesh.shape["lat"] // 2, mesh.shape["lon"]),
        ("mem_0", "mem_1", "lat_0", "lat_1", "lon"),
    )
    return jax.shard_map(
        per_device,
        mesh=torus,
        in_specs=(
            P(MEM, LAT, "lon"),
            P(),
            P(),
            P(LAT, "lon", None),
            P(LAT, "lon"),
            P(LAT, "lon", None),
            P(LAT, "lon", None),
        ),
        out_specs=(P(MEM, LAT, "lon"), P(LAT, "lon")),
        check_vma=False,
    )
```

```python
import functools
import math

import jax
import jax.numpy as jnp
from jax import lax
from jax.experimental import pallas as pl
from jax.experimental.pallas import tpu as pltpu
from jax.sharding import Mesh
from jax.sharding import PartitionSpec as P

MEM = ("mem_0", "mem_1")
LAT = ("lat_0", "lat_1")
TILES = ("lat_0", "lat_1", "lon")
X, Z = "mem_0", "mem_1"

tiny_floor = 1e-06
highest = lax.Precision.HIGHEST
f32 = jnp.float32
bf16 = jnp.bfloat16

ROWS = 112
COLS = 144
LANES = 128
TOGETHER = 2


def sent_to_all(x, axis):
    copies = jnp.broadcast_to(x, (lax.axis_size(axis), *x.shape))
    return lax.all_to_all(copies, axis, split_axis=0, concat_axis=0, tiled=True)


def scale_run(scales, first, count):
    padded = jnp.pad(scales, (8, 248), constant_values=1.0)
    return lax.dynamic_slice(padded, (first + 8,), (count,))


def kernel_block(scales, first_row, row_count, first_col, col_count):
    total = scales.shape[0]
    rows = first_row + jnp.arange(row_count, dtype=jnp.int32)
    cols = first_col + jnp.arange(col_count, dtype=jnp.int32)
    row_scale = scale_run(scales, first_row, row_count)
    col_scale = scale_run(scales, first_col, col_count)
    inside = (rows >= 0) & (rows < total)
    weight = jnp.where(inside, (jnp.sqrt(jnp.pi) * row_scale) ** (-0.5), jnp.zeros_like(row_scale))
    offset = (rows[:, None] - cols[None, :]).astype(f32)
    spread = row_scale[:, None] ** 2 + col_scale[None, :] ** 2
    return weight[:, None] * jnp.exp(-offset * offset / spread)


def split_two(x):
    high = x.astype(bf16)
    low = (x - high.astype(f32)).astype(bf16)
    return high, low


def nt_dot(a, b):
    return lax.dot_general(a, b, (((1,), (1,)), ((), ())), preferred_element_type=f32)


def dot(a, b):
    return jnp.dot(a, b, preferred_element_type=f32)


def lane_rows(read, count):
    return jnp.concatenate([read(r) for r in range(count)], axis=1)


def picked_kernel(count_ref, perturb_ref, cell_ref, innov_ref, error_ref, copies_ref, out_ref, sems):
    members, fine_lat, fine_lon = perturb_ref.shape
    lines = cell_ref.shape[0]
    step = 512
    per_step = step // LANES
    slot = lax.broadcasted_iota(jnp.int32, cell_ref.shape, 0) * LANES + lax.broadcasted_iota(
        jnp.int32, cell_ref.shape, 1
    )
    out_ref[:lines] = cell_ref[...].astype(f32)
    out_ref[lines : 2 * lines] = innov_ref[...]
    out_ref[2 * lines : 3 * lines] = jnp.where(slot < count_ref[0], 1.0 / error_ref[...], 0.0)
    blocks = []
    for k in range(members):
        blocks.extend(split_two(perturb_ref[k]))
    field = jnp.concatenate(blocks, axis=0)
    for start in range(0, lines, per_step):
        cell = lane_rows(lambda r: cell_ref[start + r : start + r + 1, :], per_step)
        row = cell // fine_lon
        col = cell - row * fine_lon
        at_col = lax.broadcasted_iota(jnp.int32, (fine_lon, step), 0) == col
        one = jnp.where(at_col, 1.0, 0.0).astype(bf16)
        values = dot(field, one)
        at_row = lax.broadcasted_iota(jnp.int32, (fine_lat, step), 0) == row
        for k in range(members):
            at = 2 * k * fine_lat
            mine = values[at : at + fine_lat] + values[at + fine_lat : at + 2 * fine_lat]
            found = jnp.sum(jnp.where(at_row, mine, 0.0), axis=0, keepdims=True)
            for r in range(per_step):
                at = (3 + k) * lines + start + r
                out_ref[at : at + 1, :] = found[:, r * LANES : (r + 1) * LANES]
    sends = [
        pltpu.make_async_copy(out_ref, copies_ref.at[n], sems.at[n]) for n in range(copies_ref.shape[0])
    ]
    for send in sends:
        send.start()
    for send in sends:
        send.wait()


def picked(count, perturb, cell, innovation, error, copies):
    whole = pl.BlockSpec(memory_space=pltpu.VMEM)
    message = ((3 + perturb.shape[0]) * cell.shape[0], LANES)
    return pl.pallas_call(
        picked_kernel,
        out_shape=pltpu.HBM((copies, *message), f32),
        in_specs=[pl.BlockSpec(memory_space=pltpu.SMEM)] + [whole] * 4,
        out_specs=pl.BlockSpec(memory_space=pltpu.HBM),
        scratch_shapes=[pltpu.VMEM(message, f32), pltpu.SemaphoreType.DMA((copies,))],
        compiler_params=pltpu.CompilerParams(vmem_limit_bytes=60 * 1024 * 1024),
        name="picked",
    )(count, perturb, cell, innovation, error)


def weights_of(observed, innovation, inverse):
    residual = (observed - innovation) * inverse
    return residual / jnp.sqrt(1.0 + residual * residual) * inverse


def length_of(grad_total, curvature):
    return grad_total / (grad_total + curvature + tiny_floor)


def masks(below, count):
    cell = lax.broadcasted_iota(jnp.int32, below.shape, 0).astype(f32)
    found = []
    for start in range(0, count, 16):
        at = (cell + start).astype(bf16)
        before = (cell + (start - 1)).astype(bf16)
        found.append((below == at, below == before))
    return found


def hat(where, lower, upper):
    zero = jnp.zeros_like(lower)
    return jnp.concatenate([jnp.where(at, lower, jnp.where(before, upper, zero)) for at, before in where], axis=0)


def sweep_kernel(first, scale, lon_tiles, members, *refs):
    tile_ref, known_ref = refs[:2]
    refs = refs[2:]
    if not first:
        seen_ref = refs[0]
        refs = refs[1:]
    left_ref, left_low_ref, right_ref, right_low_ref, part_ref, coarse_ref, total_out_ref = refs[:7]
    refs = refs[7:]
    if not first:
        length_ref, own_ref = refs[:2]
        refs = refs[2:]
    hold, total_ref, coarse_own_ref, image_ref, sems = refs
    tiles = known_ref.shape[0]
    lines = known_ref.shape[1] // (3 + members)
    width = total_ref.shape[2]

    def known(n):
        return known_ref[:, n * lines : (n + 1) * lines, :]

    cell = known(0)
    innovation = known(1)
    inverse = known(2)
    row = jnp.floor(cell * (1.0 / 512.0))
    col = (cell - row * 512.0 + 2.5) * 0.25
    row = (row + 2.5) * 0.25
    row_cell, col_cell = jnp.floor(row), jnp.floor(col)
    row_up, col_up = row - row_cell, col - col_cell
    hold[0], hold[1], hold[2], hold[3] = row_cell, col_cell, 1.0 - col_up, col_up
    hold[4], hold[5] = 1.0 - row_up, row_up
    force = weights_of(0.0, innovation, inverse)
    if not first:
        image = seen_ref[...]
        length = length_of(jnp.sum(force * image), jnp.sum((image * inverse) ** 2))
        force = weights_of(-length * image, innovation, inverse) - length * force
        length_ref[...] = jnp.broadcast_to(length, length_ref.shape)
    hold[6] = force
    n = 7
    for k in range(members):
        q = known(3 + k) * force * scale
        for share in (1.0 - row_up, row_up):
            whole = share * q
            high = whole.astype(bf16).astype(f32)
            hold[n] = high
            hold[n + 1] = whole - high
            n += 2
    total_ref[...] = jnp.zeros_like(total_ref)

    def line(i, t):
        return lane_rows(
            lambda r: jnp.broadcast_to(hold[i, t, r : r + 1, :], (16, LANES)).astype(bf16), lines
        )

    def add_tile(t):
        lat = t // lon_tiles
        lon = t - lat * lon_tiles
        cols = hat(masks(line(1, t), COLS), line(2, t), line(3, t))
        where = masks(line(0, t), ROWS)
        blocks = []
        for k in range(members):
            for term in range(2):
                at = 7 + 4 * k + term
                blocks.append(hat(where, line(at, t), line(at + 2, t)))
        made = nt_dot(jnp.concatenate(blocks, axis=0), cols)
        at = pl.ds(pl.multiple_of(lat * 96, 8), ROWS)
        for k in range(members):
            both = made[2 * k * ROWS : (2 * k + 1) * ROWS] + made[(2 * k + 1) * ROWS : (2 * k + 2) * ROWS]
            total_ref[k, at, pl.ds(pl.multiple_of(lon * 128, 128), 128)] += both[:, :128]
            total_ref[k, at, pl.ds(pl.multiple_of(lon * 128 + 128, 128), COLS - 128)] += both[:, 128:]

    def some_tiles(t, carry):
        for n in range(TOGETHER):
            add_tile(t * TOGETHER + n)
        return carry

    lax.fori_loop(0, tiles // TOGETHER, some_tiles, 0)
    total_copy = pltpu.make_async_copy(total_ref, total_out_ref, sems.at[0])
    total_copy.start()

    own = tile_ref[0]
    rows = hat(masks(line(0, own), ROWS), line(4, own), line(5, own)).astype(f32)
    cols = hat(masks(line(1, own), COLS), line(2, own), line(3, own))
    high, low = zip(*(split_two(total_ref[k]) for k in range(members)))
    high, low = jnp.concatenate(high, axis=1), jnp.concatenate(low, axis=1)
    half = dot(jnp.concatenate([left_ref[...], left_low_ref[...]], axis=0), high)
    half = half[:ROWS] + (half[ROWS:] + dot(left_ref[...], low))
    half = jnp.concatenate([half[:, k * width : (k + 1) * width] for k in range(members)], axis=0)
    high, low = split_two(half)
    count = high.shape[0]
    coarse = dot(jnp.concatenate([high, low], axis=0), right_ref[...])
    coarse = coarse[:count] + (coarse[count:] + dot(high, right_low_ref[...]))
    for k in range(members):
        coarse_own_ref[k] = coarse[k * ROWS : (k + 1) * ROWS]
    coarse_copy = pltpu.make_async_copy(coarse_own_ref, coarse_ref, sems.at[1])
    coarse_copy.start()
    made = dot(jnp.concatenate(split_two(coarse), axis=0), cols)
    for k in range(members):
        mine = made[k * ROWS : (k + 1) * ROWS] + made[count + k * ROWS : count + (k + 1) * ROWS]
        value = jnp.sum(mine * rows, axis=0, keepdims=True)
        for r in range(lines):
            image_ref[k, r : r + 1, :] = value[:, r * LANES : (r + 1) * LANES]
    image = jnp.zeros((lines, LANES), f32)
    for k in range(members):
        image = image + image_ref[k] * known_ref[own, (3 + k) * lines : (4 + k) * lines, :]
    image = image * scale
    if not first:
        own_ref[0] = known_ref[own, 2 * lines : 3 * lines, :]
        own_ref[1] = hold[6, own]
    for n in range(part_ref.shape[0]):
        part_ref[n] = image
    coarse_copy.wait()
    total_copy.wait()


def sweep(tile, known, seen, kernels, scale, lon_tiles, members, groups):
    tiles = known.shape[0]
    lines = known.shape[1] // (3 + members)
    first = seen is None
    left, _, right, _ = kernels
    total = (members, left.shape[1], right.shape[0])
    whole = pl.BlockSpec(memory_space=pltpu.VMEM)
    out_shape = [
        jax.ShapeDtypeStruct((groups, lines, LANES), f32),
        pltpu.HBM((members, ROWS, COLS), f32),
        pltpu.HBM(total, f32),
    ]
    far = pl.BlockSpec(memory_space=pltpu.HBM)
    out_specs = [whole, far, far]
    if not first:
        out_shape.append(jax.ShapeDtypeStruct((1, LANES), f32))
        out_shape.append(jax.ShapeDtypeStruct((2, lines, LANES), f32))
        out_specs += [whole, whole]
    arrays = [known] if first else [known, seen]
    arrays += kernels
    return pl.pallas_call(
        functools.partial(sweep_kernel, first, scale, lon_tiles, members),
        out_shape=out_shape,
        in_specs=[pl.BlockSpec(memory_space=pltpu.SMEM)] + [whole] * len(arrays),
        out_specs=out_specs,
        scratch_shapes=[
            pltpu.VMEM((7 + 4 * members, tiles, lines, LANES), f32),
            pltpu.VMEM(total, f32),
            pltpu.VMEM((members, ROWS, COLS), f32),
            pltpu.VMEM((members, lines, LANES), f32),
            pltpu.SemaphoreType.DMA((2,)),
        ],
        compiler_params=pltpu.CompilerParams(vmem_limit_bytes=24 * 1024 * 1024),
        name="sweep_first" if first else "sweep_second",
    )(tile, *arrays)


def refined(count, cells, axis):
    shape = (count, cells) if axis == 0 else (cells, count)
    fine = lax.broadcasted_iota(jnp.int32, shape, axis).astype(f32)
    cell = lax.broadcasted_iota(jnp.int32, shape, 1 - axis).astype(f32)
    return jnp.maximum(1.0 - jnp.abs((fine + 2.5) * 0.25 - cell), 0.0).astype(bf16)


def put_field(perturb_ref, coarse, scale, out_ref, skip):
    members, fine_lat, fine_lon = perturb_ref.shape
    to_rows = refined(fine_lat, ROWS, 0)
    to_cols = refined(fine_lon, COLS, 1)
    field = jnp.zeros((fine_lat, fine_lon), f32)
    for k in range(members):
        high, low = split_two(coarse[k])
        tall = dot(to_rows, high) + dot(to_rows, low)
        high, low = split_two(tall)
        field = field + (dot(high, to_cols) + dot(low, to_cols)) * perturb_ref[k]
    field = scale * field
    across = fine_lon // LANES
    per_part = fine_lat // 8 * across // out_ref.shape[0]
    for n in range(per_part * out_ref.shape[0]):
        i = n // across * 8
        j = n % across * LANES
        at = skip + n % per_part * 8
        out_ref[n // per_part, at : at + 8, :] = field[i : i + 8, j : j + LANES]


def fields_kernel(scale, perturb_ref, length_ref, coarse_1_ref, coarse_2_ref, out_ref):
    put_field(perturb_ref, coarse_1_ref, -scale * length_ref[0, 0], out_ref.at[0], 0)
    put_field(perturb_ref, coarse_2_ref, -scale, out_ref.at[1], 0)


def ends_length(ends_ref):
    return length_of(jnp.sum(ends_ref[:, 1, :]), jnp.sum(ends_ref[:, 0, :]))


def join_kernel(ends_ref, fields_ref, out_ref):
    out_ref[...] = fields_ref[0] + ends_length(ends_ref) * fields_ref[1]


def analysis_kernel(length_ref, ends_ref, total_1_ref, total_2_ref, left_ref, right_ref, out_ref):
    one = length_ref[0, 0]
    two = ends_length(ends_ref)
    for k in range(out_ref.shape[0]):
        total = one * total_1_ref[k] + two * total_2_ref[k]
        half = jnp.dot(left_ref[...], total, precision=highest, preferred_element_type=f32)
        out_ref[k] = -jnp.dot(half, right_ref[...], precision=highest, preferred_element_type=f32)


def small_call(kernel, shapes, flops, name, *arrays):
    whole = pl.BlockSpec(memory_space=pltpu.VMEM)
    made = pl.pallas_call(
        kernel,
        out_shape=[jax.ShapeDtypeStruct(shape, f32) for shape in shapes],
        in_specs=[whole] * len(arrays),
        out_specs=[whole] * len(shapes),
        compiler_params=pltpu.CompilerParams(vmem_limit_bytes=20 * 1024 * 1024),
        cost_estimate=pl.CostEstimate(flops=flops, bytes_accessed=2 * 10**6, transcendentals=0),
        name=name,
    )(*arrays)
    return made if len(shapes) > 1 else made[0]


def per_device(perturb, loc_lat, loc_lon, obs_cell, obs_count, obs_innov, obs_error):
    members, fine_lat, fine_lon = perturb.shape
    coarse_lat, coarse_lon = fine_lat // 4, fine_lon // 4
    groups = lax.axis_size(MEM)
    scale = 1.0 / math.sqrt(members * groups - 1)
    lat, lon = lax.axis_index(LAT), lax.axis_index("lon")
    lat_tiles, lon_tiles = lax.axis_size(LAT), lax.axis_size("lon")
    slots = obs_cell.shape[-1]
    total_lat, total_lon = lat_tiles * coarse_lat, lon_tiles * coarse_lon
    padded_lat, padded_lon = total_lat + 16, total_lon + 128
    tile = (lat * lon_tiles + lon).astype(jnp.int32).reshape(1)

    lines = slots // LANES
    cell = obs_cell.reshape(lines, LANES)
    innovation = obs_innov.reshape(lines, LANES)
    error = obs_error.reshape(lines, LANES)
    message = picked(obs_count.reshape(1), perturb, cell, innovation, error, lat_tiles * lon_tiles)
    known = lax.all_to_all(message, TILES, 0, 0, tiled=True)

    first_lat, first_lon = lat * coarse_lat, lon * coarse_lon
    lat_all = kernel_block(loc_lat, -1, padded_lat, 0, total_lat)
    lon_all = kernel_block(loc_lon, -1, padded_lon, 0, total_lon)
    lat_tile = kernel_block(loc_lat, first_lat - 1, ROWS, 0, total_lat)
    lon_tile = kernel_block(loc_lon, first_lon - 1, COLS, 0, total_lon)
    left = jnp.einsum("ab,cb->ac", lat_tile, lat_all, precision=highest)
    right = jnp.einsum("ab,cb->ac", lon_all, lon_tile, precision=highest)
    left_own = kernel_block(loc_lat, -1, padded_lat, first_lat, coarse_lat).T
    right_own = kernel_block(loc_lon, -1, padded_lon, first_lon, coarse_lon)
    kernels = [*split_two(left), *split_two(right)]

    part, coarse_1, total_1 = sweep(tile, known, None, kernels, scale, lon_tiles, members, groups)
    mine = jnp.sum(lax.all_to_all(part, MEM, 0, 0, tiled=True), axis=0)
    seen = sent_to_all(mine, TILES)
    part, coarse_2, total_2, length_1, own = sweep(
        tile, known, seen, kernels, scale, lon_tiles, members, groups
    )
    mine = jnp.sum(lax.all_to_all(part, MEM, 0, 0, tiled=True), axis=0)
    bent = jnp.sum(jnp.stack([(mine * own[0]) ** 2, mine * own[1]]), axis=1)
    ends = sent_to_all(bent, TILES)

    field_rows = fine_lat * fine_lon // LANES
    along_x = lax.axis_size(X)
    part_rows, piece_rows = field_rows // along_x, field_rows // groups
    part = (along_x, part_rows, LANES)
    fields = small_call(
        functools.partial(fields_kernel, scale),
        ((2, *part),),
        10**9,
        "fields",
        perturb,
        length_1,
        coarse_1,
        coarse_2,
    )
    field = small_call(join_kernel, (part,), 10**6, "join", ends, fields)
    field = lax.all_to_all(field.reshape(groups, piece_rows, LANES), MEM, 0, 0, tiled=True)
    field = jnp.sum(field, axis=0)
    everything = sent_to_all(sent_to_all(field, Z).reshape(part_rows, LANES), X)
    whole = pl.BlockSpec(memory_space=pltpu.VMEM)
    analysis = pl.pallas_call(
        analysis_kernel,
        out_shape=jax.ShapeDtypeStruct((members, coarse_lat, coarse_lon), f32),
        in_specs=[whole] * 6,
        out_specs=whole,
        compiler_params=pltpu.CompilerParams(vmem_limit_bytes=24 * 1024 * 1024),
        cost_estimate=pl.CostEstimate(flops=2 * 10**9, bytes_accessed=5 * 10**6, transcendentals=0),
        name="analysis",
    )(length_1, ends, total_1, total_2, left_own, right_own)
    across = fine_lon // LANES
    increment = jnp.transpose(
        everything.reshape(fine_lat // 8, across, 8, LANES), (0, 2, 1, 3)
    ).reshape(fine_lat, fine_lon)
    return analysis, increment


def solution(mesh):
    torus = Mesh(
        mesh.devices.reshape(4, -1, 2, mesh.shape["lat"] // 2, mesh.shape["lon"]),
        ("mem_0", "mem_1", "lat_0", "lat_1", "lon"),
    )
    return jax.shard_map(
        per_device,
        mesh=torus,
        in_specs=(
            P(MEM, LAT, "lon"),
            P(),
            P(),
            P(LAT, "lon", None),
            P(LAT, "lon"),
            P(LAT, "lon", None),
            P(LAT, "lon", None),
        ),
        out_specs=(P(MEM, LAT, "lon"), P(LAT, "lon")),
        check_vma=False,
    )
```

```python
import functools
import math

import jax
import jax.numpy as jnp
from jax import lax
from jax.experimental import pallas as pl
from jax.experimental.pallas import tpu as pltpu
from jax.sharding import Mesh
from jax.sharding import PartitionSpec as P

MEM = ("mem_0", "mem_1")
LAT = ("lat_0", "lat_1")
TILES = ("lat_0", "lat_1", "lon")
X, Z = "mem_0", "mem_1"

tiny_floor = 1e-06
highest = lax.Precision.HIGHEST
f32 = jnp.float32
bf16 = jnp.bfloat16

ROWS = 112
COLS = 144
LANES = 128
TOGETHER = 2


def sent_to_all(x, axis):
    copies = jnp.broadcast_to(x, (lax.axis_size(axis), *x.shape))
    return lax.all_to_all(copies, axis, split_axis=0, concat_axis=0, tiled=True)


def scale_run(scales, first, count):
    padded = jnp.pad(scales, (8, 248), constant_values=1.0)
    return lax.dynamic_slice(padded, (first + 8,), (count,))


def kernel_block(scales, first_row, row_count, first_col, col_count):
    total = scales.shape[0]
    rows = first_row + jnp.arange(row_count, dtype=jnp.int32)
    cols = first_col + jnp.arange(col_count, dtype=jnp.int32)
    row_scale = scale_run(scales, first_row, row_count)
    col_scale = scale_run(scales, first_col, col_count)
    inside = (rows >= 0) & (rows < total)
    weight = jnp.where(inside, (jnp.sqrt(jnp.pi) * row_scale) ** (-0.5), jnp.zeros_like(row_scale))
    offset = (rows[:, None] - cols[None, :]).astype(f32)
    spread = row_scale[:, None] ** 2 + col_scale[None, :] ** 2
    return weight[:, None] * jnp.exp(-offset * offset / spread)


def split_two(x):
    high = x.astype(bf16)
    low = (x - high.astype(f32)).astype(bf16)
    return high, low


def nt_dot(a, b):
    return lax.dot_general(a, b, (((1,), (1,)), ((), ())), preferred_element_type=f32)


def dot(a, b):
    return jnp.dot(a, b, preferred_element_type=f32)


def lane_rows(read, count):
    return jnp.concatenate([read(r) for r in range(count)], axis=1)


def picked_kernel(count_ref, perturb_ref, cell_ref, innov_ref, error_ref, copies_ref, out_ref, sems):
    members, fine_lat, fine_lon = perturb_ref.shape
    lines = cell_ref.shape[0]
    step = 512
    per_step = step // LANES
    slot = lax.broadcasted_iota(jnp.int32, cell_ref.shape, 0) * LANES + lax.broadcasted_iota(
        jnp.int32, cell_ref.shape, 1
    )
    out_ref[:lines] = cell_ref[...].astype(f32)
    out_ref[lines : 2 * lines] = innov_ref[...]
    out_ref[2 * lines : 3 * lines] = jnp.where(slot < count_ref[0], 1.0 / error_ref[...], 0.0)
    blocks = []
    for k in range(members):
        blocks.extend(split_two(perturb_ref[k]))
    field = jnp.concatenate(blocks, axis=0)
    for start in range(0, lines, per_step):
        cell = lane_rows(lambda r: cell_ref[start + r : start + r + 1, :], per_step)
        row = cell // fine_lon
        col = cell - row * fine_lon
        at_col = lax.broadcasted_iota(jnp.int32, (fine_lon, step), 0) == col
        one = jnp.where(at_col, 1.0, 0.0).astype(bf16)
        values = dot(field, one)
        at_row = lax.broadcasted_iota(jnp.int32, (fine_lat, step), 0) == row
        for k in range(members):
            at = 2 * k * fine_lat
            mine = values[at : at + fine_lat] + values[at + fine_lat : at + 2 * fine_lat]
            found = jnp.sum(jnp.where(at_row, mine, 0.0), axis=0, keepdims=True)
            for r in range(per_step):
                at = (3 + k) * lines + start + r
                out_ref[at : at + 1, :] = found[:, r * LANES : (r + 1) * LANES]
    sends = [
        pltpu.make_async_copy(out_ref, copies_ref.at[n], sems.at[n]) for n in range(copies_ref.shape[0])
    ]
    for send in sends:
        send.start()
    for send in sends:
        send.wait()


def picked(count, perturb, cell, innovation, error, copies):
    whole = pl.BlockSpec(memory_space=pltpu.VMEM)
    message = ((3 + perturb.shape[0]) * cell.shape[0], LANES)
    return pl.pallas_call(
        picked_kernel,
        out_shape=pltpu.HBM((copies, *message), f32),
        in_specs=[pl.BlockSpec(memory_space=pltpu.SMEM)] + [whole] * 4,
        out_specs=pl.BlockSpec(memory_space=pltpu.HBM),
        scratch_shapes=[pltpu.VMEM(message, f32), pltpu.SemaphoreType.DMA((copies,))],
        compiler_params=pltpu.CompilerParams(vmem_limit_bytes=60 * 1024 * 1024),
        name="picked",
    )(count, perturb, cell, innovation, error)


def weights_of(observed, innovation, inverse):
    residual = (observed - innovation) * inverse
    return residual / jnp.sqrt(1.0 + residual * residual) * inverse


def length_of(grad_total, curvature):
    return grad_total / (grad_total + curvature + tiny_floor)


def masks(below, count):
    cell = lax.broadcasted_iota(jnp.int32, below.shape, 0).astype(f32)
    found = []
    for start in range(0, count, 16):
        at = (cell + start).astype(bf16)
        before = (cell + (start - 1)).astype(bf16)
        found.append((below == at, below == before))
    return found


def hat(where, lower, upper):
    zero = jnp.zeros_like(lower)
    return jnp.concatenate([jnp.where(at, lower, jnp.where(before, upper, zero)) for at, before in where], axis=0)


def sweep_kernel(first, scale, lon_tiles, members, *refs):
    tile_ref, known_ref = refs[:2]
    refs = refs[2:]
    if not first:
        seen_ref = refs[0]
        refs = refs[1:]
    left_ref, left_low_ref, right_ref, right_low_ref, part_ref, coarse_ref, total_out_ref = refs[:7]
    refs = refs[7:]
    if not first:
        length_ref, own_ref = refs[:2]
        refs = refs[2:]
    hold, total_ref, coarse_own_ref, image_ref, sems = refs
    tiles = known_ref.shape[0]
    lines = known_ref.shape[1] // (3 + members)
    width = total_ref.shape[2]

    def known(n):
        return known_ref[:, n * lines : (n + 1) * lines, :]

    cell = known(0)
    innovation = known(1)
    inverse = known(2)
    row = jnp.floor(cell * (1.0 / 512.0))
    col = (cell - row * 512.0 + 2.5) * 0.25
    row = (row + 2.5) * 0.25
    row_cell, col_cell = jnp.floor(row), jnp.floor(col)
    row_up, col_up = row - row_cell, col - col_cell
    hold[0], hold[1], hold[2], hold[3] = row_cell, col_cell, 1.0 - col_up, col_up
    hold[4], hold[5] = 1.0 - row_up, row_up
    force = weights_of(0.0, innovation, inverse)
    if not first:
        image = seen_ref[...]
        length = length_of(jnp.sum(force * image), jnp.sum((image * inverse) ** 2))
        force = weights_of(-length * image, innovation, inverse) - length * force
        length_ref[...] = jnp.broadcast_to(length, length_ref.shape)
    hold[6] = force
    n = 7
    for k in range(members):
        q = known(3 + k) * force * scale
        for share in (1.0 - row_up, row_up):
            whole = share * q
            high = whole.astype(bf16).astype(f32)
            hold[n] = high
            hold[n + 1] = whole - high
            n += 2
    total_ref[...] = jnp.zeros_like(total_ref)

    def line(i, t):
        return lane_rows(
            lambda r: jnp.broadcast_to(hold[i, t, r : r + 1, :], (16, LANES)).astype(bf16), lines
        )

    def add_tile(t):
        lat = t // lon_tiles
        lon = t - lat * lon_tiles
        cols = hat(masks(line(1, t), COLS), line(2, t), line(3, t))
        where = masks(line(0, t), ROWS)
        blocks = []
        for k in range(members):
            for term in range(2):
                at = 7 + 4 * k + term
                blocks.append(hat(where, line(at, t), line(at + 2, t)))
        made = nt_dot(jnp.concatenate(blocks, axis=0), cols)
        at = pl.ds(pl.multiple_of(lat * 96, 8), ROWS)
        for k in range(members):
            both = made[2 * k * ROWS : (2 * k + 1) * ROWS] + made[(2 * k + 1) * ROWS : (2 * k + 2) * ROWS]
            total_ref[k, at, pl.ds(pl.multiple_of(lon * 128, 128), 128)] += both[:, :128]
            total_ref[k, at, pl.ds(pl.multiple_of(lon * 128 + 128, 128), COLS - 128)] += both[:, 128:]

    def some_tiles(t, carry):
        for n in range(TOGETHER):
            add_tile(t * TOGETHER + n)
        return carry

    lax.fori_loop(0, tiles // TOGETHER, some_tiles, 0)
    total_copy = pltpu.make_async_copy(total_ref, total_out_ref, sems.at[0])
    total_copy.start()

    own = tile_ref[0]
    rows = hat(masks(line(0, own), ROWS), line(4, own), line(5, own)).astype(f32)
    cols = hat(masks(line(1, own), COLS), line(2, own), line(3, own))
    high, low = zip(*(split_two(total_ref[k]) for k in range(members)))
    high, low = jnp.concatenate(high, axis=1), jnp.concatenate(low, axis=1)
    half = dot(jnp.concatenate([left_ref[...], left_low_ref[...]], axis=0), high)
    half = half[:ROWS] + (half[ROWS:] + dot(left_ref[...], low))
    half = jnp.concatenate([half[:, k * width : (k + 1) * width] for k in range(members)], axis=0)
    high, low = split_two(half)
    count = high.shape[0]
    coarse = dot(jnp.concatenate([high, low], axis=0), right_ref[...])
    coarse = coarse[:count] + (coarse[count:] + dot(high, right_low_ref[...]))
    for k in range(members):
        coarse_own_ref[k] = coarse[k * ROWS : (k + 1) * ROWS]
    coarse_copy = pltpu.make_async_copy(coarse_own_ref, coarse_ref, sems.at[1])
    coarse_copy.start()
    made = dot(jnp.concatenate(split_two(coarse), axis=0), cols)
    for k in range(members):
        mine = made[k * ROWS : (k + 1) * ROWS] + made[count + k * ROWS : count + (k + 1) * ROWS]
        value = jnp.sum(mine * rows, axis=0, keepdims=True)
        for r in range(lines):
            image_ref[k, r : r + 1, :] = value[:, r * LANES : (r + 1) * LANES]
    image = jnp.zeros((lines, LANES), f32)
    for k in range(members):
        image = image + image_ref[k] * known_ref[own, (3 + k) * lines : (4 + k) * lines, :]
    image = image * scale
    if not first:
        own_ref[0] = known_ref[own, 2 * lines : 3 * lines, :]
        own_ref[1] = hold[6, own]
    for n in range(part_ref.shape[0]):
        part_ref[n] = image
    coarse_copy.wait()
    total_copy.wait()


def sweep(tile, known, seen, kernels, scale, lon_tiles, members, groups):
    tiles = known.shape[0]
    lines = known.shape[1] // (3 + members)
    first = seen is None
    left, _, right, _ = kernels
    total = (members, left.shape[1], right.shape[0])
    whole = pl.BlockSpec(memory_space=pltpu.VMEM)
    out_shape = [
        jax.ShapeDtypeStruct((groups, lines, LANES), f32),
        pltpu.HBM((members, ROWS, COLS), f32),
        pltpu.HBM(total, f32),
    ]
    far = pl.BlockSpec(memory_space=pltpu.HBM)
    out_specs = [whole, far, far]
    if not first:
        out_shape.append(jax.ShapeDtypeStruct((1, LANES), f32))
        out_shape.append(jax.ShapeDtypeStruct((2, lines, LANES), f32))
        out_specs += [whole, whole]
    arrays = [known] if first else [known, seen]
    arrays += kernels
    return pl.pallas_call(
        functools.partial(sweep_kernel, first, scale, lon_tiles, members),
        out_shape=out_shape,
        in_specs=[pl.BlockSpec(memory_space=pltpu.SMEM)] + [whole] * len(arrays),
        out_specs=out_specs,
        scratch_shapes=[
            pltpu.VMEM((7 + 4 * members, tiles, lines, LANES), f32),
            pltpu.VMEM(total, f32),
            pltpu.VMEM((members, ROWS, COLS), f32),
            pltpu.VMEM((members, lines, LANES), f32),
            pltpu.SemaphoreType.DMA((2,)),
        ],
        compiler_params=pltpu.CompilerParams(vmem_limit_bytes=24 * 1024 * 1024),
        name="sweep_first" if first else "sweep_second",
    )(tile, *arrays)


def refined(count, cells, axis):
    shape = (count, cells) if axis == 0 else (cells, count)
    fine = lax.broadcasted_iota(jnp.int32, shape, axis).astype(f32)
    cell = lax.broadcasted_iota(jnp.int32, shape, 1 - axis).astype(f32)
    return jnp.maximum(1.0 - jnp.abs((fine + 2.5) * 0.25 - cell), 0.0).astype(bf16)


def put_field(perturb_ref, coarse, scale, out_ref, skip):
    members, fine_lat, fine_lon = perturb_ref.shape
    to_rows = refined(fine_lat, ROWS, 0)
    to_cols = refined(fine_lon, COLS, 1)
    field = jnp.zeros((fine_lat, fine_lon), f32)
    for k in range(members):
        high, low = split_two(coarse[k])
        tall = dot(to_rows, high) + dot(to_rows, low)
        high, low = split_two(tall)
        field = field + (dot(high, to_cols) + dot(low, to_cols)) * perturb_ref[k]
    field = scale * field
    across = fine_lon // LANES
    per_part = fine_lat // 8 * across // out_ref.shape[0]
    for n in range(per_part * out_ref.shape[0]):
        i = n // across * 8
        j = n % across * LANES
        at = skip + n % per_part * 8
        out_ref[n // per_part, at : at + 8, :] = field[i : i + 8, j : j + LANES]


def fields_kernel(scale, perturb_ref, length_ref, coarse_1_ref, coarse_2_ref, out_ref):
    put_field(perturb_ref, coarse_1_ref, -scale * length_ref[0, 0], out_ref.at[0], 0)
    put_field(perturb_ref, coarse_2_ref, -scale, out_ref.at[1], 0)


def ends_length(ends_ref):
    return length_of(jnp.sum(ends_ref[:, 1, :]), jnp.sum(ends_ref[:, 0, :]))


def join_kernel(ends_ref, fields_ref, out_ref):
    out_ref[...] = fields_ref[0] + ends_length(ends_ref) * fields_ref[1]


def join(ends, fields):
    _, parts, rows, lanes = fields.shape
    return pl.pallas_call(
        join_kernel,
        grid=(parts,),
        out_shape=jax.ShapeDtypeStruct((parts, rows, lanes), f32),
        in_specs=[
            pl.BlockSpec(memory_space=pltpu.VMEM),
            pl.BlockSpec((2, 1, rows, lanes), lambda n: (0, n, 0, 0)),
        ],
        out_specs=pl.BlockSpec((1, rows, lanes), lambda n: (n, 0, 0)),
        compiler_params=pltpu.CompilerParams(vmem_limit_bytes=60 * 1024 * 1024),
        name="join",
    )(ends, fields)


def analysis_kernel(length_ref, ends_ref, total_1_ref, total_2_ref, left_ref, right_ref, out_ref):
    one = length_ref[0, 0]
    two = ends_length(ends_ref)
    for k in range(out_ref.shape[0]):
        total = one * total_1_ref[k] + two * total_2_ref[k]
        half = jnp.dot(left_ref[...], total, precision=highest, preferred_element_type=f32)
        out_ref[k] = -jnp.dot(half, right_ref[...], precision=highest, preferred_element_type=f32)


def small_call(kernel, shapes, flops, name, *arrays):
    whole = pl.BlockSpec(memory_space=pltpu.VMEM)
    made = pl.pallas_call(
        kernel,
        out_shape=[jax.ShapeDtypeStruct(shape, f32) for shape in shapes],
        in_specs=[whole] * len(arrays),
        out_specs=[whole] * len(shapes),
        compiler_params=pltpu.CompilerParams(vmem_limit_bytes=20 * 1024 * 1024),
        cost_estimate=pl.CostEstimate(flops=flops, bytes_accessed=2 * 10**6, transcendentals=0),
        name=name,
    )(*arrays)
    return made if len(shapes) > 1 else made[0]


def per_device(perturb, loc_lat, loc_lon, obs_cell, obs_count, obs_innov, obs_error):
    members, fine_lat, fine_lon = perturb.shape
    coarse_lat, coarse_lon = fine_lat // 4, fine_lon // 4
    groups = lax.axis_size(MEM)
    scale = 1.0 / math.sqrt(members * groups - 1)
    lat, lon = lax.axis_index(LAT), lax.axis_index("lon")
    lat_tiles, lon_tiles = lax.axis_size(LAT), lax.axis_size("lon")
    slots = obs_cell.shape[-1]
    total_lat, total_lon = lat_tiles * coarse_lat, lon_tiles * coarse_lon
    padded_lat, padded_lon = total_lat + 16, total_lon + 128
    tile = (lat * lon_tiles + lon).astype(jnp.int32).reshape(1)

    lines = slots // LANES
    cell = obs_cell.reshape(lines, LANES)
    innovation = obs_innov.reshape(lines, LANES)
    error = obs_error.reshape(lines, LANES)
    message = picked(obs_count.reshape(1), perturb, cell, innovation, error, lat_tiles * lon_tiles)
    known = lax.all_to_all(message, TILES, 0, 0, tiled=True)

    first_lat, first_lon = lat * coarse_lat, lon * coarse_lon
    lat_all = kernel_block(loc_lat, -1, padded_lat, 0, total_lat)
    lon_all = kernel_block(loc_lon, -1, padded_lon, 0, total_lon)
    lat_tile = kernel_block(loc_lat, first_lat - 1, ROWS, 0, total_lat)
    lon_tile = kernel_block(loc_lon, first_lon - 1, COLS, 0, total_lon)
    left = jnp.einsum("ab,cb->ac", lat_tile, lat_all, precision=highest)
    right = jnp.einsum("ab,cb->ac", lon_all, lon_tile, precision=highest)
    left_own = kernel_block(loc_lat, -1, padded_lat, first_lat, coarse_lat).T
    right_own = kernel_block(loc_lon, -1, padded_lon, first_lon, coarse_lon)
    kernels = [*split_two(left), *split_two(right)]

    part, coarse_1, total_1 = sweep(tile, known, None, kernels, scale, lon_tiles, members, groups)
    mine = jnp.sum(lax.all_to_all(part, MEM, 0, 0, tiled=True), axis=0)
    seen = sent_to_all(mine, TILES)
    part, coarse_2, total_2, length_1, own = sweep(
        tile, known, seen, kernels, scale, lon_tiles, members, groups
    )
    mine = jnp.sum(lax.all_to_all(part, MEM, 0, 0, tiled=True), axis=0)
    bent = jnp.sum(jnp.stack([(mine * own[0]) ** 2, mine * own[1]]), axis=1)
    field_rows = fine_lat * fine_lon // LANES
    along_x = lax.axis_size(X)
    part_rows, piece_rows = field_rows // along_x, field_rows // groups
    part = (along_x, part_rows, LANES)
    fields = small_call(
        functools.partial(fields_kernel, scale),
        ((2, *part),),
        10**9,
        "fields",
        perturb,
        length_1,
        coarse_1,
        coarse_2,
    )
    bent, fields = lax.optimization_barrier((bent, fields))
    ends = sent_to_all(bent, TILES)

    field = join(ends, fields)
    field = lax.all_to_all(field.reshape(groups, piece_rows, LANES), MEM, 0, 0, tiled=True)
    field = jnp.sum(field, axis=0)
    everything = sent_to_all(sent_to_all(field, Z).reshape(part_rows, LANES), X)
    whole = pl.BlockSpec(memory_space=pltpu.VMEM)
    analysis = pl.pallas_call(
        analysis_kernel,
        out_shape=jax.ShapeDtypeStruct((members, coarse_lat, coarse_lon), f32),
        in_specs=[whole] * 6,
        out_specs=whole,
        compiler_params=pltpu.CompilerParams(vmem_limit_bytes=24 * 1024 * 1024),
        cost_estimate=pl.CostEstimate(flops=2 * 10**9, bytes_accessed=5 * 10**6, transcendentals=0),
        name="analysis",
    )(length_1, ends, total_1, total_2, left_own, right_own)
    across = fine_lon // LANES
    increment = jnp.transpose(
        everything.reshape(fine_lat // 8, across, 8, LANES), (0, 2, 1, 3)
    ).reshape(fine_lat, fine_lon)
    return analysis, increment


def solution(mesh):
    torus = Mesh(
        mesh.devices.reshape(4, -1, 2, mesh.shape["lat"] // 2, mesh.shape["lon"]),
        ("mem_0", "mem_1", "lat_0", "lat_1", "lon"),
    )
    return jax.shard_map(
        per_device,
        mesh=torus,
        in_specs=(
            P(MEM, LAT, "lon"),
            P(),
            P(),
            P(LAT, "lon", None),
            P(LAT, "lon"),
            P(LAT, "lon", None),
            P(LAT, "lon", None),
        ),
        out_specs=(P(MEM, LAT, "lon"), P(LAT, "lon")),
        check_vma=False,
    )
```

```python
import functools
import math

import jax
import jax.numpy as jnp
from jax import lax
from jax.experimental import pallas as pl
from jax.experimental.pallas import tpu as pltpu
from jax.sharding import Mesh
from jax.sharding import PartitionSpec as P

MEM = ("mem_0", "mem_1")
LAT = ("lat_0", "lat_1")
TILES = ("lat_0", "lat_1", "lon")
X, Z = "mem_0", "mem_1"

tiny_floor = 1e-06
highest = lax.Precision.HIGHEST
f32 = jnp.float32
bf16 = jnp.bfloat16

ROWS = 112
COLS = 144
LANES = 128
TOGETHER = 2


def sent_to_all(x, axis):
    copies = jnp.broadcast_to(x, (lax.axis_size(axis), *x.shape))
    return lax.all_to_all(copies, axis, split_axis=0, concat_axis=0, tiled=True)


def scale_run(scales, first, count):
    padded = jnp.pad(scales, (8, 248), constant_values=1.0)
    return lax.dynamic_slice(padded, (first + 8,), (count,))


def kernel_block(scales, first_row, row_count, first_col, col_count):
    total = scales.shape[0]
    rows = first_row + jnp.arange(row_count, dtype=jnp.int32)
    cols = first_col + jnp.arange(col_count, dtype=jnp.int32)
    row_scale = scale_run(scales, first_row, row_count)
    col_scale = scale_run(scales, first_col, col_count)
    inside = (rows >= 0) & (rows < total)
    weight = jnp.where(inside, (jnp.sqrt(jnp.pi) * row_scale) ** (-0.5), jnp.zeros_like(row_scale))
    offset = (rows[:, None] - cols[None, :]).astype(f32)
    spread = row_scale[:, None] ** 2 + col_scale[None, :] ** 2
    return weight[:, None] * jnp.exp(-offset * offset / spread)


def split_two(x):
    high = x.astype(bf16)
    low = (x - high.astype(f32)).astype(bf16)
    return high, low


def nt_dot(a, b):
    return lax.dot_general(a, b, (((1,), (1,)), ((), ())), preferred_element_type=f32)


def dot(a, b):
    return jnp.dot(a, b, preferred_element_type=f32)


def lane_rows(read, count):
    return jnp.concatenate([read(r) for r in range(count)], axis=1)


def picked_kernel(count_ref, perturb_ref, cell_ref, innov_ref, error_ref, copies_ref, out_ref, sems):
    members, fine_lat, fine_lon = perturb_ref.shape
    lines = cell_ref.shape[0]
    step = 512
    per_step = step // LANES
    slot = lax.broadcasted_iota(jnp.int32, cell_ref.shape, 0) * LANES + lax.broadcasted_iota(
        jnp.int32, cell_ref.shape, 1
    )
    out_ref[:lines] = cell_ref[...].astype(f32)
    out_ref[lines : 2 * lines] = innov_ref[...]
    out_ref[2 * lines : 3 * lines] = jnp.where(slot < count_ref[0], 1.0 / error_ref[...], 0.0)
    blocks = []
    for k in range(members):
        blocks.extend(split_two(perturb_ref[k]))
    field = jnp.concatenate(blocks, axis=0)
    for start in range(0, lines, per_step):
        cell = lane_rows(lambda r: cell_ref[start + r : start + r + 1, :], per_step)
        row = cell // fine_lon
        col = cell - row * fine_lon
        at_col = lax.broadcasted_iota(jnp.int32, (fine_lon, step), 0) == col
        one = jnp.where(at_col, 1.0, 0.0).astype(bf16)
        values = dot(field, one)
        at_row = lax.broadcasted_iota(jnp.int32, (fine_lat, step), 0) == row
        for k in range(members):
            at = 2 * k * fine_lat
            mine = values[at : at + fine_lat] + values[at + fine_lat : at + 2 * fine_lat]
            found = jnp.sum(jnp.where(at_row, mine, 0.0), axis=0, keepdims=True)
            for r in range(per_step):
                at = (3 + k) * lines + start + r
                out_ref[at : at + 1, :] = found[:, r * LANES : (r + 1) * LANES]
    sends = [
        pltpu.make_async_copy(out_ref, copies_ref.at[n], sems.at[n]) for n in range(copies_ref.shape[0])
    ]
    for send in sends:
        send.start()
    for send in sends:
        send.wait()


def picked(count, perturb, cell, innovation, error, copies):
    whole = pl.BlockSpec(memory_space=pltpu.VMEM)
    message = ((3 + perturb.shape[0]) * cell.shape[0], LANES)
    return pl.pallas_call(
        picked_kernel,
        out_shape=pltpu.HBM((copies, *message), f32),
        in_specs=[pl.BlockSpec(memory_space=pltpu.SMEM)] + [whole] * 4,
        out_specs=pl.BlockSpec(memory_space=pltpu.HBM),
        scratch_shapes=[pltpu.VMEM(message, f32), pltpu.SemaphoreType.DMA((copies,))],
        compiler_params=pltpu.CompilerParams(vmem_limit_bytes=60 * 1024 * 1024),
        name="picked",
    )(count, perturb, cell, innovation, error)


def weights_of(observed, innovation, inverse):
    residual = (observed - innovation) * inverse
    return residual / jnp.sqrt(1.0 + residual * residual) * inverse


def length_of(grad_total, curvature):
    return grad_total / (grad_total + curvature + tiny_floor)


def masks(below, count):
    cell = lax.broadcasted_iota(jnp.int32, below.shape, 0).astype(f32)
    found = []
    for start in range(0, count, 16):
        at = (cell + start).astype(bf16)
        before = (cell + (start - 1)).astype(bf16)
        found.append((below == at, below == before))
    return found


def hat(where, lower, upper):
    zero = jnp.zeros_like(lower)
    return jnp.concatenate([jnp.where(at, lower, jnp.where(before, upper, zero)) for at, before in where], axis=0)


def sweep_kernel(first, scale, lon_tiles, members, *refs):
    tile_ref, known_ref = refs[:2]
    refs = refs[2:]
    if not first:
        seen_ref = refs[0]
        refs = refs[1:]
    left_ref, left_low_ref, right_ref, right_low_ref, part_ref, coarse_ref, total_out_ref = refs[:7]
    refs = refs[7:]
    if not first:
        length_ref, own_ref = refs[:2]
        refs = refs[2:]
    hold, total_ref, coarse_own_ref, image_ref, sems = refs
    tiles = known_ref.shape[0]
    lines = known_ref.shape[1] // (3 + members)
    width = total_ref.shape[2]

    def known(n):
        return known_ref[:, n * lines : (n + 1) * lines, :]

    cell = known(0)
    innovation = known(1)
    inverse = known(2)
    row = jnp.floor(cell * (1.0 / 512.0))
    col = (cell - row * 512.0 + 2.5) * 0.25
    row = (row + 2.5) * 0.25
    row_cell, col_cell = jnp.floor(row), jnp.floor(col)
    row_up, col_up = row - row_cell, col - col_cell
    hold[0], hold[1], hold[2], hold[3] = row_cell, col_cell, 1.0 - col_up, col_up
    hold[4], hold[5] = 1.0 - row_up, row_up
    force = weights_of(0.0, innovation, inverse)
    if not first:
        image = seen_ref[...]
        length = length_of(jnp.sum(force * image), jnp.sum((image * inverse) ** 2))
        force = weights_of(-length * image, innovation, inverse) - length * force
        length_ref[...] = jnp.broadcast_to(length, length_ref.shape)
    hold[6] = force
    n = 7
    for k in range(members):
        q = known(3 + k) * force * scale
        for share in (1.0 - row_up, row_up):
            whole = share * q
            high = whole.astype(bf16).astype(f32)
            hold[n] = high
            hold[n + 1] = whole - high
            n += 2
    total_ref[...] = jnp.zeros_like(total_ref)

    def line(i, t):
        return lane_rows(
            lambda r: jnp.broadcast_to(hold[i, t, r : r + 1, :], (16, LANES)).astype(bf16), lines
        )

    def add_tile(t):
        lat = t // lon_tiles
        lon = t - lat * lon_tiles
        cols = hat(masks(line(1, t), COLS), line(2, t), line(3, t))
        where = masks(line(0, t), ROWS)
        blocks = []
        for k in range(members):
            for term in range(2):
                at = 7 + 4 * k + term
                blocks.append(hat(where, line(at, t), line(at + 2, t)))
        made = nt_dot(jnp.concatenate(blocks, axis=0), cols)
        at = pl.ds(pl.multiple_of(lat * 96, 8), ROWS)
        for k in range(members):
            both = made[2 * k * ROWS : (2 * k + 1) * ROWS] + made[(2 * k + 1) * ROWS : (2 * k + 2) * ROWS]
            total_ref[k, at, pl.ds(pl.multiple_of(lon * 128, 128), 128)] += both[:, :128]
            total_ref[k, at, pl.ds(pl.multiple_of(lon * 128 + 128, 128), COLS - 128)] += both[:, 128:]

    def some_tiles(t, carry):
        for n in range(TOGETHER):
            add_tile(t * TOGETHER + n)
        return carry

    lax.fori_loop(0, tiles // TOGETHER, some_tiles, 0)
    total_copy = pltpu.make_async_copy(total_ref, total_out_ref, sems.at[0])
    total_copy.start()

    own = tile_ref[0]
    rows = hat(masks(line(0, own), ROWS), line(4, own), line(5, own)).astype(f32)
    cols = hat(masks(line(1, own), COLS), line(2, own), line(3, own))
    high, low = zip(*(split_two(total_ref[k]) for k in range(members)))
    high, low = jnp.concatenate(high, axis=1), jnp.concatenate(low, axis=1)
    half = dot(jnp.concatenate([left_ref[...], left_low_ref[...]], axis=0), high)
    half = half[:ROWS] + (half[ROWS:] + dot(left_ref[...], low))
    half = jnp.concatenate([half[:, k * width : (k + 1) * width] for k in range(members)], axis=0)
    high, low = split_two(half)
    count = high.shape[0]
    coarse = dot(jnp.concatenate([high, low], axis=0), right_ref[...])
    coarse = coarse[:count] + (coarse[count:] + dot(high, right_low_ref[...]))
    for k in range(members):
        coarse_own_ref[k] = coarse[k * ROWS : (k + 1) * ROWS]
    coarse_copy = pltpu.make_async_copy(coarse_own_ref, coarse_ref, sems.at[1])
    coarse_copy.start()
    made = dot(jnp.concatenate(split_two(coarse), axis=0), cols)
    for k in range(members):
        mine = made[k * ROWS : (k + 1) * ROWS] + made[count + k * ROWS : count + (k + 1) * ROWS]
        value = jnp.sum(mine * rows, axis=0, keepdims=True)
        for r in range(lines):
            image_ref[k, r : r + 1, :] = value[:, r * LANES : (r + 1) * LANES]
    image = jnp.zeros((lines, LANES), f32)
    for k in range(members):
        image = image + image_ref[k] * known_ref[own, (3 + k) * lines : (4 + k) * lines, :]
    image = image * scale
    if not first:
        own_ref[0] = known_ref[own, 2 * lines : 3 * lines, :]
        own_ref[1] = hold[6, own]
    for n in range(part_ref.shape[0]):
        part_ref[n] = image
    coarse_copy.wait()
    total_copy.wait()


def sweep(tile, known, seen, kernels, scale, lon_tiles, members, groups):
    tiles = known.shape[0]
    lines = known.shape[1] // (3 + members)
    first = seen is None
    left, _, right, _ = kernels
    total = (members, left.shape[1], right.shape[0])
    whole = pl.BlockSpec(memory_space=pltpu.VMEM)
    out_shape = [
        jax.ShapeDtypeStruct((groups, lines, LANES), f32),
        pltpu.HBM((members, ROWS, COLS), f32),
        pltpu.HBM(total, f32),
    ]
    far = pl.BlockSpec(memory_space=pltpu.HBM)
    out_specs = [whole, far, far]
    if not first:
        out_shape.append(jax.ShapeDtypeStruct((1, LANES), f32))
        out_shape.append(jax.ShapeDtypeStruct((2, lines, LANES), f32))
        out_specs += [whole, whole]
    arrays = [known] if first else [known, seen]
    arrays += kernels
    return pl.pallas_call(
        functools.partial(sweep_kernel, first, scale, lon_tiles, members),
        out_shape=out_shape,
        in_specs=[pl.BlockSpec(memory_space=pltpu.SMEM)] + [whole] * len(arrays),
        out_specs=out_specs,
        scratch_shapes=[
            pltpu.VMEM((7 + 4 * members, tiles, lines, LANES), f32),
            pltpu.VMEM(total, f32),
            pltpu.VMEM((members, ROWS, COLS), f32),
            pltpu.VMEM((members, lines, LANES), f32),
            pltpu.SemaphoreType.DMA((2,)),
        ],
        compiler_params=pltpu.CompilerParams(vmem_limit_bytes=24 * 1024 * 1024),
        name="sweep_first" if first else "sweep_second",
    )(tile, *arrays)


def refined(count, cells, axis):
    shape = (count, cells) if axis == 0 else (cells, count)
    fine = lax.broadcasted_iota(jnp.int32, shape, axis).astype(f32)
    cell = lax.broadcasted_iota(jnp.int32, shape, 1 - axis).astype(f32)
    return jnp.maximum(1.0 - jnp.abs((fine + 2.5) * 0.25 - cell), 0.0).astype(bf16)


def put_field(perturb_ref, coarse, scale, out_ref, skip):
    members, fine_lat, fine_lon = perturb_ref.shape
    to_rows = refined(fine_lat, ROWS, 0)
    to_cols = refined(fine_lon, COLS, 1)
    field = jnp.zeros((fine_lat, fine_lon), f32)
    for k in range(members):
        high, low = split_two(coarse[k])
        tall = dot(to_rows, high) + dot(to_rows, low)
        high, low = split_two(tall)
        field = field + (dot(high, to_cols) + dot(low, to_cols)) * perturb_ref[k]
    field = scale * field
    across = fine_lon // LANES
    per_part = fine_lat // 8 * across // out_ref.shape[0]
    for n in range(per_part * out_ref.shape[0]):
        i = n // across * 8
        j = n % across * LANES
        at = skip + n % per_part * 8
        out_ref[n // per_part, at : at + 8, :] = field[i : i + 8, j : j + LANES]


def fields_kernel(scale, perturb_ref, length_ref, coarse_1_ref, coarse_2_ref, out_ref):
    put_field(perturb_ref, coarse_1_ref, -scale * length_ref[0, 0], out_ref.at[0], 0)
    put_field(perturb_ref, coarse_2_ref, -scale, out_ref.at[1], 0)


def ends_length(ends_ref):
    return length_of(jnp.sum(ends_ref[:, 1, :]), jnp.sum(ends_ref[:, 0, :]))


def join_kernel(ends_ref, fields_ref, out_ref):
    out_ref[...] = fields_ref[0] + ends_length(ends_ref) * fields_ref[1]


def analysis_kernel(length_ref, ends_ref, total_1_ref, total_2_ref, left_ref, right_ref, out_ref):
    one = length_ref[0, 0]
    two = ends_length(ends_ref)
    for k in range(out_ref.shape[0]):
        total = one * total_1_ref[k] + two * total_2_ref[k]
        half = jnp.dot(left_ref[...], total, precision=highest, preferred_element_type=f32)
        out_ref[k] = -jnp.dot(half, right_ref[...], precision=highest, preferred_element_type=f32)


def small_call(kernel, shapes, flops, name, *arrays):
    whole = pl.BlockSpec(memory_space=pltpu.VMEM)
    made = pl.pallas_call(
        kernel,
        out_shape=[jax.ShapeDtypeStruct(shape, f32) for shape in shapes],
        in_specs=[whole] * len(arrays),
        out_specs=[whole] * len(shapes),
        compiler_params=pltpu.CompilerParams(vmem_limit_bytes=20 * 1024 * 1024),
        cost_estimate=pl.CostEstimate(flops=flops, bytes_accessed=2 * 10**6, transcendentals=0),
        name=name,
    )(*arrays)
    return made if len(shapes) > 1 else made[0]


def per_device(perturb, loc_lat, loc_lon, obs_cell, obs_count, obs_innov, obs_error):
    members, fine_lat, fine_lon = perturb.shape
    coarse_lat, coarse_lon = fine_lat // 4, fine_lon // 4
    groups = lax.axis_size(MEM)
    scale = 1.0 / math.sqrt(members * groups - 1)
    lat, lon = lax.axis_index(LAT), lax.axis_index("lon")
    lat_tiles, lon_tiles = lax.axis_size(LAT), lax.axis_size("lon")
    slots = obs_cell.shape[-1]
    total_lat, total_lon = lat_tiles * coarse_lat, lon_tiles * coarse_lon
    padded_lat, padded_lon = total_lat + 16, total_lon + 128
    tile = (lat * lon_tiles + lon).astype(jnp.int32).reshape(1)

    lines = slots // LANES
    cell = obs_cell.reshape(lines, LANES)
    innovation = obs_innov.reshape(lines, LANES)
    error = obs_error.reshape(lines, LANES)
    message = picked(obs_count.reshape(1), perturb, cell, innovation, error, lat_tiles * lon_tiles)
    known = lax.all_to_all(message, TILES, 0, 0, tiled=True)

    first_lat, first_lon = lat * coarse_lat, lon * coarse_lon
    lat_all = kernel_block(loc_lat, -1, padded_lat, 0, total_lat)
    lon_all = kernel_block(loc_lon, -1, padded_lon, 0, total_lon)
    lat_tile = kernel_block(loc_lat, first_lat - 1, ROWS, 0, total_lat)
    lon_tile = kernel_block(loc_lon, first_lon - 1, COLS, 0, total_lon)
    left = jnp.einsum("ab,cb->ac", lat_tile, lat_all, precision=highest)
    right = jnp.einsum("ab,cb->ac", lon_all, lon_tile, precision=highest)
    left_own = kernel_block(loc_lat, -1, padded_lat, first_lat, coarse_lat).T
    right_own = kernel_block(loc_lon, -1, padded_lon, first_lon, coarse_lon)
    kernels = [*split_two(left), *split_two(right)]

    part, coarse_1, total_1 = sweep(tile, known, None, kernels, scale, lon_tiles, members, groups)
    mine = jnp.sum(lax.all_to_all(part, MEM, 0, 0, tiled=True), axis=0)
    seen = sent_to_all(mine, TILES)
    part, coarse_2, total_2, length_1, own = sweep(
        tile, known, seen, kernels, scale, lon_tiles, members, groups
    )
    mine = jnp.sum(lax.all_to_all(part, MEM, 0, 0, tiled=True), axis=0)
    bent = jnp.sum(jnp.stack([(mine * own[0]) ** 2, mine * own[1]]), axis=1)
    ends = sent_to_all(bent, TILES)

    field_rows = fine_lat * fine_lon // LANES
    along_x, along_z = lax.axis_size(X), lax.axis_size(Z)
    part_rows, piece_rows = field_rows // along_x, field_rows // groups
    part = (along_x, part_rows, LANES)
    fields = small_call(
        functools.partial(fields_kernel, scale),
        ((2, *part),),
        10**9,
        "fields",
        perturb,
        length_1,
        coarse_1,
        coarse_2,
    )
    field = small_call(join_kernel, (part,), 10**6, "join", ends, fields)
    field = jnp.sum(lax.all_to_all(field, X, 0, 0, tiled=True), axis=0).reshape(along_z, piece_rows, LANES)
    field = jnp.sum(lax.all_to_all(field, Z, 0, 0, tiled=True), axis=0)
    everything = sent_to_all(sent_to_all(field, Z).reshape(part_rows, LANES), X)
    whole = pl.BlockSpec(memory_space=pltpu.VMEM)
    analysis = pl.pallas_call(
        analysis_kernel,
        out_shape=jax.ShapeDtypeStruct((members, coarse_lat, coarse_lon), f32),
        in_specs=[whole] * 6,
        out_specs=whole,
        compiler_params=pltpu.CompilerParams(vmem_limit_bytes=24 * 1024 * 1024),
        cost_estimate=pl.CostEstimate(flops=2 * 10**9, bytes_accessed=5 * 10**6, transcendentals=0),
        name="analysis",
    )(length_1, ends, total_1, total_2, left_own, right_own)
    across = fine_lon // LANES
    increment = jnp.transpose(
        everything.reshape(fine_lat // 8, across, 8, LANES), (0, 2, 1, 3)
    ).reshape(fine_lat, fine_lon)
    return analysis, increment


def solution(mesh):
    torus = Mesh(
        mesh.devices.reshape(4, -1, 2, mesh.shape["lat"] // 2, mesh.shape["lon"]),
        ("mem_0", "mem_1", "lat_0", "lat_1", "lon"),
    )
    return jax.shard_map(
        per_device,
        mesh=torus,
        in_specs=(
            P(MEM, LAT, "lon"),
            P(),
            P(),
            P(LAT, "lon", None),
            P(LAT, "lon"),
            P(LAT, "lon", None),
            P(LAT, "lon", None),
        ),
        out_specs=(P(MEM, LAT, "lon"), P(LAT, "lon")),
        check_vma=False,
    )
```
